32 devices in a mesh: batch: 4 (over y, x), layer: 8 (over z, core).
Axes of the slice: x: 2, y: 2, z: 4, core: 2. Of those that a mesh axis runs over, the one named last changes fastest.
Arguments:
- inputs: float32 [256, 1024], P(None, 'batch'), parts along dimension 1, may hold values from -6 to 6
- guess: float32 [8, 256, 1024], P('layer', None, 'batch'), parts along dimension 2, may hold values from -6 to 6
- weights: bfloat16 [32, 256, 2304], P('layer'), may hold values from -0.125 to 0.125
Outputs:
- states: float32 [32, 256, 1024], P('layer', None, 'batch'), parts along dimension 2
The draws below stay inside these ranges and needn't reach their ends.
There are 4 independent parts, one for each index of `batch`. The reference program is written for one: setup_inputs(seed, part) draws one part's arguments, and reference() takes and returns one part's arrays. A program takes and returns all parts, laid end to end along the dimension named above; an argument that names none is the same for every part. Nothing has to cross between parts.
All inputs are finite; a program needn't handle non-finite values.
Results may differ from the reference program's by a relative error of at most 0.01.
Values may be sent and summed in bfloat16 or wider, within the bound.
A program may use at most 64 MiB of HBM per device.

```python
import jax
import jax.numpy as jnp

CHANNELS = 256
HEIGHT = 16
WIDTH = 16
COARSEN = 4
CELLS = 256
LAYERS = 32
POINTS = 8


def level_of(own_key, dims, split, least, high):
    level, own = 1.0, jax.random.fold_in(own_key, 6)
    for dim, shards_of in split:
        steps = jnp.exp(jax.random.uniform(jax.random.fold_in(own, dim), (shards_of,), jnp.float32, least / len(split), high / len(split)))
        level = level * jnp.repeat(steps, dims[dim] // shards_of).reshape([-1 if axis == dim else 1 for axis in range(len(dims))])
    return level


def normal_values(own_key, dims, width, limit, cuts=(), dtype=jnp.bfloat16):
    loudness = level_of(own_key, dims, cuts, -0.22, 0.18) if cuts else 1.0
    entries = jax.random.normal(own_key, dims, jnp.float32) * width * loudness
    return jnp.minimum(jnp.maximum(entries, -limit), limit).astype(dtype)


def setup_inputs(seed: int = 0, part: int = 0) -> dict:
    seeds = jax.random.split(jax.random.key(seed), 4)
    own_keys = jax.random.split(jax.random.fold_in(seeds[3], part), 4)
    inputs = normal_values(own_keys[0], (CHANNELS, CELLS), 1.0, 6.0, (), jnp.float32)
    guess = normal_values(own_keys[1], (POINTS, CHANNELS, CELLS), 1.0, 6.0, ((0, 8),), jnp.float32)
    weights = normal_values(seeds[2], (LAYERS, CHANNELS, 9 * CHANNELS), (9 * CHANNELS) ** -0.5, 0.125, ((0, 8),))
    return {"inputs": inputs, "guess": guess, "weights": weights}


def convolve(weight, state):
    chans = state.shape[0]
    grid = state.astype(jnp.bfloat16).reshape(chans, HEIGHT, WIDTH)
    padded = jnp.pad(grid, ((0, 0), (1, 1), (1, 1)))
    pieces = [padded[:, 1 + rowoff:1 + rowoff + HEIGHT, 1 + coloff:1 + coloff + WIDTH] for rowoff in (-1, 0, 1) for coloff in (-1, 0, 1)]
    stacked = jnp.concatenate(pieces, 0).reshape(9 * chans, HEIGHT * WIDTH)
    return jnp.dot(weight, stacked, preferred_element_type=jnp.float32)


def advance(weight, state, factor):
    return state + factor * jnp.tanh(convolve(weight, state))


many = jax.vmap(advance, in_axes=(0, 0, None))


def reference(inputs, guess, weights):
    points = guess.shape[0]
    blocks = weights.reshape(points, COARSEN, weights.shape[1], weights.shape[2])
    firsts = blocks[:, 0]

    def fine_sweep(lefts):
        result = []
        state = lefts
        for inner in range(COARSEN - 1):
            state = many(blocks[:, inner], state, 0.25)
            result.append(state)
        return result

    def shifted(values):
        return jnp.concatenate([inputs[None], values[:-1]], 0)

    position = jnp.arange(points)[:, None, None] % COARSEN
    lefts = jnp.concatenate([inputs[None], guess[1:]], 0)
    interior = fine_sweep(lefts)
    cpoints = many(blocks[:, COARSEN - 1], interior[-1], 0.25)
    lefts = shifted(cpoints)
    interior = fine_sweep(lefts)
    resid = many(blocks[:, COARSEN - 1], interior[-1], 0.25) - cpoints
    restricted = cpoints
    rhs = restricted - many(firsts, lefts, 1.0) + resid

    def relax(values, phases):
        for phase in phases:
            update = many(firsts, shifted(values), 1.0) + rhs
            values = jnp.where(position == phase, update, values)
        return values

    phases = list(range(COARSEN - 1))
    coarse = relax(restricted, phases + [COARSEN - 1] + phases)
    second = rhs - (coarse - many(firsts, shifted(coarse), 1.0))
    owners = slice(COARSEN - 1, None, COARSEN)
    upper = coarse[owners]
    upper_w = firsts[owners]
    upper_prev = jnp.concatenate([inputs[None], upper[:-1]], 0)
    coarse_rhs = upper - many(upper_w, upper_prev, 4.0) + second[owners]
    solved = []
    current = inputs
    for index in range(points // COARSEN):
        current = advance(upper_w[index], current, 4.0) + coarse_rhs[index]
        solved.append(current)
    coarse = coarse.at[owners].add(jnp.stack(solved, 0) - upper)
    coarse = relax(coarse, phases)
    cpoints = cpoints + coarse - restricted
    interior = fine_sweep(shifted(cpoints))
    states = jnp.stack(interior + [cpoints], 1)
    return states.reshape(points * COARSEN, weights.shape[1], inputs.shape[1])
```

```python
import functools

import jax
import jax.numpy as jnp
from jax import lax
from jax.experimental import pallas as pl
from jax.experimental.pallas import tpu as pltpu
from jax.sharding import PartitionSpec as P

WIDTH = 16
COARSEN = 4
LEFT, FIRST, SECOND, FINAL, CHANGE, RHS, UNSENT, WEIGHT = range(8)
NONE = 15
SLOTS = 7
PIECES = 8
MAX_STEPS = 16
ZERO, CP, LF, CC, RH, RHM, TT, PSI, QQ, XZ, OUT, TMP, DUMP = range(13)
STATES = 13
NOTHING, PSI_OF_LEFT, FIRST_POINT, START, PUT_0, PUT_1, PUT_2, OWNER_0, OWNER, CHANGES = range(10)
FIELDS = ("src", "dst", "w", "add", "factor", "tanh", "send", "by", "recv", "relay", "need", "op")
BY_ONE, BY_TWO = 0, 1
QUARTER, WHOLE, FOUR = 0, 1, 2


def step(src, dst, w, add=ZERO, factor=QUARTER, tanh=DUMP, send=UNSENT, by=BY_ONE,
         recv=NONE, relay=0, need=0, op=NOTHING):
    return dict(src=src, dst=dst, w=w, add=add, factor=factor, tanh=tanh, send=send, by=by,
                recv=recv, relay=relay, need=need, op=op)


def programs():
    def fine(send=UNSENT, tanh=DUMP, op=NOTHING):
        return [step(CP, CP, 0, tanh=tanh), step(CP, CP, 1), step(CP, CP, 2),
                step(CP, CP, 3, send=send, op=op)]

    def again(send=UNSENT, op=NOTHING):
        return [step(LF, CC, 0, tanh=TT, recv=LEFT, op=PSI_OF_LEFT), step(CC, CC, 1),
                step(CC, CC, 2), step(CC, RH, 3, add=QQ, send=send, op=op)]

    def whole(recv, dst, relay=0, need=0):
        return step(TMP, dst, COARSEN, add=RHM, factor=WHOLE, recv=recv, relay=relay, need=need)

    def own(src, dst, **kw):
        return step(src, dst, 0, add=RH, factor=WHOLE, **kw)

    last = [step(OUT, OUT, 1, op=PUT_1), step(OUT, OUT, 2, op=PUT_2)]
    body = fine(LEFT) + again()
    mate = fine(LEFT) + again(RHS)
    final = [whole(FINAL, LF, relay=1)]
    owner_second = [whole(SECOND, TMP), step(TMP, PSI, 0, factor=WHOLE, op=OWNER)]
    relaxed = [whole(FIRST, TMP, need=1), own(TMP, CC)] + final + [
        step(LF, DUMP, 0, factor=WHOLE, tanh=TT, op=PUT_0)]
    return {
        "start": fine(LEFT, TT, START) + last,
        "lead_first": body + [own(LF, CC, tanh=TT, recv=FIRST, send=FIRST, by=BY_TWO, op=PUT_0)] + last,
        "mate_first": mate + [own(LF, CC, tanh=TT, recv=FIRST, op=PUT_0)] + last,
        "owner_first": body + [
            step(TMP, XZ, 0, factor=FOUR), whole(FIRST, LF, relay=1, need=1),
            own(LF, CC, tanh=TT, op=OWNER_0)] + last,
        "head": fine(LEFT) + again(RHS, FIRST_POINT) + [
            own(LF, CC, tanh=TT, recv=FINAL, op=PUT_0)] + last + [
            step(LF, XZ, COARSEN, factor=FOUR, need=2),
            step(TMP, TMP, COARSEN, factor=FOUR, recv=SECOND, op=CHANGES)],
        "lead": body + [
            own(LF, TMP, recv=FIRST, send=FIRST, by=BY_TWO),
            whole(FINAL, LF, relay=1, need=1),
            own(LF, CC, tanh=TT, send=FINAL, by=BY_TWO, op=PUT_0),
            whole(SECOND, TMP, relay=1),
            own(TMP, TMP, send=SECOND, by=BY_TWO)] + last,
        "mate": mate + [own(LF, CC, tanh=TT, recv=FINAL, op=PUT_0)] + last,
        "owner": body + relaxed + owner_second + last,
        "owner_last": body + relaxed + last + owner_second,
    }


def packed(values):
    words = []
    for start in (0, 8):
        word = sum(v << (4 * k) for k, v in enumerate(values[start:start + 8]))
        words.append(word - 2**32 if word >= 2**31 else word)
    return words


def kernel(
    devices, x_hbm, g_hbm, w_hbm, o_ref,
    xg, w, pad, st, sent, got,
    send_sem, relay_sem, extra_sem, recv_sem, load_sem, weight_sem,
):
    f32, bf16 = jnp.float32, jnp.bfloat16
    p = lax.axis_index("layer")
    phase = lax.rem(p, COARSEN)
    owner = phase == COARSEN - 1
    group = lax.div(p, COARSEN)
    lead = lax.rem(p, 2) == 1
    mate = jnp.logical_not(lead)
    _, cells, chans = st.shape

    own_load = pltpu.make_async_copy(g_hbm.at[0], xg.at[0], load_sem.at[0])
    x_load = pltpu.make_async_copy(x_hbm, xg.at[0], load_sem.at[0])
    start_load = pltpu.make_async_copy(x_hbm, xg.at[1], load_sem.at[1])
    first_owner = jnp.logical_and(owner, group == 0)

    def weight_loads(j):
        rows = w.shape[1] // PIECES
        return [
            pltpu.make_async_copy(
                w_hbm.at[j, pl.ds(n * rows, rows)], w.at[j, pl.ds(n * rows, rows)],
                weight_sem.at[j, n],
            )
            for n in range(PIECES)
        ]

    @pl.when(p == 0)
    def _():
        x_load.start()

    @pl.when(p > 0)
    def _():
        own_load.start()

    for load in weight_loads(0) + weight_loads(1):
        load.start()

    @pl.when(first_owner)
    def _():
        start_load.start()

    barrier = pltpu.get_barrier_semaphore()

    def greet(by, cond):
        @pl.when(cond)
        def _():
            pl.semaphore_signal(
                barrier, inc=1, device_id={"layer": p + by},
                device_id_type=pl.DeviceIdType.MESH,
            )
        return cond.astype(jnp.int32)

    has_next = p < devices - 1
    lead_next = jnp.logical_and(lead, p + 2 < devices)
    last_owner = p + COARSEN >= devices
    greeted = (
        greet(1, has_next) + greet(-1, p > 0)
        + greet(COARSEN - 1, jnp.logical_and(phase == 0, group > 0))
        + greet(1 - COARSEN, jnp.logical_and(owner, group > 0))
        + greet(2, lead_next) + greet(-2, jnp.logical_and(lead, p >= 2))
    )
    shares = jnp.logical_and(mate, p > 0)
    owner_shares = jnp.logical_and(owner, group > 0)
    changes = jnp.logical_and(phase == 0, group > 0)

    roles = [
        ("start", p == 0),
        ("lead_first", jnp.logical_and(group == 0, phase == 1)),
        ("mate_first", jnp.logical_and(group == 0, phase == 2)),
        ("owner_first", first_owner),
        ("head", changes),
        ("lead", jnp.logical_and(group > 0, phase == 1)),
        ("mate", jnp.logical_and(group > 0, phase == 2)),
        ("owner_last", jnp.logical_and(owner, jnp.logical_and(group > 0, last_owner))),
    ]
    listed = programs()

    def chosen(value_of):
        value = jnp.int32(value_of(listed["owner"]))
        for name, cond in roles:
            value = jnp.where(cond, jnp.int32(value_of(listed[name])), value)
        return value

    count = chosen(len)
    words = {
        field: [
            chosen(lambda steps: packed([s[field] for s in steps])[half]) for half in (0, 1)
        ]
        for field in FIELDS
    }

    def entry(field, i):
        low, high = words[field]
        word = jnp.where(i < 8, low, high)
        return jnp.bitwise_and(
            lax.shift_right_logical(word, 4 * jnp.bitwise_and(i, 7)), 15
        )

    def remote(src, dst, ssem, rsem, by):
        return pltpu.make_async_remote_copy(
            src_ref=src, dst_ref=dst, send_sem=ssem, recv_sem=rsem,
            device_id={"layer": p + by}, device_id_type=pl.DeviceIdType.MESH,
        )

    def message(i, slot, by):
        return remote(sent.at[slot], got.at[slot], send_sem.at[i], recv_sem.at[slot], by)

    def relay_of(i, slot):
        return remote(got.at[slot], got.at[slot], relay_sem.at[i], recv_sem.at[slot], -1)

    back = jnp.where(p > 0, -1, 1)

    def arrived(slot):
        remote(sent.at[slot], got.at[slot], extra_sem.at[0], recv_sem.at[slot], back).wait_recv()

    def weight_to(by):
        return remote(w.at[0], w.at[COARSEN], extra_sem.at[0], recv_sem.at[WEIGHT], by)

    def special(n, slot, by):
        return remote(sent.at[slot], got.at[slot], extra_sem.at[n], recv_sem.at[slot], by)

    def distance(code):
        return jnp.where(code == BY_TWO, 2, 1)

    pad[:, 0:WIDTH, :] = jnp.zeros((3, WIDTH, chans), bf16)
    pad[:, WIDTH + cells:, :] = jnp.zeros((3, WIDTH, chans), bf16)
    st[ZERO] = jnp.zeros((cells, chans), f32)

    def put(n):
        o_ref[n] = st[OUT].T

    own_load.wait()
    loaded = xg[0].T
    st[LF] = loaded
    st[CP] = loaded

    @pl.when(first_owner)
    def _():
        start_load.wait()
        st[TMP] = xg[1].T

    def finish_owner(xy):
        cc = st[CC]
        second = st[RH] - (cc - st[PSI])
        solved = st[XZ] + ((cc - st[xy]) + second)

        @pl.when(lead_next)
        def _():
            sent[FINAL] = solved.astype(bf16)
            special(1, FINAL, 2).start()
            sent[SECOND] = cc.astype(bf16)
            special(2, SECOND, 2).start()

        st[CC] = solved

    def run(i, _):
        f = {field: entry(field, i) for field in FIELDS}
        is_fine = i < COARSEN

        @pl.when(is_fine)
        def _():
            for load in weight_loads(i):
                load.wait()

            @pl.when(i < COARSEN - 2)
            def _():
                for load in weight_loads(i + 2):
                    load.start()

        @pl.when(i == 1)
        def _():
            pl.semaphore_wait(barrier, greeted)

            @pl.when(shares)
            def _():
                weight_to(1).start()

            @pl.when(owner_shares)
            def _():
                weight_to(1 - COARSEN).start()

        @pl.when(f["need"] > 0)
        def _():
            remote(w.at[0], w.at[COARSEN], extra_sem.at[0], recv_sem.at[WEIGHT], back).wait_recv()

        @pl.when(f["need"] == 1)
        def _():
            arrived(RHS)
            st[RHM] = got[RHS].astype(f32)

        @pl.when(f["recv"] != NONE)
        def _():
            arrived(f["recv"])

            @pl.when(f["relay"] == 1)
            def _():
                relay_of(i, f["recv"]).start()

            st[f["src"]] = got[f["recv"]].astype(f32)

        v = st[f["src"]]
        col = lax.rem(lax.broadcasted_iota(jnp.int32, v.shape, 0), WIDTH)
        zero = jnp.zeros_like(v)
        before = jnp.where(col == 0, zero, pltpu.roll(v, 1, 0))
        after = jnp.where(col == WIDTH - 1, zero, pltpu.roll(v, cells - 1, 0))
        for d, piece in enumerate((before, v, after)):
            pad[d, WIDTH:WIDTH + cells, :] = piece.astype(bf16)
        patches = jnp.concatenate([
            pad[dx, WIDTH * dy:WIDTH * dy + cells, :] for dy in range(3) for dx in range(3)
        ], 1)
        total = lax.dot_general(
            patches, w[f["w"]], (((1,), (1,)), ((), ())), preferred_element_type=f32,
        )
        t = jnp.tanh(total)
        factor = jnp.where(f["factor"] == QUARTER, 0.25, jnp.where(f["factor"] == WHOLE, 1.0, 4.0))
        new = (st[f["src"]] + factor * t) + st[f["add"]]
        st[f["tanh"]] = t
        st[f["dst"]] = new
        sent[f["send"]] = new.astype(bf16)

        @pl.when(jnp.logical_and(f["send"] != UNSENT, has_next))
        def _():
            message(i, f["send"], distance(f["by"])).start()

        op = f["op"]

        @pl.when(op == PSI_OF_LEFT)
        def _():
            psi = st[LF] + st[TT]
            st[PSI] = psi
            st[QQ] = (st[CP] - psi) - st[CP]

        @pl.when(op == START)
        def _():
            psi = st[LF] + st[TT]
            rhs = st[CP] + ((st[CP] - psi) - st[CP])
            first = psi + rhs
            st[CC] = first
            sent[FIRST] = first.astype(bf16)
            special(1, FIRST, 1).start()

        @pl.when(op == FIRST_POINT)
        def _():
            sent[FIRST] = (st[PSI] + st[RH]).astype(bf16)
            special(1, FIRST, 1).start()

        @pl.when(op == OWNER_0)
        def _():
            st[PSI] = st[LF] + st[TT]
            finish_owner(XZ)

        @pl.when(jnp.logical_or(op == PUT_0, jnp.logical_or(op == START, op == OWNER_0)))
        def _():
            st[OUT] = st[LF] + 0.25 * st[TT]

        put_at = jnp.where(op == PUT_1, 1, jnp.where(op == PUT_2, 2, 0))

        @pl.when(jnp.logical_and(op >= START, op <= OWNER_0))
        def _():
            put(put_at)

        @pl.when(op == OWNER)
        def _():
            arrived(CHANGE)
            st[XZ] = got[CHANGE].astype(f32)
            finish_owner(ZERO)

        @pl.when(op == CHANGES)
        def _():
            sent[CHANGE] = (st[XZ] - st[TMP]).astype(bf16)
            special(2, CHANGE, COARSEN - 1).start()

        return 0

    lax.fori_loop(0, count, run, 0)
    o_ref[COARSEN - 1] = st[CC].T

    def drain(i, _):
        slot = entry("send", i)

        @pl.when(jnp.logical_and(slot != UNSENT, has_next))
        def _():
            message(i, slot, distance(entry("by", i))).wait_send()

        @pl.when(entry("relay", i) == 1)
        def _():
            relay_of(i, entry("recv", i)).wait_send()

        return 0

    lax.fori_loop(0, count, drain, 0)

    def drain_special(copy, cond):
        @pl.when(cond)
        def _():
            copy.wait_send()

    drain_special(weight_to(1), jnp.logical_or(shares, owner_shares))
    drain_special(special(1, FIRST, 1), phase == 0)
    drain_special(special(2, CHANGE, COARSEN - 1), changes)
    sends_solved = jnp.logical_and(owner, lead_next)
    drain_special(special(1, FINAL, 2), sends_solved)
    drain_special(special(2, SECOND, 2), sends_solved)


def per_device(devices, inputs, guess, weights):
    chans, cells = inputs.shape
    messages = pltpu.VMEM((SLOTS, cells, chans), jnp.bfloat16)
    return pl.pallas_call(
        functools.partial(kernel, devices),
        name="cycle",
        out_shape=pltpu.VMEM((COARSEN, chans, cells), jnp.float32),
        in_specs=[pl.BlockSpec(memory_space=pltpu.HBM)] * 3,
        out_specs=pl.BlockSpec(memory_space=pltpu.VMEM),
        scratch_shapes=[
            pltpu.VMEM((2, chans, cells), jnp.float32),
            pltpu.VMEM((COARSEN + 1,) + weights.shape[1:], jnp.bfloat16),
            pltpu.VMEM((3, cells + 2 * WIDTH, chans), jnp.bfloat16),
            pltpu.VMEM((STATES, cells, chans), jnp.float32),
            messages, messages,
            pltpu.SemaphoreType.DMA((MAX_STEPS,)),
            pltpu.SemaphoreType.DMA((MAX_STEPS,)),
            pltpu.SemaphoreType.DMA((3,)),
            pltpu.SemaphoreType.DMA((SLOTS + 1,)),
            pltpu.SemaphoreType.DMA((2,)),
            pltpu.SemaphoreType.DMA((COARSEN, PIECES)),
        ],
        compiler_params=pltpu.CompilerParams(
            collective_id=0, has_side_effects=True, vmem_limit_bytes=56 * 2**20,
        ),
    )(*[pltpu.with_memory_space_constraint(a, pltpu.HBM) for a in (inputs, guess, weights)])


def solution(mesh):
    return jax.shard_map(
        functools.partial(per_device, mesh.shape["layer"]),
        mesh=mesh,
        in_specs=(P(None, "batch"), P("layer", None, "batch"), P("layer", None, None)),
        out_specs=P("layer", None, "batch"),
        check_vma=False,
    )
```

```python
import functools

import jax
import jax.numpy as jnp
from jax import lax
from jax.experimental import pallas as pl
from jax.experimental.pallas import tpu as pltpu
from jax.sharding import PartitionSpec as P

WIDTH = 16
COARSEN = 4
NONE = 15
PIECES = 8
MAX_STEPS = 16
BLOCKS = 4
ZERO, CP, LF, CC, RH, RHM, TT, PSI, QQ, XZ, OUT, TMP, DUMP = range(13)
STATES = 13
CPB, LFB, OUTB, CCB, TMPB, LEFT, FIRST, SECOND, FINAL, UNSENT = range(10)
TO_LEFT, TO_FIRST, TO_SECOND, TO_FINAL, TO_CHANGE, TO_RHS, CHANGE, RHS = range(10, 18)
ROUNDED = 18
WEIGHT = ROUNDED
NOTHING, PSI_OF_LEFT, FIRST_POINT, START, PUT_0, PUT_1, PUT_2, OWNER_0, OWNER, CHANGES = range(10)
FIELDS = ("src", "dst", "w", "add", "factor", "tanh", "rsrc", "rdst", "by", "recv", "relay", "need", "op")
BY_ONE, BY_TWO = 0, 1
QUARTER, WHOLE, FOUR = 0, 1, 2
ROUNDED_OF = {CP: CPB, LF: LFB, CC: CCB, OUT: OUTB, TMP: TMPB}


def step(src, dst, w, add=ZERO, factor=QUARTER, tanh=DUMP, send=UNSENT, by=BY_ONE,
         recv=NONE, relay=0, need=0, op=NOTHING, rsrc=None):
    if rsrc is None:
        rsrc = ROUNDED_OF[src] if recv == NONE else recv
    rdst = ROUNDED_OF.get(dst, UNSENT) if send == UNSENT else send
    return dict(src=src, dst=dst, w=w, add=add, factor=factor, tanh=tanh, rsrc=rsrc, rdst=rdst,
                by=by, recv=recv, relay=relay, need=need, op=op)


def programs():
    def fine(send=UNSENT, tanh=DUMP, op=NOTHING):
        return [step(CP, CP, 0, tanh=tanh), step(CP, CP, 1), step(CP, CP, 2),
                step(CP, CP, 3, send=send, op=op)]

    def again(send=UNSENT, op=NOTHING):
        return [step(LF, CC, 0, tanh=TT, recv=LEFT, op=PSI_OF_LEFT), step(CC, CC, 1),
                step(CC, CC, 2), step(CC, RH, 3, add=QQ, send=send, op=op)]

    def whole(recv, dst, relay=0, need=0):
        return step(TMP, dst, COARSEN, add=RHM, factor=WHOLE, recv=recv, relay=relay, need=need)

    def own(src, dst, **kw):
        return step(src, dst, 0, add=RH, factor=WHOLE, **kw)

    last = [step(OUT, OUT, 1, op=PUT_1), step(OUT, OUT, 2, op=PUT_2)]
    body = fine(TO_LEFT) + again()
    mate = fine(TO_LEFT) + again(TO_RHS)
    final = [whole(FINAL, LF, relay=1)]
    owner_second = [whole(SECOND, TMP), step(TMP, PSI, 0, factor=WHOLE, op=OWNER)]
    relaxed = [whole(FIRST, TMP, need=1), own(TMP, CC)] + final + [
        step(LF, DUMP, 0, factor=WHOLE, tanh=TT, op=PUT_0)]
    return {
        "start": fine(TO_LEFT, TT, START) + last,
        "lead_first": body + [own(LF, CC, tanh=TT, recv=FIRST, send=TO_FIRST, by=BY_TWO, op=PUT_0)] + last,
        "mate_first": mate + [own(LF, CC, tanh=TT, recv=FIRST, op=PUT_0)] + last,
        "owner_first": body + [
            step(TMP, XZ, 0, factor=FOUR), whole(FIRST, LF, relay=1, need=1),
            own(LF, CC, tanh=TT, op=OWNER_0)] + last,
        "head": fine(TO_LEFT) + again(TO_RHS, FIRST_POINT) + [
            own(LF, CC, tanh=TT, recv=FINAL, op=PUT_0)] + last + [
            step(LF, XZ, COARSEN, factor=FOUR, need=2, rsrc=FINAL),
            step(TMP, TMP, COARSEN, factor=FOUR, recv=SECOND, op=CHANGES)],
        "lead": body + [
            own(LF, TMP, recv=FIRST, send=TO_FIRST, by=BY_TWO),
            whole(FINAL, LF, relay=1, need=1),
            own(LF, CC, tanh=TT, send=TO_FINAL, by=BY_TWO, op=PUT_0),
            whole(SECOND, TMP, relay=1),
            own(TMP, TMP, send=TO_SECOND, by=BY_TWO)] + last,
        "mate": mate + [own(LF, CC, tanh=TT, recv=FINAL, op=PUT_0)] + last,
        "owner": body + relaxed + owner_second + last,
        "owner_last": body + relaxed + last + owner_second,
    }


def packed(values):
    words = []
    for start in (0, 8):
        word = sum(v << (4 * k) for k, v in enumerate(values[start:start + 8]))
        words.append(word - 2**32 if word >= 2**31 else word)
    return words


def kernel(
    devices, x_hbm, g_hbm, w_hbm, o_ref,
    xg, w, st, rounded, part, side_sum, base,
    send_sem, relay_sem, extra_sem, recv_sem, load_sem, weight_sem,
):
    f32, bf16 = jnp.float32, jnp.bfloat16
    p = lax.axis_index("layer")
    phase = lax.rem(p, COARSEN)
    owner = phase == COARSEN - 1
    group = lax.div(p, COARSEN)
    lead = lax.rem(p, 2) == 1
    mate = jnp.logical_not(lead)
    _, cells, chans = st.shape

    own_load = pltpu.make_async_copy(g_hbm.at[0], xg.at[0], load_sem.at[0])
    x_load = pltpu.make_async_copy(x_hbm, xg.at[0], load_sem.at[0])
    start_load = pltpu.make_async_copy(x_hbm, xg.at[1], load_sem.at[1])
    first_owner = jnp.logical_and(owner, group == 0)

    def weight_loads(j):
        rows = w.shape[1] // PIECES
        return [
            pltpu.make_async_copy(
                w_hbm.at[j, pl.ds(n * rows, rows)], w.at[j, pl.ds(n * rows, rows)],
                weight_sem.at[j, n],
            )
            for n in range(PIECES)
        ]

    @pl.when(p == 0)
    def _():
        x_load.start()

    @pl.when(p > 0)
    def _():
        own_load.start()

    for load in weight_loads(0) + weight_loads(1):
        load.start()

    @pl.when(first_owner)
    def _():
        start_load.start()

    barrier = pltpu.get_barrier_semaphore()

    def greet(by, cond):
        @pl.when(cond)
        def _():
            pl.semaphore_signal(
                barrier, inc=1, device_id={"layer": p + by},
                device_id_type=pl.DeviceIdType.MESH,
            )
        return cond.astype(jnp.int32)

    has_next = p < devices - 1
    lead_next = jnp.logical_and(lead, p + 2 < devices)
    last_owner = p + COARSEN >= devices
    greeted = (
        greet(1, has_next) + greet(-1, p > 0)
        + greet(COARSEN - 1, jnp.logical_and(phase == 0, group > 0))
        + greet(1 - COARSEN, jnp.logical_and(owner, group > 0))
        + greet(2, lead_next) + greet(-2, jnp.logical_and(lead, p >= 2))
    )
    shares = jnp.logical_and(mate, p > 0)
    owner_shares = jnp.logical_and(owner, group > 0)
    changes = jnp.logical_and(phase == 0, group > 0)

    roles = [
        ("start", p == 0),
        ("lead_first", jnp.logical_and(group == 0, phase == 1)),
        ("mate_first", jnp.logical_and(group == 0, phase == 2)),
        ("owner_first", first_owner),
        ("head", changes),
        ("lead", jnp.logical_and(group > 0, phase == 1)),
        ("mate", jnp.logical_and(group > 0, phase == 2)),
        ("owner_last", jnp.logical_and(owner, jnp.logical_and(group > 0, last_owner))),
    ]
    listed = programs()

    def chosen(value_of):
        value = jnp.int32(value_of(listed["owner"]))
        for name, cond in roles:
            value = jnp.where(cond, jnp.int32(value_of(listed[name])), value)
        return value

    count = chosen(len)
    words = {
        field: [
            chosen(lambda steps: packed([s[field] for s in steps])[half]) for half in (0, 1)
        ]
        for field in FIELDS
    }

    def entry(field, i):
        low, high = words[field]
        word = jnp.where(i < 8, low, high)
        return jnp.bitwise_and(
            lax.shift_right_logical(word, 4 * jnp.bitwise_and(i, 7)), 15
        )

    def remote(src, dst, ssem, rsem, by):
        return pltpu.make_async_remote_copy(
            src_ref=src, dst_ref=dst, send_sem=ssem, recv_sem=rsem,
            device_id={"layer": p + by}, device_id_type=pl.DeviceIdType.MESH,
        )

    def inner(slot):
        return rounded.at[slot, pl.ds(WIDTH, cells)]

    def landing(slot):
        return jnp.where(slot == TO_RHS, RHS, slot - (TO_LEFT - LEFT))

    def message(i, slot, by):
        to = landing(slot)
        return remote(inner(slot), inner(to), send_sem.at[i], recv_sem.at[to], by)

    def relay_of(i, slot):
        return remote(inner(slot), inner(slot), relay_sem.at[i], recv_sem.at[slot], -1)

    back = jnp.where(p > 0, -1, 1)

    def arrived(slot):
        remote(inner(slot), inner(slot), extra_sem.at[0], recv_sem.at[slot], back).wait_recv()

    def weight_to(by):
        return remote(w.at[0], w.at[COARSEN], extra_sem.at[0], recv_sem.at[WEIGHT], by)

    def special(n, slot, to, by):
        return remote(inner(slot), inner(to), extra_sem.at[n], recv_sem.at[to], by)

    def rounded_store(slot, value):
        rounded[slot, WIDTH:WIDTH + cells, :] = value.astype(bf16)

    def distance(code):
        return jnp.where(code == BY_TWO, 2, 1)

    half = chans // 2
    rounded[:, 0:WIDTH, :] = jnp.zeros((ROUNDED, WIDTH, chans), bf16)
    rounded[:, WIDTH + cells:, :] = jnp.zeros((ROUNDED, WIDTH, chans), bf16)
    part[:, :, 0:8, :] = jnp.zeros((2, 2, 8, half), f32)
    part[:, :, 8 + cells:, :] = jnp.zeros((2, 2, 8, half), f32)
    st[ZERO] = jnp.zeros((cells, chans), f32)

    def put(n):
        o_ref[n] = st[OUT].T

    own_load.wait()
    loaded = xg[0].T
    st[LF] = loaded
    st[CP] = loaded
    rounded_store(CPB, loaded)

    @pl.when(first_owner)
    def _():
        start_load.wait()
        start = xg[1].T
        st[TMP] = start
        rounded_store(TMPB, start)

    def finish_owner(xy):
        cc = st[CC]
        second = st[RH] - (cc - st[PSI])
        solved = st[XZ] + ((cc - st[xy]) + second)

        @pl.when(lead_next)
        def _():
            rounded_store(TO_FINAL, solved)
            special(1, TO_FINAL, FINAL, 2).start()
            rounded_store(TO_SECOND, cc)
            special(2, TO_SECOND, SECOND, 2).start()

        st[CC] = solved

    rows_of = cells // BLOCKS
    col = lax.rem(lax.broadcasted_iota(jnp.int32, (rows_of, chans), 0), WIDTH)
    order = [
        [(1, 0), (0, 0), (2, 0), (0, 1), (1, 1)],
        [(1, 2), (0, 2), (2, 2), (2, 1), (1, 1)],
    ]

    def push(which, k, m):
        dy, dx = order[m][k]
        tap = 3 * dy + dx
        pltpu.matmul_push_rhs(
            w[which, :, tap * chans:(tap + 1) * chans], k % 2, m, transpose=True
        )

    def wait_weights(j):
        for load in weight_loads(j):
            load.wait()

    def run(sides, middles, i, _):
        f = {field: entry(field, i) for field in FIELDS}
        next_w = entry("w", i + 1)
        next_need = jnp.where(i + 1 < count, entry("need", i + 1), 0)

        @pl.when(i < COARSEN - 2)
        def _():
            for load in weight_loads(i + 2):
                load.start()

        @pl.when(i == 1)
        def _():
            pl.semaphore_wait(barrier, greeted)

            @pl.when(shares)
            def _():
                weight_to(1).start()

            @pl.when(owner_shares)
            def _():
                weight_to(1 - COARSEN).start()

        received = f["recv"] != NONE

        @pl.when(received)
        def _():
            arrived(f["recv"])

            @pl.when(f["relay"] == 1)
            def _():
                relay_of(i, f["recv"]).start()

        source = f["rsrc"]

        def lhs(dy, r):
            return rounded[source, WIDTH * dy + r * rows_of:WIDTH * dy + (r + 1) * rows_of, :]

        for k in range(5):
            for m in (0, 1):
                if k < 4:
                    push(f["w"], k + 1, m)
            for m in (0, 1):
                dy = order[m][k][0]
                total = sides[m] if k < 3 else middles[m]
                taken = range(BLOCKS) if k < 4 else range(m, BLOCKS, 2)
                for n, r in enumerate(taken):
                    pltpu.matmul_acc_lhs(total[r], lhs(dy, r), k % 2 if n == 0 else None)
        for r in range(BLOCKS):
            for m in (0, 1):
                t = pltpu.matmul_pop(sides[m][r])
                t = jnp.where(col == (0 if m else WIDTH - 1), 0.0, t)
                for h in (0, 1):
                    part[m, h, 8 + r * rows_of:8 + (r + 1) * rows_of, :] = t[:, h * half:(h + 1) * half]
        for r in range(BLOCKS):
            for h in (0, 1):
                side_sum[r * rows_of:(r + 1) * rows_of, h * half:(h + 1) * half] = (
                    part[0, h, 7 + r * rows_of:7 + (r + 1) * rows_of, :]
                    + part[1, h, 9 + r * rows_of:9 + (r + 1) * rows_of, :]
                )
        v = jnp.where(received, rounded[source, WIDTH:WIDTH + cells, :].astype(f32), st[f["src"]])
        base[...] = v + st[f["add"]]
        st[f["src"]] = v

        @pl.when(i < COARSEN - 1)
        def _():
            wait_weights(i + 1)

        @pl.when(next_need > 0)
        def _():
            remote(w.at[0], w.at[COARSEN], extra_sem.at[0], recv_sem.at[WEIGHT], back).wait_recv()

        @pl.when(next_need == 1)
        def _():
            arrived(RHS)
            st[RHM] = rounded[RHS, WIDTH:WIDTH + cells, :].astype(f32)

        for m in (0, 1):
            push(next_w, 0, m)
        factor = jnp.where(f["factor"] == QUARTER, 0.25, jnp.where(f["factor"] == WHOLE, 1.0, 4.0))
        for r in range(BLOCKS):
            at = slice(r * rows_of, (r + 1) * rows_of)
            t = jnp.tanh(
                (pltpu.matmul_pop(middles[0][r]) + pltpu.matmul_pop(middles[1][r])) + side_sum[at]
            )
            new = base[at] + factor * t
            st[f["tanh"], at] = t
            st[f["dst"], at] = new
            rounded[f["rdst"], WIDTH + r * rows_of:WIDTH + (r + 1) * rows_of, :] = new.astype(bf16)

        @pl.when(jnp.logical_and(f["rdst"] > UNSENT, has_next))
        def _():
            message(i, f["rdst"], distance(f["by"])).start()

        op = f["op"]

        @pl.when(op == PSI_OF_LEFT)
        def _():
            psi = st[LF] + st[TT]
            st[PSI] = psi
            st[QQ] = (st[CP] - psi) - st[CP]

        @pl.when(op == START)
        def _():
            psi = st[LF] + st[TT]
            rhs = st[CP] + ((st[CP] - psi) - st[CP])
            first = psi + rhs
            st[CC] = first
            rounded_store(TO_FIRST, first)
            special(1, TO_FIRST, FIRST, 1).start()

        @pl.when(op == FIRST_POINT)
        def _():
            rounded_store(TO_FIRST, st[PSI] + st[RH])
            special(1, TO_FIRST, FIRST, 1).start()

        @pl.when(op == OWNER_0)
        def _():
            st[PSI] = st[LF] + st[TT]
            finish_owner(XZ)

        @pl.when(jnp.logical_or(op == PUT_0, jnp.logical_or(op == START, op == OWNER_0)))
        def _():
            out = st[LF] + 0.25 * st[TT]
            st[OUT] = out
            rounded_store(OUTB, out)

        put_at = jnp.where(op == PUT_1, 1, jnp.where(op == PUT_2, 2, 0))

        @pl.when(jnp.logical_and(op >= START, op <= OWNER_0))
        def _():
            put(put_at)

        @pl.when(op == OWNER)
        def _():
            arrived(CHANGE)
            st[XZ] = rounded[CHANGE, WIDTH:WIDTH + cells, :].astype(f32)
            finish_owner(ZERO)

        @pl.when(op == CHANGES)
        def _():
            rounded_store(TO_CHANGE, st[XZ] - st[TMP])
            special(2, TO_CHANGE, CHANGE, COARSEN - 1).start()

        return 0

    def loop(*totals):
        sides = (totals[:BLOCKS], totals[2 * BLOCKS:3 * BLOCKS])
        middles = (totals[BLOCKS:2 * BLOCKS], totals[3 * BLOCKS:])
        wait_weights(0)
        for m in (0, 1):
            push(0, 0, m)
        lax.fori_loop(0, count, functools.partial(run, sides, middles), 0)
        for m in (0, 1):
            pltpu.matmul_acc_lhs(sides[m][0], rounded[CPB, 0:rows_of, :], 0)
            side_sum[0:rows_of, :] = pltpu.matmul_pop(sides[m][0])

    pl.run_scoped(
        loop, *[pltpu.ACC(m)((rows_of, chans), f32) for m in (0, 1) for _ in range(2 * BLOCKS)]
    )
    o_ref[COARSEN - 1] = st[CC].T

    def drain(i, _):
        slot = entry("rdst", i)

        @pl.when(jnp.logical_and(slot > UNSENT, has_next))
        def _():
            message(i, slot, distance(entry("by", i))).wait_send()

        @pl.when(entry("relay", i) == 1)
        def _():
            relay_of(i, entry("recv", i)).wait_send()

        return 0

    lax.fori_loop(0, count, drain, 0)

    def drain_special(copy, cond):
        @pl.when(cond)
        def _():
            copy.wait_send()

    drain_special(weight_to(1), jnp.logical_or(shares, owner_shares))
    drain_special(special(1, TO_FIRST, FIRST, 1), phase == 0)
    drain_special(special(2, TO_CHANGE, CHANGE, COARSEN - 1), changes)
    sends_solved = jnp.logical_and(owner, lead_next)
    drain_special(special(1, TO_FINAL, FINAL, 2), sends_solved)
    drain_special(special(2, TO_SECOND, SECOND, 2), sends_solved)


def per_device(devices, inputs, guess, weights):
    chans, cells = inputs.shape
    return pl.pallas_call(
        functools.partial(kernel, devices),
        name="cycle",
        out_shape=pltpu.VMEM((COARSEN, chans, cells), jnp.float32),
        in_specs=[pl.BlockSpec(memory_space=pltpu.HBM)] * 3,
        out_specs=pl.BlockSpec(memory_space=pltpu.VMEM),
        scratch_shapes=[
            pltpu.VMEM((2, chans, cells), jnp.float32),
            pltpu.VMEM((COARSEN + 1,) + weights.shape[1:], jnp.bfloat16),
            pltpu.VMEM((STATES, cells, chans), jnp.float32),
            pltpu.VMEM((ROUNDED, cells + 2 * WIDTH, chans), jnp.bfloat16),
            pltpu.VMEM((2, 2, cells + 16, chans // 2), jnp.float32),
            pltpu.VMEM((cells, chans), jnp.float32),
            pltpu.VMEM((cells, chans), jnp.float32),
            pltpu.SemaphoreType.DMA((MAX_STEPS,)),
            pltpu.SemaphoreType.DMA((MAX_STEPS,)),
            pltpu.SemaphoreType.DMA((3,)),
            pltpu.SemaphoreType.DMA((ROUNDED + 1,)),
            pltpu.SemaphoreType.DMA((2,)),
            pltpu.SemaphoreType.DMA((COARSEN, PIECES)),
        ],
        compiler_params=pltpu.CompilerParams(
            collective_id=0, has_side_effects=True, vmem_limit_bytes=56 * 2**20,
        ),
    )(*[pltpu.with_memory_space_constraint(a, pltpu.HBM) for a in (inputs, guess, weights)])


def solution(mesh):
    return jax.shard_map(
        functools.partial(per_device, mesh.shape["layer"]),
        mesh=mesh,
        in_specs=(P(None, "batch"), P("layer", None, "batch"), P("layer", None, None)),
        out_specs=P("layer", None, "batch"),
        check_vma=False,
    )
```

```python
import functools

import jax
import jax.numpy as jnp
from jax import lax
from jax.experimental import pallas as pl
from jax.experimental.pallas import tpu as pltpu
from jax.sharding import PartitionSpec as P

WIDTH = 16
COARSEN = 4
NONE = 15
PIECES = 8
BLOCKS = 4
ZERO, CP, LF, CC, RH, RHM, TT, PSI, QQ, XZ, OUT, TMP, DUMP = range(13)
STATES = 13
CPB, LFB, OUTB, CCB, TMPB, LEFT, FIRST, SECOND, FINAL, UNSENT = range(10)
TO_LEFT, TO_FIRST, TO_SECOND, TO_FINAL, TO_CHANGE, TO_RHS, CHANGE, RHS = range(10, 18)
ROUNDED = 18
WEIGHT = ROUNDED
NOTHING, PSI_OF_LEFT, FIRST_POINT, START, PUT_0, PUT_1, PUT_2, OWNER_0, OWNER, CHANGES, KEEP = range(11)
FIELDS = ("src", "dst", "w", "add", "factor", "rsrc", "rdst", "by", "recv", "relay", "need", "op")
BY_ONE, BY_TWO = 0, 1
QUARTER, WHOLE, FOUR = 0, 1, 2
ROUNDED_OF = {CP: CPB, LF: LFB, CC: CCB, OUT: OUTB, TMP: TMPB}


def step(src, dst, w, add=ZERO, factor=QUARTER, send=UNSENT, by=BY_ONE,
         recv=NONE, relay=0, need=0, op=NOTHING, rsrc=None):
    if rsrc is None:
        rsrc = ROUNDED_OF[src] if recv == NONE else recv
    rdst = ROUNDED_OF.get(dst, UNSENT) if send == UNSENT else send
    return dict(src=src, dst=dst, w=w, add=add, factor=factor, rsrc=rsrc, rdst=rdst,
                by=by, recv=recv, relay=relay, need=need, op=op)


def programs():
    def fine(send=UNSENT, first=NOTHING, op=NOTHING):
        return [step(CP, CP, 0, op=first), step(CP, CP, 1), step(CP, CP, 2),
                step(CP, CP, 3, send=send, op=op)]

    def again(send=UNSENT, op=NOTHING):
        return [step(LF, CC, 0, recv=LEFT, op=PSI_OF_LEFT), step(CC, CC, 1),
                step(CC, CC, 2), step(CC, RH, 3, add=QQ, send=send, op=op)]

    def whole(recv, dst, relay=0, need=0):
        return step(TMP, dst, COARSEN, add=RHM, factor=WHOLE, recv=recv, relay=relay, need=need)

    def own(src, dst, **kw):
        return step(src, dst, 0, add=RH, factor=WHOLE, **kw)

    last = [step(OUT, OUT, 1, op=PUT_1), step(OUT, OUT, 2, op=PUT_2)]
    body = fine(TO_LEFT) + again()
    mate = fine(TO_LEFT) + again(TO_RHS)
    final = [whole(FINAL, LF, relay=1)]
    owner_second = [whole(SECOND, TMP), step(TMP, PSI, 0, factor=WHOLE, op=OWNER)]
    relaxed = [whole(FIRST, TMP, need=1), own(TMP, CC)] + final + [
        step(LF, DUMP, 0, factor=WHOLE, op=PUT_0)]
    return {
        "start": fine(TO_LEFT, KEEP, START) + last,
        "lead_first": body + [own(LF, CC, recv=FIRST, send=TO_FIRST, by=BY_TWO, op=PUT_0)] + last,
        "mate_first": mate + [own(LF, CC, recv=FIRST, op=PUT_0)] + last,
        "owner_first": body + [
            step(TMP, XZ, 0, factor=FOUR), whole(FIRST, LF, relay=1, need=1),
            own(LF, CC, op=OWNER_0)] + last,
        "head": fine(TO_LEFT) + again(TO_RHS, FIRST_POINT) + [
            own(LF, CC, recv=FINAL, op=PUT_0)] + last + [
            step(LF, XZ, COARSEN, factor=FOUR, need=2, rsrc=FINAL),
            step(TMP, TMP, COARSEN, factor=FOUR, recv=SECOND, op=CHANGES)],
        "lead": body + [
            own(LF, TMP, recv=FIRST, send=TO_FIRST, by=BY_TWO),
            whole(FINAL, LF, relay=1, need=1),
            own(LF, CC, send=TO_FINAL, by=BY_TWO, op=PUT_0),
            whole(SECOND, TMP, relay=1),
            own(TMP, TMP, send=TO_SECOND, by=BY_TWO)] + last,
        "mate": mate + [own(LF, CC, recv=FINAL, op=PUT_0)] + last,
        "owner": body + relaxed + owner_second + last,
        "owner_last": body + relaxed + last + owner_second,
    }


def packed(values):
    words = []
    for start in (0, 8):
        word = sum(v << (4 * k) for k, v in enumerate(values[start:start + 8]))
        words.append(word - 2**32 if word >= 2**31 else word)
    return words


def kernel(
    devices, x_hbm, g_hbm, w_hbm, o_ref,
    xg, w, st, rounded, part, side_sum, base,
    send_sem, relay_sem, extra_sem, recv_sem, load_sem, weight_sem,
):
    f32, bf16 = jnp.float32, jnp.bfloat16
    p = lax.axis_index("layer")
    phase = lax.rem(p, COARSEN)
    owner = phase == COARSEN - 1
    group = lax.div(p, COARSEN)
    lead = lax.rem(p, 2) == 1
    mate = jnp.logical_not(lead)
    _, cells, chans = st.shape

    own_load = pltpu.make_async_copy(g_hbm.at[0], xg.at[0], load_sem.at[0])
    x_load = pltpu.make_async_copy(x_hbm, xg.at[0], load_sem.at[0])
    start_load = pltpu.make_async_copy(x_hbm, xg.at[1], load_sem.at[1])
    first_owner = jnp.logical_and(owner, group == 0)

    def weight_loads(j):
        rows = w.shape[1] // PIECES
        return [
            pltpu.make_async_copy(
                w_hbm.at[j, pl.ds(n * rows, rows)], w.at[j, pl.ds(n * rows, rows)],
                weight_sem.at[j, n],
            )
            for n in range(PIECES)
        ]

    @pl.when(p == 0)
    def _():
        x_load.start()

    @pl.when(p > 0)
    def _():
        own_load.start()

    for load in weight_loads(0):
        load.start()

    @pl.when(first_owner)
    def _():
        start_load.start()

    barrier = pltpu.get_barrier_semaphore()

    def greet(by, cond):
        @pl.when(cond)
        def _():
            pl.semaphore_signal(
                barrier, inc=1, device_id={"layer": p + by},
                device_id_type=pl.DeviceIdType.MESH,
            )
        return cond.astype(jnp.int32)

    has_next = p < devices - 1
    lead_next = jnp.logical_and(lead, p + 2 < devices)
    last_owner = p + COARSEN >= devices
    greeted = (
        greet(1, has_next) + greet(-1, p > 0)
        + greet(COARSEN - 1, jnp.logical_and(phase == 0, group > 0))
        + greet(1 - COARSEN, jnp.logical_and(owner, group > 0))
        + greet(2, lead_next) + greet(-2, jnp.logical_and(lead, p >= 2))
    )
    shares = jnp.logical_and(mate, p > 0)
    owner_shares = jnp.logical_and(owner, group > 0)
    changes = jnp.logical_and(phase == 0, group > 0)

    roles = [
        ("start", p == 0),
        ("lead_first", jnp.logical_and(group == 0, phase == 1)),
        ("mate_first", jnp.logical_and(group == 0, phase == 2)),
        ("owner_first", first_owner),
        ("head", changes),
        ("lead", jnp.logical_and(group > 0, phase == 1)),
        ("mate", jnp.logical_and(group > 0, phase == 2)),
        ("owner_last", jnp.logical_and(owner, jnp.logical_and(group > 0, last_owner))),
    ]
    listed = programs()

    def chosen(value_of):
        value = jnp.int32(value_of(listed["owner"]))
        for name, cond in roles:
            value = jnp.where(cond, jnp.int32(value_of(listed[name])), value)
        return value

    count = chosen(len)
    words = {
        field: [
            chosen(lambda steps: packed([s[field] for s in steps])[half]) for half in (0, 1)
        ]
        for field in FIELDS
    }

    def entry(field, i):
        low, high = words[field]
        word = jnp.where(i < 8, low, high)
        return jnp.bitwise_and(
            lax.shift_right_logical(word, 4 * jnp.bitwise_and(i, 7)), 15
        )

    def remote(src, dst, ssem, rsem, by):
        return pltpu.make_async_remote_copy(
            src_ref=src, dst_ref=dst, send_sem=ssem, recv_sem=rsem,
            device_id={"layer": p + by}, device_id_type=pl.DeviceIdType.MESH,
        )

    def inner(slot):
        return rounded.at[slot, pl.ds(WIDTH, cells)]

    def landing(slot):
        return jnp.where(slot == TO_RHS, RHS, slot - (TO_LEFT - LEFT))

    def message(slot, by):
        to = landing(slot)
        return remote(inner(slot), inner(to), send_sem.at[slot - TO_LEFT], recv_sem.at[to], by)

    def relay_of(slot):
        return remote(inner(slot), inner(slot), relay_sem.at[slot - LEFT], recv_sem.at[slot], -1)

    back = jnp.where(p > 0, -1, 1)

    def arrived(slot):
        remote(inner(slot), inner(slot), extra_sem.at[0], recv_sem.at[slot], back).wait_recv()

    def weight_to(by):
        return remote(w.at[0], w.at[COARSEN], extra_sem.at[0], recv_sem.at[WEIGHT], by)

    def special(slot, to, by):
        return remote(inner(slot), inner(to), send_sem.at[slot - TO_LEFT], recv_sem.at[to], by)

    def rounded_store(slot, value):
        rounded[slot, WIDTH:WIDTH + cells, :] = value.astype(bf16)

    def distance(code):
        return jnp.where(code == BY_TWO, 2, 1)

    half = chans // 2
    rounded[:, 0:WIDTH, :] = jnp.zeros((ROUNDED, WIDTH, chans), bf16)
    rounded[:, WIDTH + cells:, :] = jnp.zeros((ROUNDED, WIDTH, chans), bf16)
    part[:, :, 0:8, :] = jnp.zeros((2, 2, 8, half), f32)
    part[:, :, 8 + cells:, :] = jnp.zeros((2, 2, 8, half), f32)
    st[ZERO] = jnp.zeros((cells, chans), f32)

    def put(n):
        o_ref[n] = st[OUT].T

    own_load.wait()
    for load in weight_loads(1):
        load.start()
    loaded = xg[0].T
    st[LF] = loaded
    st[CP] = loaded
    rounded_store(CPB, loaded)

    @pl.when(first_owner)
    def _():
        start_load.wait()
        start = xg[1].T
        st[TMP] = start
        rounded_store(TMPB, start)

    def finish_owner(xy):
        cc = st[CC]
        second = st[RH] - (cc - st[PSI])
        solved = st[XZ] + ((cc - st[xy]) + second)

        @pl.when(lead_next)
        def _():
            rounded_store(TO_FINAL, solved)
            special(TO_FINAL, FINAL, 2).start()
            rounded_store(TO_SECOND, cc)
            special(TO_SECOND, SECOND, 2).start()

        st[CC] = solved

    rows_of = cells // BLOCKS
    col = lax.rem(lax.broadcasted_iota(jnp.int32, (rows_of, chans), 0), WIDTH)
    order = [
        [(1, 0), (0, 0), (2, 0), (0, 1), (1, 1)],
        [(1, 2), (0, 2), (2, 2), (2, 1), (1, 1)],
    ]

    def push(which, k, m):
        dy, dx = order[m][k]
        tap = 3 * dy + dx
        pltpu.matmul_push_rhs(
            w[which, :, tap * chans:(tap + 1) * chans], k % 2, m, transpose=True
        )

    def wait_weights(j):
        for load in weight_loads(j):
            load.wait()

    def fields_of(i):
        return tuple(entry(field, i) for field in FIELDS)

    def run(sides, middles, i, fields):
        f = dict(zip(FIELDS, fields))

        @pl.when(i < COARSEN - 1)
        def _():
            @pl.when(i < COARSEN - 2)
            def _():
                for load in weight_loads(i + 2):
                    load.start()

            @pl.when(i == 1)
            def _():
                pl.semaphore_wait(barrier, greeted)

                @pl.when(shares)
                def _():
                    weight_to(1).start()

                @pl.when(owner_shares)
                def _():
                    weight_to(1 - COARSEN).start()

        received = f["recv"] != NONE

        @pl.when(received)
        def _():
            arrived(f["recv"])

            @pl.when(f["relay"] == 1)
            def _():
                relay_of(f["recv"]).start()

        source = f["rsrc"]

        def lhs(dy, r):
            return rounded[source, WIDTH * dy + r * rows_of:WIDTH * dy + (r + 1) * rows_of, :]

        for k in range(5):
            for m in (0, 1):
                if k < 4:
                    push(f["w"], k + 1, m)
            for m in (0, 1):
                dy = order[m][k][0]
                total = sides[m] if k < 3 else middles[m]
                taken = range(BLOCKS) if k < 4 else range(m, BLOCKS, 2)
                for n, r in enumerate(taken):
                    pltpu.matmul_acc_lhs(total[r], lhs(dy, r), k % 2 if n == 0 else None)
        for r in range(BLOCKS):
            for m in (0, 1):
                t = pltpu.matmul_pop(sides[m][r])
                t = jnp.where(col == (0 if m else WIDTH - 1), 0.0, t)
                for h in (0, 1):
                    part[m, h, 8 + r * rows_of:8 + (r + 1) * rows_of, :] = t[:, h * half:(h + 1) * half]
        for r in range(BLOCKS):
            for h in (0, 1):
                side_sum[r * rows_of:(r + 1) * rows_of, h * half:(h + 1) * half] = (
                    part[0, h, 7 + r * rows_of:7 + (r + 1) * rows_of, :]
                    + part[1, h, 9 + r * rows_of:9 + (r + 1) * rows_of, :]
                )
        v = jnp.where(received, rounded[source, WIDTH:WIDTH + cells, :].astype(f32), st[f["src"]])
        base[...] = v + st[f["add"]]
        st[f["src"]] = v

        later = fields_of(i + 1)
        following = dict(zip(FIELDS, later))
        next_need = jnp.where(i + 1 < count, following["need"], 0)

        @pl.when(jnp.logical_or(i < COARSEN - 1, next_need > 0))
        def _():
            @pl.when(i < COARSEN - 1)
            def _():
                wait_weights(i + 1)

            @pl.when(next_need > 0)
            def _():
                remote(w.at[0], w.at[COARSEN], extra_sem.at[0], recv_sem.at[WEIGHT], back).wait_recv()

            @pl.when(next_need == 1)
            def _():
                arrived(RHS)
                st[RHM] = rounded[RHS, WIDTH:WIDTH + cells, :].astype(f32)

        for m in (0, 1):
            push(following["w"], 0, m)
        factor = jnp.where(f["factor"] == QUARTER, 0.25, jnp.where(f["factor"] == WHOLE, 1.0, 4.0))
        for r in range(BLOCKS):
            at = slice(r * rows_of, (r + 1) * rows_of)
            t = jnp.tanh(
                (pltpu.matmul_pop(middles[0][r]) + pltpu.matmul_pop(middles[1][r])) + side_sum[at]
            )
            new = base[at] + factor * t
            st[f["dst"], at] = new
            rounded[f["rdst"], WIDTH + r * rows_of:WIDTH + (r + 1) * rows_of, :] = new.astype(bf16)

        @pl.when(jnp.logical_and(f["rdst"] > UNSENT, has_next))
        def _():
            message(f["rdst"], distance(f["by"])).start()

        op = f["op"]

        @pl.when(op != NOTHING)
        def _():
            @pl.when(op == PSI_OF_LEFT)
            def _():
                psi = st[LF] + 4.0 * (st[CC] - base[...])
                st[PSI] = psi
                st[QQ] = (st[CP] - psi) - st[CP]

            @pl.when(op == KEEP)
            def _():
                st[TT] = 4.0 * (st[CP] - base[...])

            @pl.when(op == START)
            def _():
                psi = st[LF] + st[TT]
                rhs = st[CP] + ((st[CP] - psi) - st[CP])
                first = psi + rhs
                st[CC] = first
                rounded_store(TO_FIRST, first)
                special(TO_FIRST, FIRST, 1).start()

            @pl.when(op == FIRST_POINT)
            def _():
                rounded_store(TO_FIRST, st[PSI] + st[RH])
                special(TO_FIRST, FIRST, 1).start()

            @pl.when(op == OWNER_0)
            def _():
                t = st[CC] - base[...]
                st[TT] = t
                st[PSI] = st[LF] + t
                finish_owner(XZ)

            @pl.when(jnp.logical_or(op == PUT_0, jnp.logical_or(op == START, op == OWNER_0)))
            def _():
                t = jnp.where(op == PUT_0, st[f["dst"]] - base[...], st[TT])
                out = st[LF] + 0.25 * t
                st[OUT] = out
                rounded_store(OUTB, out)

            put_at = jnp.where(op == PUT_1, 1, jnp.where(op == PUT_2, 2, 0))

            @pl.when(jnp.logical_and(op >= START, op <= OWNER_0))
            def _():
                put(put_at)

            @pl.when(op == OWNER)
            def _():
                arrived(CHANGE)
                st[XZ] = rounded[CHANGE, WIDTH:WIDTH + cells, :].astype(f32)
                finish_owner(ZERO)

            @pl.when(op == CHANGES)
            def _():
                rounded_store(TO_CHANGE, st[XZ] - st[TMP])
                special(TO_CHANGE, CHANGE, COARSEN - 1).start()

        return later

    def loop(*totals):
        sides = (totals[:BLOCKS], totals[2 * BLOCKS:3 * BLOCKS])
        middles = (totals[BLOCKS:2 * BLOCKS], totals[3 * BLOCKS:])
        wait_weights(0)
        for m in (0, 1):
            push(0, 0, m)
        lax.fori_loop(0, count, functools.partial(run, sides, middles), fields_of(0))
        for m in (0, 1):
            pltpu.matmul_acc_lhs(sides[m][0], rounded[CPB, 0:rows_of, :], 0)
            side_sum[0:rows_of, :] = pltpu.matmul_pop(sides[m][0])

    pl.run_scoped(
        loop, *[pltpu.ACC(m)((rows_of, chans), f32) for m in (0, 1) for _ in range(2 * BLOCKS)]
    )
    o_ref[COARSEN - 1] = st[CC].T

    def drain(copy, cond):
        @pl.when(cond)
        def _():
            copy.wait_send()

    relaxed = jnp.logical_or(
        jnp.logical_and(owner, lead_next), jnp.logical_and(phase == 1, group > 0)
    )
    drain(weight_to(back), jnp.logical_or(shares, owner_shares))
    drain(special(TO_LEFT, LEFT, back), has_next)
    drain(special(TO_RHS, RHS, back), shares)
    drain(special(TO_FIRST, FIRST, back), phase < 2)
    drain(special(TO_FINAL, FINAL, back), relaxed)
    drain(special(TO_SECOND, SECOND, back), relaxed)
    drain(special(TO_CHANGE, CHANGE, back), changes)
    drain(relay_of(FIRST), first_owner)
    drain(relay_of(FINAL), jnp.logical_and(lead, group > 0))
    drain(relay_of(SECOND), jnp.logical_and(phase == 1, group > 0))


def per_device(devices, inputs, guess, weights):
    chans, cells = inputs.shape
    return pl.pallas_call(
        functools.partial(kernel, devices),
        name="cycle",
        out_shape=pltpu.VMEM((COARSEN, chans, cells), jnp.float32),
        in_specs=[pl.BlockSpec(memory_space=pltpu.HBM)] * 3,
        out_specs=pl.BlockSpec(memory_space=pltpu.VMEM),
        scratch_shapes=[
            pltpu.VMEM((2, chans, cells), jnp.float32),
            pltpu.VMEM((COARSEN + 1,) + weights.shape[1:], jnp.bfloat16),
            pltpu.VMEM((STATES, cells, chans), jnp.float32),
            pltpu.VMEM((ROUNDED, cells + 2 * WIDTH, chans), jnp.bfloat16),
            pltpu.VMEM((2, 2, cells + 16, chans // 2), jnp.float32),
            pltpu.VMEM((cells, chans), jnp.float32),
            pltpu.VMEM((cells, chans), jnp.float32),
            pltpu.SemaphoreType.DMA((TO_RHS - TO_LEFT + 1,)),
            pltpu.SemaphoreType.DMA((FINAL - LEFT + 1,)),
            pltpu.SemaphoreType.DMA((1,)),
            pltpu.SemaphoreType.DMA((ROUNDED + 1,)),
            pltpu.SemaphoreType.DMA((2,)),
            pltpu.SemaphoreType.DMA((COARSEN, PIECES)),
        ],
        compiler_params=pltpu.CompilerParams(
            collective_id=0, has_side_effects=True, vmem_limit_bytes=56 * 2**20,
        ),
    )(*[pltpu.with_memory_space_constraint(a, pltpu.HBM) for a in (inputs, guess, weights)])


def solution(mesh):
    return jax.shard_map(
        functools.partial(per_device, mesh.shape["layer"]),
        mesh=mesh,
        in_specs=(P(None, "batch"), P("layer", None, "batch"), P("layer", None, None)),
        out_specs=P("layer", None, "batch"),
        check_vma=False,
    )
```

```python
import functools

import jax
import jax.numpy as jnp
from jax import lax
from jax.experimental import pallas as pl
from jax.experimental.pallas import tpu as pltpu
from jax.sharding import PartitionSpec as P

WIDTH = 16
COARSEN = 4
NONE = 15
PIECES = 2
BLOCKS = 4
ZERO, CP, LF, CC, RH, RHM, TT, PSI, QQ, XZ, OUT, TMP, DUMP = range(13)
STATES = 13
CPB, LFB, OUTB, CCB, TMPB, LEFT, FIRST, SECOND, FINAL, UNSENT = range(10)
TO_LEFT, TO_FIRST, TO_SECOND, TO_FINAL, TO_CHANGE, TO_RHS, CHANGE, RHS = range(10, 18)
ROUNDED = 18
WEIGHT = ROUNDED
NOTHING, PSI_OF_LEFT, FIRST_POINT, START, PUT_0, PUT_1, PUT_2, OWNER_0, OWNER, CHANGES, KEEP = range(11)
FIELDS = ("src", "dst", "w", "add", "factor", "rsrc", "rdst", "by", "recv", "relay", "need", "op")
BY_ONE, BY_TWO = 0, 1
QUARTER, WHOLE, FOUR = 0, 1, 2
ROUNDED_OF = {CP: CPB, LF: LFB, CC: CCB, OUT: OUTB, TMP: TMPB}


def step(src, dst, w, add=ZERO, factor=QUARTER, send=UNSENT, by=BY_ONE,
         recv=NONE, relay=0, need=0, op=NOTHING, rsrc=None):
    if rsrc is None:
        rsrc = ROUNDED_OF[src] if recv == NONE else recv
    rdst = ROUNDED_OF.get(dst, UNSENT) if send == UNSENT else send
    return dict(src=src, dst=dst, w=w, add=add, factor=factor, rsrc=rsrc, rdst=rdst,
                by=by, recv=recv, relay=relay, need=need, op=op)


def programs():
    def fine(send=UNSENT, first=NOTHING, op=NOTHING):
        return [step(CP, CP, 0, op=first), step(CP, CP, 1), step(CP, CP, 2),
                step(CP, CP, 3, send=send, op=op)]

    def again(send=UNSENT, op=NOTHING):
        return [step(LF, CC, 0, recv=LEFT, op=PSI_OF_LEFT), step(CC, CC, 1),
                step(CC, CC, 2), step(CC, RH, 3, add=QQ, send=send, op=op)]

    def whole(recv, dst, relay=0, need=0):
        return step(TMP, dst, COARSEN, add=RHM, factor=WHOLE, recv=recv, relay=relay, need=need)

    def own(src, dst, **kw):
        return step(src, dst, 0, add=RH, factor=WHOLE, **kw)

    last = [step(OUT, OUT, 1, op=PUT_1), step(OUT, OUT, 2, op=PUT_2)]
    body = fine(TO_LEFT) + again()
    mate = fine(TO_LEFT) + again(TO_RHS)
    final = [whole(FINAL, LF, relay=1)]
    owner_second = [whole(SECOND, TMP), step(TMP, PSI, 0, factor=WHOLE, op=OWNER)]
    relaxed = [whole(FIRST, TMP, need=1), own(TMP, CC)] + final + [
        step(LF, DUMP, 0, factor=WHOLE, op=PUT_0)]
    return {
        "start": fine(TO_LEFT, KEEP, START) + last,
        "lead_first": body + [own(LF, CC, recv=FIRST, send=TO_FIRST, by=BY_TWO, op=PUT_0)] + last,
        "mate_first": mate + [own(LF, CC, recv=FIRST, op=PUT_0)] + last,
        "owner_first": body + [
            step(TMP, XZ, 0, factor=FOUR), whole(FIRST, LF, relay=1, need=1),
            own(LF, CC, op=OWNER_0)] + last,
        "head": fine(TO_LEFT) + again(TO_RHS, FIRST_POINT) + [
            own(LF, CC, recv=FINAL, op=PUT_0)] + last + [
            step(LF, XZ, COARSEN, factor=FOUR, need=2, rsrc=FINAL),
            step(TMP, TMP, COARSEN, factor=FOUR, recv=SECOND, op=CHANGES)],
        "lead": body + [
            own(LF, TMP, recv=FIRST, send=TO_FIRST, by=BY_TWO),
            whole(FINAL, LF, relay=1, need=1),
            own(LF, CC, send=TO_FINAL, by=BY_TWO, op=PUT_0),
            whole(SECOND, TMP, relay=1),
            own(TMP, TMP, send=TO_SECOND, by=BY_TWO)] + last,
        "mate": mate + [own(LF, CC, recv=FINAL, op=PUT_0)] + last,
        "owner": body + relaxed + owner_second + last,
        "owner_last": body + relaxed + last + owner_second,
    }


def packed(values):
    words = []
    for start in (0, 8):
        word = sum(v << (4 * k) for k, v in enumerate(values[start:start + 8]))
        words.append(word - 2**32 if word >= 2**31 else word)
    return words


def kernel(
    devices, x_hbm, g_hbm, w_hbm, o_ref,
    xg, w, st, rounded, part, side_sum, base,
    send_sem, relay_sem, extra_sem, recv_sem, load_sem, weight_sem,
):
    f32, bf16 = jnp.float32, jnp.bfloat16
    p = lax.axis_index("layer")
    phase = lax.rem(p, COARSEN)
    owner = phase == COARSEN - 1
    group = lax.div(p, COARSEN)
    lead = lax.rem(p, 2) == 1
    mate = jnp.logical_not(lead)
    _, cells, chans = st.shape

    own_load = pltpu.make_async_copy(g_hbm.at[0], xg.at[0], load_sem.at[0])
    x_load = pltpu.make_async_copy(x_hbm, xg.at[0], load_sem.at[0])
    start_load = pltpu.make_async_copy(x_hbm, xg.at[1], load_sem.at[1])
    first_owner = jnp.logical_and(owner, group == 0)

    def weight_loads(j):
        rows = w.shape[1] // PIECES
        return [
            pltpu.make_async_copy(
                w_hbm.at[j, pl.ds(n * rows, rows)], w.at[j, pl.ds(n * rows, rows)],
                weight_sem.at[j, n],
            )
            for n in range(PIECES)
        ]

    @pl.when(p == 0)
    def _():
        x_load.start()

    @pl.when(p > 0)
    def _():
        own_load.start()

    for load in weight_loads(0) + weight_loads(1):
        load.start()

    @pl.when(first_owner)
    def _():
        start_load.start()

    barrier = pltpu.get_barrier_semaphore()

    def greet(by, cond):
        @pl.when(cond)
        def _():
            pl.semaphore_signal(
                barrier, inc=1, device_id={"layer": p + by},
                device_id_type=pl.DeviceIdType.MESH,
            )
        return cond.astype(jnp.int32)

    has_next = p < devices - 1
    lead_next = jnp.logical_and(lead, p + 2 < devices)
    last_owner = p + COARSEN >= devices
    greeted = (
        greet(1, has_next) + greet(-1, p > 0)
        + greet(COARSEN - 1, jnp.logical_and(phase == 0, group > 0))
        + greet(1 - COARSEN, jnp.logical_and(owner, group > 0))
        + greet(2, lead_next) + greet(-2, jnp.logical_and(lead, p >= 2))
    )
    shares = jnp.logical_and(mate, p > 0)
    owner_shares = jnp.logical_and(owner, group > 0)
    changes = jnp.logical_and(phase == 0, group > 0)

    roles = [
        ("start", p == 0),
        ("lead_first", jnp.logical_and(group == 0, phase == 1)),
        ("mate_first", jnp.logical_and(group == 0, phase == 2)),
        ("owner_first", first_owner),
        ("head", changes),
        ("lead", jnp.logical_and(group > 0, phase == 1)),
        ("mate", jnp.logical_and(group > 0, phase == 2)),
        ("owner_last", jnp.logical_and(owner, jnp.logical_and(group > 0, last_owner))),
    ]
    listed = programs()

    def chosen(value_of):
        value = jnp.int32(value_of(listed["owner"]))
        for name, cond in roles:
            value = jnp.where(cond, jnp.int32(value_of(listed[name])), value)
        return value

    count = chosen(len)
    words = {
        field: [
            chosen(lambda steps: packed([s[field] for s in steps])[half]) for half in (0, 1)
        ]
        for field in FIELDS
    }

    def entry(field, i):
        low, high = words[field]
        word = jnp.where(i < 8, low, high)
        return jnp.bitwise_and(
            lax.shift_right_logical(word, 4 * jnp.bitwise_and(i, 7)), 15
        )

    def remote(src, dst, ssem, rsem, by):
        return pltpu.make_async_remote_copy(
            src_ref=src, dst_ref=dst, send_sem=ssem, recv_sem=rsem,
            device_id={"layer": p + by}, device_id_type=pl.DeviceIdType.MESH,
        )

    def inner(slot):
        return rounded.at[slot, pl.ds(WIDTH, cells)]

    def landing(slot):
        return jnp.where(slot == TO_RHS, RHS, slot - (TO_LEFT - LEFT))

    def message(slot, by):
        to = landing(slot)
        return remote(inner(slot), inner(to), send_sem.at[slot - TO_LEFT], recv_sem.at[to], by)

    def relay_of(slot):
        return remote(inner(slot), inner(slot), relay_sem.at[slot - LEFT], recv_sem.at[slot], -1)

    back = jnp.where(p > 0, -1, 1)

    def arrived(slot):
        remote(inner(slot), inner(slot), extra_sem.at[0], recv_sem.at[slot], back).wait_recv()

    def weight_to(by):
        return remote(w.at[0], w.at[COARSEN], extra_sem.at[0], recv_sem.at[WEIGHT], by)

    def special(slot, to, by):
        return remote(inner(slot), inner(to), send_sem.at[slot - TO_LEFT], recv_sem.at[to], by)

    def rounded_store(slot, value):
        rounded[slot, WIDTH:WIDTH + cells, :] = value.astype(bf16)

    def distance(code):
        return jnp.where(code == BY_TWO, 2, 1)

    half = chans // 2
    rounded[:, 0:WIDTH, :] = jnp.zeros((ROUNDED, WIDTH, chans), bf16)
    rounded[:, WIDTH + cells:, :] = jnp.zeros((ROUNDED, WIDTH, chans), bf16)
    part[:, :, 0:8, :] = jnp.zeros((2, 2, 8, half), f32)
    part[:, :, 8 + cells:, :] = jnp.zeros((2, 2, 8, half), f32)
    st[ZERO] = jnp.zeros((cells, chans), f32)

    def put(n):
        o_ref[n] = st[OUT].T

    own_load.wait()
    for load in weight_loads(2):
        load.start()
    loaded = xg[0].T
    st[LF] = loaded
    st[CP] = loaded
    rounded_store(CPB, loaded)

    @pl.when(first_owner)
    def _():
        start_load.wait()
        start = xg[1].T
        st[TMP] = start
        rounded_store(TMPB, start)

    def finish_owner(xy):
        cc = st[CC]
        second = st[RH] - (cc - st[PSI])
        solved = st[XZ] + ((cc - st[xy]) + second)

        @pl.when(lead_next)
        def _():
            rounded_store(TO_FINAL, solved)
            special(TO_FINAL, FINAL, 2).start()
            rounded_store(TO_SECOND, cc)
            special(TO_SECOND, SECOND, 2).start()

        st[CC] = solved

    rows_of = cells // BLOCKS
    col = lax.rem(lax.broadcasted_iota(jnp.int32, (rows_of, chans), 0), WIDTH)
    order = [
        [(1, 0), (0, 0), (2, 0), (0, 1), (1, 1)],
        [(1, 2), (0, 2), (2, 2), (2, 1), (1, 1)],
    ]

    def push(which, k, m):
        dy, dx = order[m][k]
        tap = 3 * dy + dx
        pltpu.matmul_push_rhs(
            w[which, :, tap * chans:(tap + 1) * chans], k % 2, m, transpose=True
        )

    def wait_weights(j):
        for load in weight_loads(j):
            load.wait()

    def fields_of(i):
        return tuple(entry(field, i) for field in FIELDS)

    def run(sides, middles, i, fields):
        f = dict(zip(FIELDS, fields))

        @pl.when(i == 1)
        def _():
            pl.semaphore_wait(barrier, greeted)

            @pl.when(shares)
            def _():
                weight_to(1).start()

            @pl.when(owner_shares)
            def _():
                weight_to(1 - COARSEN).start()

        received = f["recv"] != NONE

        @pl.when(received)
        def _():
            arrived(f["recv"])

            @pl.when(f["relay"] == 1)
            def _():
                relay_of(f["recv"]).start()

        source = f["rsrc"]

        def lhs(dy, r):
            return rounded[source, WIDTH * dy + r * rows_of:WIDTH * dy + (r + 1) * rows_of, :]

        def stream(k):
            for m in (0, 1):
                dy = order[m][k][0]
                total = sides[m] if k < 3 else middles[m]
                taken = range(BLOCKS) if k < 4 else range(m, BLOCKS, 2)
                for n, r in enumerate(taken):
                    pltpu.matmul_acc_lhs(total[r], lhs(dy, r), k % 2 if n == 0 else None)

        for m in (0, 1):
            push(f["w"], 1, m)
        stream(0)
        later = fields_of(i + 1)
        following = dict(zip(FIELDS, later))
        next_weight = jnp.logical_and(i + 1 < count, following["need"] > 0)

        @pl.when(jnp.logical_or(i < COARSEN - 1, jnp.logical_or(next_weight, f["need"] > 0)))
        def _():
            @pl.when(i < COARSEN - 1)
            def _():
                wait_weights(i + 1)

            @pl.when(next_weight)
            def _():
                remote(w.at[0], w.at[COARSEN], extra_sem.at[0], recv_sem.at[WEIGHT], back).wait_recv()

            @pl.when(f["need"] == 1)
            def _():
                arrived(RHS)
                st[RHM] = rounded[RHS, WIDTH:WIDTH + cells, :].astype(f32)

        for k in range(1, 5):
            for m in (0, 1):
                if k < 4:
                    push(f["w"], k + 1, m)
            stream(k)
        for m in (0, 1):
            push(following["w"], 0, m)
        for r in range(BLOCKS):
            for m in (0, 1):
                t = pltpu.matmul_pop(sides[m][r])
                t = jnp.where(col == (0 if m else WIDTH - 1), 0.0, t)
                for h in (0, 1):
                    part[m, h, 8 + r * rows_of:8 + (r + 1) * rows_of, :] = t[:, h * half:(h + 1) * half]
        for r in range(BLOCKS):
            for h in (0, 1):
                side_sum[r * rows_of:(r + 1) * rows_of, h * half:(h + 1) * half] = (
                    part[0, h, 7 + r * rows_of:7 + (r + 1) * rows_of, :]
                    + part[1, h, 9 + r * rows_of:9 + (r + 1) * rows_of, :]
                )
        v = jnp.where(received, rounded[source, WIDTH:WIDTH + cells, :].astype(f32), st[f["src"]])
        base[...] = v + st[f["add"]]
        st[f["src"]] = v

        factor = jnp.where(f["factor"] == QUARTER, 0.25, jnp.where(f["factor"] == WHOLE, 1.0, 4.0))
        for r in range(BLOCKS):
            at = slice(r * rows_of, (r + 1) * rows_of)
            t = jnp.tanh(
                (pltpu.matmul_pop(middles[0][r]) + pltpu.matmul_pop(middles[1][r])) + side_sum[at]
            )
            new = base[at] + factor * t
            st[f["dst"], at] = new
            rounded[f["rdst"], WIDTH + r * rows_of:WIDTH + (r + 1) * rows_of, :] = new.astype(bf16)

        @pl.when(jnp.logical_and(f["rdst"] > UNSENT, has_next))
        def _():
            message(f["rdst"], distance(f["by"])).start()

        op = f["op"]

        @pl.when(op != NOTHING)
        def _():
            @pl.when(op == PSI_OF_LEFT)
            def _():
                psi = st[LF] + 4.0 * (st[CC] - base[...])
                st[PSI] = psi
                st[QQ] = (st[CP] - psi) - st[CP]

            @pl.when(op == KEEP)
            def _():
                st[TT] = 4.0 * (st[CP] - base[...])

            @pl.when(op == START)
            def _():
                psi = st[LF] + st[TT]
                rhs = st[CP] + ((st[CP] - psi) - st[CP])
                first = psi + rhs
                st[CC] = first
                rounded_store(TO_FIRST, first)
                special(TO_FIRST, FIRST, 1).start()

            @pl.when(op == FIRST_POINT)
            def _():
                rounded_store(TO_FIRST, st[PSI] + st[RH])
                special(TO_FIRST, FIRST, 1).start()

            @pl.when(op == OWNER_0)
            def _():
                t = st[CC] - base[...]
                st[TT] = t
                st[PSI] = st[LF] + t
                finish_owner(XZ)

            @pl.when(jnp.logical_or(op == PUT_0, jnp.logical_or(op == START, op == OWNER_0)))
            def _():
                t = jnp.where(op == PUT_0, st[f["dst"]] - base[...], st[TT])
                out = st[LF] + 0.25 * t
                st[OUT] = out
                rounded_store(OUTB, out)

            put_at = jnp.where(op == PUT_1, 1, jnp.where(op == PUT_2, 2, 0))

            @pl.when(jnp.logical_and(op >= START, op <= OWNER_0))
            def _():
                put(put_at)

            @pl.when(op == OWNER)
            def _():
                arrived(CHANGE)
                st[XZ] = rounded[CHANGE, WIDTH:WIDTH + cells, :].astype(f32)
                finish_owner(ZERO)

            @pl.when(op == CHANGES)
            def _():
                rounded_store(TO_CHANGE, st[XZ] - st[TMP])
                special(TO_CHANGE, CHANGE, COARSEN - 1).start()

        return later

    def loop(*totals):
        sides = (totals[:BLOCKS], totals[2 * BLOCKS:3 * BLOCKS])
        middles = (totals[BLOCKS:2 * BLOCKS], totals[3 * BLOCKS:])
        wait_weights(0)
        for load in weight_loads(3):
            load.start()
        for m in (0, 1):
            push(0, 0, m)
        lax.fori_loop(0, count, functools.partial(run, sides, middles), fields_of(0))
        for m in (0, 1):
            pltpu.matmul_acc_lhs(sides[m][0], rounded[CPB, 0:rows_of, :], 0)
            side_sum[0:rows_of, :] = pltpu.matmul_pop(sides[m][0])

    pl.run_scoped(
        loop, *[pltpu.ACC(m)((rows_of, chans), f32) for m in (0, 1) for _ in range(2 * BLOCKS)]
    )
    o_ref[COARSEN - 1] = st[CC].T

    def drain(copy, cond):
        @pl.when(cond)
        def _():
            copy.wait_send()

    relaxed = jnp.logical_or(
        jnp.logical_and(owner, lead_next), jnp.logical_and(phase == 1, group > 0)
    )
    drain(weight_to(back), jnp.logical_or(shares, owner_shares))
    drain(special(TO_LEFT, LEFT, back), has_next)
    drain(special(TO_RHS, RHS, back), shares)
    drain(special(TO_FIRST, FIRST, back), phase < 2)
    drain(special(TO_FINAL, FINAL, back), relaxed)
    drain(special(TO_SECOND, SECOND, back), relaxed)
    drain(special(TO_CHANGE, CHANGE, back), changes)
    drain(relay_of(FIRST), first_owner)
    drain(relay_of(FINAL), jnp.logical_and(lead, group > 0))
    drain(relay_of(SECOND), jnp.logical_and(phase == 1, group > 0))


def per_device(devices, inputs, guess, weights):
    chans, cells = inputs.shape
    return pl.pallas_call(
        functools.partial(kernel, devices),
        name="cycle",
        out_shape=pltpu.VMEM((COARSEN, chans, cells), jnp.float32),
        in_specs=[pl.BlockSpec(memory_space=pltpu.HBM)] * 3,
        out_specs=pl.BlockSpec(memory_space=pltpu.VMEM),
        scratch_shapes=[
            pltpu.VMEM((2, chans, cells), jnp.float32),
            pltpu.VMEM((COARSEN + 1,) + weights.shape[1:], jnp.bfloat16),
            pltpu.VMEM((STATES, cells, chans), jnp.float32),
            pltpu.VMEM((ROUNDED, cells + 2 * WIDTH, chans), jnp.bfloat16),
            pltpu.VMEM((2, 2, cells + 16, chans // 2), jnp.float32),
            pltpu.VMEM((cells, chans), jnp.float32),
            pltpu.VMEM((cells, chans), jnp.float32),
            pltpu.SemaphoreType.DMA((TO_RHS - TO_LEFT + 1,)),
            pltpu.SemaphoreType.DMA((FINAL - LEFT + 1,)),
            pltpu.SemaphoreType.DMA((1,)),
            pltpu.SemaphoreType.DMA((ROUNDED + 1,)),
            pltpu.SemaphoreType.DMA((2,)),
            pltpu.SemaphoreType.DMA((COARSEN, PIECES)),
        ],
        compiler_params=pltpu.CompilerParams(
            collective_id=0, has_side_effects=True, vmem_limit_bytes=56 * 2**20,
        ),
    )(*[pltpu.with_memory_space_constraint(a, pltpu.HBM) for a in (inputs, guess, weights)])


def solution(mesh):
    return jax.shard_map(
        functools.partial(per_device, mesh.shape["layer"]),
        mesh=mesh,
        in_specs=(P(None, "batch"), P("layer", None, "batch"), P("layer", None, None)),
        out_specs=P("layer", None, "batch"),
        check_vma=False,
    )
```

```python
import functools

import jax
import jax.numpy as jnp
from jax import lax
from jax.experimental import pallas as pl
from jax.experimental.pallas import tpu as pltpu
from jax.sharding import PartitionSpec as P

WIDTH = 16
COARSEN = 4
NONE = 15
PIECES = 2
BLOCKS = 4
ROWS = 32
ZERO, CP, LF, CC, RH, RHM, TT, PSI, QQ, XZ, OUT, TMP, DUMP = range(13)
STATES = 13
CPB, LFB, OUTB, CCB, TMPB, LEFT, FIRST, SECOND, FINAL, UNSENT = range(10)
TO_LEFT, TO_FIRST, TO_SECOND, TO_FINAL, TO_CHANGE, TO_RHS, CHANGE, RHS = range(10, 18)
ROUNDED = 18
WEIGHT = ROUNDED
NOTHING, PSI_OF_LEFT, FIRST_POINT, CHANGES, KEEP, START, PUT_0, OWNER_0, PUT_1, PUT_2, PUT_LAST, OWNER = range(12)
FIELDS = ("src", "dst", "w", "add", "factor", "rsrc", "rdst", "by", "recv", "relay", "need", "op")
BY_ONE, BY_TWO = 0, 1
QUARTER, WHOLE, FOUR = 0, 1, 2
ROUNDED_OF = {CP: CPB, LF: LFB, CC: CCB, OUT: OUTB, TMP: TMPB}


def step(src, dst, w, add=ZERO, factor=QUARTER, send=UNSENT, by=BY_ONE,
         recv=NONE, relay=0, need=0, op=NOTHING, rsrc=None):
    if rsrc is None:
        rsrc = ROUNDED_OF[src] if recv == NONE else recv
    rdst = ROUNDED_OF.get(dst, UNSENT) if send == UNSENT else send
    return dict(src=src, dst=dst, w=w, add=add, factor=factor, rsrc=rsrc, rdst=rdst,
                by=by, recv=recv, relay=relay, need=need, op=op)


def programs():
    def fine(send=UNSENT, first=NOTHING, op=NOTHING):
        return [step(CP, CP, 0, op=first), step(CP, CP, 1), step(CP, CP, 2),
                step(CP, CP, 3, send=send, op=op)]

    def again(send=UNSENT, op=NOTHING):
        return [step(LF, CC, 0, recv=LEFT, op=PSI_OF_LEFT), step(CC, CC, 1),
                step(CC, CC, 2), step(CC, RH, 3, add=QQ, send=send, op=op)]

    def whole(recv, dst, relay=0, need=0):
        return step(TMP, dst, COARSEN, add=RHM, factor=WHOLE, recv=recv, relay=relay, need=need)

    def own(src, dst, **kw):
        return step(src, dst, 0, add=RH, factor=WHOLE, **kw)

    last = [step(OUT, OUT, 1, op=PUT_1), step(OUT, OUT, 2, op=PUT_LAST)]
    early = [step(OUT, OUT, 1, op=PUT_1), step(OUT, OUT, 2, op=PUT_2)]
    body = fine(TO_LEFT) + again()
    mate = fine(TO_LEFT) + again(TO_RHS)
    final = [whole(FINAL, LF, relay=1)]
    owner_second = [whole(SECOND, TMP), step(TMP, PSI, 0, factor=WHOLE, op=OWNER)]
    relaxed = [whole(FIRST, TMP, need=1), own(TMP, CC)] + final + [
        step(LF, DUMP, 0, factor=WHOLE, op=PUT_0)]
    return {
        "start": fine(TO_LEFT, KEEP, START) + last,
        "lead_first": body + [own(LF, CC, recv=FIRST, send=TO_FIRST, by=BY_TWO, op=PUT_0)] + last,
        "mate_first": mate + [own(LF, CC, recv=FIRST, op=PUT_0)] + last,
        "owner_first": body + [
            step(TMP, XZ, 0, factor=FOUR), whole(FIRST, LF, relay=1, need=1),
            own(LF, CC, op=OWNER_0)] + last,
        "head": fine(TO_LEFT) + again(TO_RHS, FIRST_POINT) + [
            own(LF, CC, recv=FINAL, op=PUT_0)] + last + [
            step(LF, XZ, COARSEN, factor=FOUR, need=2, rsrc=FINAL),
            step(TMP, TMP, COARSEN, factor=FOUR, recv=SECOND, op=CHANGES)],
        "lead": body + [
            own(LF, TMP, recv=FIRST, send=TO_FIRST, by=BY_TWO),
            whole(FINAL, LF, relay=1, need=1),
            own(LF, CC, send=TO_FINAL, by=BY_TWO, op=PUT_0),
            whole(SECOND, TMP, relay=1),
            own(TMP, TMP, send=TO_SECOND, by=BY_TWO)] + last,
        "mate": mate + [own(LF, CC, recv=FINAL, op=PUT_0)] + last,
        "owner": body + relaxed + owner_second + last,
        "owner_last": body + relaxed + early + owner_second,
    }


def packed(values):
    words = []
    for start in (0, 8):
        word = sum(v << (4 * k) for k, v in enumerate(values[start:start + 8]))
        words.append(word - 2**32 if word >= 2**31 else word)
    return words


def kernel(
    devices, x_hbm, g_hbm, w_hbm, o_ref,
    xg, w, st, rounded, part, side_sum, base,
    send_sem, relay_sem, extra_sem, recv_sem, load_sem, weight_sem,
):
    f32, bf16 = jnp.float32, jnp.bfloat16
    p = lax.axis_index("layer")
    phase = lax.rem(p, COARSEN)
    owner = phase == COARSEN - 1
    group = lax.div(p, COARSEN)
    lead = lax.rem(p, 2) == 1
    mate = jnp.logical_not(lead)
    _, cells, chans = st.shape

    own_load = pltpu.make_async_copy(g_hbm.at[0], xg.at[0], load_sem.at[0])
    x_load = pltpu.make_async_copy(x_hbm, xg.at[0], load_sem.at[0])
    start_load = pltpu.make_async_copy(x_hbm, xg.at[1], load_sem.at[1])
    first_owner = jnp.logical_and(owner, group == 0)

    def weight_loads(j):
        rows = w.shape[1] // PIECES
        return [
            pltpu.make_async_copy(
                w_hbm.at[j, pl.ds(n * rows, rows)], w.at[j, pl.ds(n * rows, rows)],
                weight_sem.at[j, n],
            )
            for n in range(PIECES)
        ]

    @pl.when(p == 0)
    def _():
        x_load.start()

    @pl.when(p > 0)
    def _():
        own_load.start()

    for load in weight_loads(0) + weight_loads(1):
        load.start()

    @pl.when(first_owner)
    def _():
        start_load.start()

    barrier = pltpu.get_barrier_semaphore()

    def greet(by, cond):
        @pl.when(cond)
        def _():
            pl.semaphore_signal(
                barrier, inc=1, device_id={"layer": p + by},
                device_id_type=pl.DeviceIdType.MESH,
            )
        return cond.astype(jnp.int32)

    has_next = p < devices - 1
    lead_next = jnp.logical_and(lead, p + 2 < devices)
    last_owner = p + COARSEN >= devices
    greeted = (
        greet(1, has_next) + greet(-1, p > 0)
        + greet(COARSEN - 1, jnp.logical_and(phase == 0, group > 0))
        + greet(1 - COARSEN, jnp.logical_and(owner, group > 0))
        + greet(2, lead_next) + greet(-2, jnp.logical_and(lead, p >= 2))
    )
    shares = jnp.logical_and(mate, p > 0)
    owner_shares = jnp.logical_and(owner, group > 0)
    changes = jnp.logical_and(phase == 0, group > 0)

    roles = [
        ("start", p == 0),
        ("lead_first", jnp.logical_and(group == 0, phase == 1)),
        ("mate_first", jnp.logical_and(group == 0, phase == 2)),
        ("owner_first", first_owner),
        ("head", changes),
        ("lead", jnp.logical_and(group > 0, phase == 1)),
        ("mate", jnp.logical_and(group > 0, phase == 2)),
        ("owner_last", jnp.logical_and(owner, jnp.logical_and(group > 0, last_owner))),
    ]
    listed = programs()

    def chosen(value_of):
        value = jnp.int32(value_of(listed["owner"]))
        for name, cond in roles:
            value = jnp.where(cond, jnp.int32(value_of(listed[name])), value)
        return value

    count = chosen(len)
    words = {
        field: [
            chosen(lambda steps: packed([s[field] for s in steps])[half]) for half in (0, 1)
        ]
        for field in FIELDS
    }

    def entry(field, i):
        low, high = words[field]
        word = jnp.where(i < 8, low, high)
        return jnp.bitwise_and(
            lax.shift_right_logical(word, 4 * jnp.bitwise_and(i, 7)), 15
        )

    def remote(src, dst, ssem, rsem, by):
        return pltpu.make_async_remote_copy(
            src_ref=src, dst_ref=dst, send_sem=ssem, recv_sem=rsem,
            device_id={"layer": p + by}, device_id_type=pl.DeviceIdType.MESH,
        )

    def inner(slot):
        return rounded.at[slot, pl.ds(WIDTH, cells)]

    def landing(slot):
        return jnp.where(slot == TO_RHS, RHS, slot - (TO_LEFT - LEFT))

    def message(slot, by):
        to = landing(slot)
        return remote(inner(slot), inner(to), send_sem.at[slot - TO_LEFT], recv_sem.at[to], by)

    def relay_of(slot):
        return remote(inner(slot), inner(slot), relay_sem.at[slot - LEFT], recv_sem.at[slot], -1)

    back = jnp.where(p > 0, -1, 1)

    def arrived(slot):
        remote(inner(slot), inner(slot), extra_sem.at[0], recv_sem.at[slot], back).wait_recv()

    def weight_to(by):
        return remote(w.at[0], w.at[COARSEN], extra_sem.at[0], recv_sem.at[WEIGHT], by)

    def special(slot, to, by):
        return remote(inner(slot), inner(to), send_sem.at[slot - TO_LEFT], recv_sem.at[to], by)

    def rounded_store(slot, value):
        rounded[slot, WIDTH:WIDTH + cells, :] = value.astype(bf16)

    def distance(code):
        return jnp.where(code == BY_TWO, 2, 1)

    half = chans // 2
    rounded[:, 0:WIDTH, :] = jnp.zeros((ROUNDED, WIDTH, chans), bf16)
    rounded[:, WIDTH + cells:, :] = jnp.zeros((ROUNDED, WIDTH, chans), bf16)
    part[:, :, 0:8, :] = jnp.zeros((2, 2, 8, half), f32)
    part[:, :, 8 + cells:, :] = jnp.zeros((2, 2, 8, half), f32)
    st[ZERO] = jnp.zeros((cells, chans), f32)

    def put(slot, n):
        o_ref[n] = st[slot].T

    def by_rows(body):
        def rows(r, _):
            first = pl.multiple_of(r * ROWS, ROWS)
            body(pl.ds(first, ROWS), pl.ds(WIDTH + first, ROWS))
            return 0

        lax.fori_loop(0, cells // ROWS, rows, 0)

    own_load.wait()
    for load in weight_loads(2):
        load.start()
    loaded = xg[0].T
    st[LF] = loaded
    st[CP] = loaded
    rounded_store(CPB, loaded)

    @pl.when(first_owner)
    def _():
        start_load.wait()
        start = xg[1].T
        st[TMP] = start
        rounded_store(TMPB, start)

    def send_solved():
        @pl.when(lead_next)
        def _():
            special(TO_FINAL, FINAL, 2).start()
            special(TO_SECOND, SECOND, 2).start()

    def solve(at, inner_at, psi, xz, xy):
        cc = st[CC, at]
        second = st[RH, at] - (cc - psi)
        solved = xz + ((cc - xy) + second)
        rounded[TO_FINAL, inner_at] = solved.astype(bf16)
        rounded[TO_SECOND, inner_at] = cc.astype(bf16)
        st[CC, at] = solved

    rows_of = cells // BLOCKS
    col = lax.rem(lax.broadcasted_iota(jnp.int32, (rows_of, chans), 0), WIDTH)
    order = [
        [(1, 0), (0, 0), (2, 0), (0, 1), (1, 1)],
        [(1, 2), (0, 2), (2, 2), (2, 1), (1, 1)],
    ]

    def push(which, k, m):
        dy, dx = order[m][k]
        tap = 3 * dy + dx
        pltpu.matmul_push_rhs(
            w[which, :, tap * chans:(tap + 1) * chans], k % 2, m, transpose=True
        )

    def wait_weights(j):
        for load in weight_loads(j):
            load.wait()

    def fields_of(i):
        return tuple(entry(field, i) for field in FIELDS)

    def run(sides, middles, i, fields):
        f = dict(zip(FIELDS, fields))

        @pl.when(i == 1)
        def _():
            pl.semaphore_wait(barrier, greeted)

            @pl.when(shares)
            def _():
                weight_to(1).start()

            @pl.when(owner_shares)
            def _():
                weight_to(1 - COARSEN).start()

        received = f["recv"] != NONE

        @pl.when(received)
        def _():
            arrived(f["recv"])

            @pl.when(f["relay"] == 1)
            def _():
                relay_of(f["recv"]).start()

        source = f["rsrc"]

        def lhs(dy, r):
            return rounded[source, WIDTH * dy + r * rows_of:WIDTH * dy + (r + 1) * rows_of, :]

        def stream(k):
            for m in (0, 1):
                dy = order[m][k][0]
                total = sides[m] if k < 3 else middles[m]
                taken = range(BLOCKS) if k < 4 else range(m, BLOCKS, 2)
                for n, r in enumerate(taken):
                    pltpu.matmul_acc_lhs(total[r], lhs(dy, r), k % 2 if n == 0 else None)

        for m in (0, 1):
            push(f["w"], 1, m)
        stream(0)
        later = fields_of(i + 1)
        following = dict(zip(FIELDS, later))
        next_weight = jnp.logical_and(i + 1 < count, following["need"] > 0)

        @pl.when(jnp.logical_or(i < COARSEN - 1, jnp.logical_or(next_weight, f["need"] > 0)))
        def _():
            @pl.when(i < COARSEN - 1)
            def _():
                wait_weights(i + 1)

            @pl.when(next_weight)
            def _():
                remote(w.at[0], w.at[COARSEN], extra_sem.at[0], recv_sem.at[WEIGHT], back).wait_recv()

            @pl.when(f["need"] == 1)
            def _():
                arrived(RHS)
                st[RHM] = rounded[RHS, WIDTH:WIDTH + cells, :].astype(f32)

        for k in range(1, 5):
            for m in (0, 1):
                if k < 4:
                    push(f["w"], k + 1, m)
            stream(k)
        for m in (0, 1):
            push(following["w"], 0, m)
        for r in range(BLOCKS):
            for m in (0, 1):
                t = pltpu.matmul_pop(sides[m][r])
                t = jnp.where(col == (0 if m else WIDTH - 1), 0.0, t)
                for h in (0, 1):
                    part[m, h, 8 + r * rows_of:8 + (r + 1) * rows_of, :] = t[:, h * half:(h + 1) * half]
        for r in range(BLOCKS):
            for h in (0, 1):
                side_sum[r * rows_of:(r + 1) * rows_of, h * half:(h + 1) * half] = (
                    part[0, h, 7 + r * rows_of:7 + (r + 1) * rows_of, :]
                    + part[1, h, 9 + r * rows_of:9 + (r + 1) * rows_of, :]
                )
        v = jnp.where(received, rounded[source, WIDTH:WIDTH + cells, :].astype(f32), st[f["src"]])
        base[...] = v + st[f["add"]]
        st[f["src"]] = v

        factor = jnp.where(f["factor"] == QUARTER, 0.25, jnp.where(f["factor"] == WHOLE, 1.0, 4.0))
        for r in range(BLOCKS):
            at = slice(r * rows_of, (r + 1) * rows_of)
            t = jnp.tanh(
                (pltpu.matmul_pop(middles[0][r]) + pltpu.matmul_pop(middles[1][r])) + side_sum[at]
            )
            new = base[at] + factor * t
            st[f["dst"], at] = new
            rounded[f["rdst"], WIDTH + r * rows_of:WIDTH + (r + 1) * rows_of, :] = new.astype(bf16)

        @pl.when(jnp.logical_and(f["rdst"] > UNSENT, has_next))
        def _():
            message(f["rdst"], distance(f["by"])).start()

        op = f["op"]

        @pl.when(op != NOTHING)
        def _():
            @pl.when(op == PSI_OF_LEFT)
            def _():
                def rows(at, _):
                    psi = st[LF, at] + 4.0 * (st[CC, at] - base[at])
                    st[PSI, at] = psi
                    st[QQ, at] = (st[CP, at] - psi) - st[CP, at]

                by_rows(rows)

            @pl.when(op == KEEP)
            def _():
                def rows(at, _):
                    st[TT, at] = 4.0 * (st[CP, at] - base[at])

                by_rows(rows)

            @pl.when(op == START)
            def _():
                def rows(at, inner_at):
                    psi = st[LF, at] + st[TT, at]
                    rhs = st[CP, at] + ((st[CP, at] - psi) - st[CP, at])
                    first = psi + rhs
                    st[CC, at] = first
                    rounded[TO_FIRST, inner_at] = first.astype(bf16)

                by_rows(rows)
                special(TO_FIRST, FIRST, 1).start()

            @pl.when(op == FIRST_POINT)
            def _():
                def rows(at, inner_at):
                    rounded[TO_FIRST, inner_at] = (st[PSI, at] + st[RH, at]).astype(bf16)

                by_rows(rows)
                special(TO_FIRST, FIRST, 1).start()

            @pl.when(op == OWNER_0)
            def _():
                def rows(at, inner_at):
                    t = st[CC, at] - base[at]
                    st[TT, at] = t
                    solve(at, inner_at, st[LF, at] + t, st[XZ, at], st[XZ, at])

                by_rows(rows)
                send_solved()

            @pl.when(jnp.logical_and(op >= START, op <= OWNER_0))
            def _():
                def rows(at, inner_at):
                    t = jnp.where(op == PUT_0, st[f["dst"], at] - base[at], st[TT, at])
                    out = st[LF, at] + 0.25 * t
                    st[OUT, at] = out
                    rounded[OUTB, inner_at] = out.astype(bf16)

                by_rows(rows)

            @pl.when(op == OWNER)
            def _():
                arrived(CHANGE)

                def rows(at, inner_at):
                    change = rounded[CHANGE, inner_at].astype(f32)
                    solve(at, inner_at, st[PSI, at], change, st[ZERO, at])

                by_rows(rows)
                send_solved()

            @pl.when(op >= START)
            def _():
                whole_put = op == OWNER

                def one(n, _):
                    put_last = jnp.logical_or(whole_put, n == 1)
                    place = jnp.where(op >= PUT_1, op - PUT_1 + 1, 0)
                    put(
                        jnp.where(put_last, CC, OUT),
                        jnp.where(put_last, COARSEN - 1, jnp.minimum(place, COARSEN - 2)),
                    )
                    return 0

                lax.fori_loop(0, jnp.where(op == PUT_LAST, 2, 1), one, 0)

            @pl.when(op == CHANGES)
            def _():
                def rows(at, inner_at):
                    rounded[TO_CHANGE, inner_at] = (st[XZ, at] - st[TMP, at]).astype(bf16)

                by_rows(rows)
                special(TO_CHANGE, CHANGE, COARSEN - 1).start()

        return later

    def loop(*totals):
        sides = (totals[:BLOCKS], totals[2 * BLOCKS:3 * BLOCKS])
        middles = (totals[BLOCKS:2 * BLOCKS], totals[3 * BLOCKS:])
        wait_weights(0)
        for load in weight_loads(3):
            load.start()
        for m in (0, 1):
            push(0, 0, m)
        lax.fori_loop(0, count, functools.partial(run, sides, middles), fields_of(0))
        for m in (0, 1):
            pltpu.matmul_acc_lhs(sides[m][0], rounded[CPB, 0:rows_of, :], 0)
            side_sum[0:rows_of, :] = pltpu.matmul_pop(sides[m][0])

    pl.run_scoped(
        loop, *[pltpu.ACC(m)((rows_of, chans), f32) for m in (0, 1) for _ in range(2 * BLOCKS)]
    )

    def drain(copy, cond):
        @pl.when(cond)
        def _():
            copy.wait_send()

    relaxed = jnp.logical_or(
        jnp.logical_and(owner, lead_next), jnp.logical_and(phase == 1, group > 0)
    )
    drain(weight_to(back), jnp.logical_or(shares, owner_shares))
    drain(special(TO_LEFT, LEFT, back), has_next)
    drain(special(TO_RHS, RHS, back), shares)
    drain(special(TO_FIRST, FIRST, back), phase < 2)
    drain(special(TO_FINAL, FINAL, back), relaxed)
    drain(special(TO_SECOND, SECOND, back), relaxed)
    drain(special(TO_CHANGE, CHANGE, back), changes)
    drain(relay_of(FIRST), first_owner)
    drain(relay_of(FINAL), jnp.logical_and(lead, group > 0))
    drain(relay_of(SECOND), jnp.logical_and(phase == 1, group > 0))


def per_device(devices, inputs, guess, weights):
    chans, cells = inputs.shape
    return pl.pallas_call(
        functools.partial(kernel, devices),
        name="cycle",
        out_shape=pltpu.VMEM((COARSEN, chans, cells), jnp.float32),
        in_specs=[pl.BlockSpec(memory_space=pltpu.HBM)] * 3,
        out_specs=pl.BlockSpec(memory_space=pltpu.VMEM),
        scratch_shapes=[
            pltpu.VMEM((2, chans, cells), jnp.float32),
            pltpu.VMEM((COARSEN + 1,) + weights.shape[1:], jnp.bfloat16),
            pltpu.VMEM((STATES, cells, chans), jnp.float32),
            pltpu.VMEM((ROUNDED, cells + 2 * WIDTH, chans), jnp.bfloat16),
            pltpu.VMEM((2, 2, cells + 16, chans // 2), jnp.float32),
            pltpu.VMEM((cells, chans), jnp.float32),
            pltpu.VMEM((cells, chans), jnp.float32),
            pltpu.SemaphoreType.DMA((TO_RHS - TO_LEFT + 1,)),
            pltpu.SemaphoreType.DMA((FINAL - LEFT + 1,)),
            pltpu.SemaphoreType.DMA((1,)),
            pltpu.SemaphoreType.DMA((ROUNDED + 1,)),
            pltpu.SemaphoreType.DMA((2,)),
            pltpu.SemaphoreType.DMA((COARSEN, PIECES)),
        ],
        compiler_params=pltpu.CompilerParams(
            collective_id=0, has_side_effects=True, vmem_limit_bytes=56 * 2**20,
        ),
    )(*[pltpu.with_memory_space_constraint(a, pltpu.HBM) for a in (inputs, guess, weights)])


def solution(mesh):
    return jax.shard_map(
        functools.partial(per_device, mesh.shape["layer"]),
        mesh=mesh,
        in_specs=(P(None, "batch"), P("layer", None, "batch"), P("layer", None, None)),
        out_specs=P("layer", None, "batch"),
        check_vma=False,
    )
```

```python
import functools

import jax
import jax.numpy as jnp
from jax import lax
from jax.experimental import pallas as pl
from jax.experimental.pallas import tpu as pltpu
from jax.sharding import PartitionSpec as P

WIDTH = 16
COARSEN = 4
NONE = 15
PIECES = 2
BLOCKS = 8
ZERO, CP, LF, CC, RH, RHM, TT, PSI, QQ, XZ, OUT, TMP, DUMP = range(13)
STATES = 13
CPB, LFB, OUTB, CCB, TMPB, LEFT, FIRST, SECOND, FINAL, UNSENT = range(10)
TO_LEFT, TO_FIRST, TO_SECOND, TO_FINAL, TO_CHANGE, TO_RHS, CHANGE, RHS = range(10, 18)
ROUNDED = 18
WEIGHT = ROUNDED
NOTHING, PSI_OF_LEFT, FIRST_POINT, START, PUT_0, PUT_1, PUT_2, OWNER_0, OWNER, CHANGES, KEEP = range(11)
FIELDS = ("src", "dst", "w", "add", "factor", "rsrc", "rdst", "by", "recv", "relay", "need", "op")
BY_ONE, BY_TWO = 0, 1
QUARTER, WHOLE, FOUR = 0, 1, 2
ROUNDED_OF = {CP: CPB, LF: LFB, CC: CCB, OUT: OUTB, TMP: TMPB}


def step(src, dst, w, add=ZERO, factor=QUARTER, send=UNSENT, by=BY_ONE,
         recv=NONE, relay=0, need=0, op=NOTHING, rsrc=None):
    if rsrc is None:
        rsrc = ROUNDED_OF[src] if recv == NONE else recv
    rdst = ROUNDED_OF.get(dst, UNSENT) if send == UNSENT else send
    return dict(src=src, dst=dst, w=w, add=add, factor=factor, rsrc=rsrc, rdst=rdst,
                by=by, recv=recv, relay=relay, need=need, op=op)


def programs():
    def fine(send=UNSENT, first=NOTHING, op=NOTHING):
        return [step(CP, CP, 0, op=first), step(CP, CP, 1), step(CP, CP, 2),
                step(CP, CP, 3, send=send, op=op)]

    def again(send=UNSENT, op=NOTHING):
        return [step(LF, CC, 0, recv=LEFT, op=PSI_OF_LEFT), step(CC, CC, 1),
                step(CC, CC, 2), step(CC, RH, 3, add=QQ, send=send, op=op)]

    def whole(recv, dst, relay=0, need=0):
        return step(TMP, dst, COARSEN, add=RHM, factor=WHOLE, recv=recv, relay=relay, need=need)

    def own(src, dst, **kw):
        return step(src, dst, 0, add=RH, factor=WHOLE, **kw)

    last = [step(OUT, OUT, 1, op=PUT_1), step(OUT, OUT, 2, op=PUT_2)]
    body = fine(TO_LEFT) + again()
    mate = fine(TO_LEFT) + again(TO_RHS)
    final = [whole(FINAL, LF, relay=1)]
    owner_second = [whole(SECOND, TMP), step(TMP, PSI, 0, factor=WHOLE, op=OWNER)]
    relaxed = [whole(FIRST, TMP, need=1), own(TMP, CC)] + final + [
        step(LF, DUMP, 0, factor=WHOLE, op=PUT_0)]
    return {
        "start": fine(TO_LEFT, KEEP, START) + last,
        "lead_first": body + [own(LF, CC, recv=FIRST, send=TO_FIRST, by=BY_TWO, op=PUT_0)] + last,
        "mate_first": mate + [own(LF, CC, recv=FIRST, op=PUT_0)] + last,
        "owner_first": body + [
            step(TMP, XZ, 0, factor=FOUR), whole(FIRST, LF, relay=1, need=1),
            own(LF, CC, op=OWNER_0)] + last,
        "head": fine(TO_LEFT) + again(TO_RHS, FIRST_POINT) + [
            own(LF, CC, recv=FINAL, op=PUT_0)] + last + [
            step(LF, XZ, COARSEN, factor=FOUR, need=2, rsrc=FINAL),
            step(TMP, TMP, COARSEN, factor=FOUR, recv=SECOND, op=CHANGES)],
        "lead": body + [
            own(LF, TMP, recv=FIRST, send=TO_FIRST, by=BY_TWO),
            whole(FINAL, LF, relay=1, need=1),
            own(LF, CC, send=TO_FINAL, by=BY_TWO, op=PUT_0),
            whole(SECOND, TMP, relay=1),
            own(TMP, TMP, send=TO_SECOND, by=BY_TWO)] + last,
        "mate": mate + [own(LF, CC, recv=FINAL, op=PUT_0)] + last,
        "owner": body + relaxed + owner_second + last,
        "owner_last": body + relaxed + last + owner_second,
    }


def packed(values):
    words = []
    for start in (0, 8):
        word = sum(v << (4 * k) for k, v in enumerate(values[start:start + 8]))
        words.append(word - 2**32 if word >= 2**31 else word)
    return words


def kernel(
    devices, x_hbm, g_hbm, w_hbm, o_ref,
    xg, w, st, rounded, part, side_sum, base,
    send_sem, relay_sem, extra_sem, recv_sem, load_sem, weight_sem,
):
    f32, bf16 = jnp.float32, jnp.bfloat16
    p = lax.axis_index("layer")
    phase = lax.rem(p, COARSEN)
    owner = phase == COARSEN - 1
    group = lax.div(p, COARSEN)
    lead = lax.rem(p, 2) == 1
    mate = jnp.logical_not(lead)
    _, cells, chans = st.shape

    own_load = pltpu.make_async_copy(g_hbm.at[0], xg.at[0], load_sem.at[0])
    x_load = pltpu.make_async_copy(x_hbm, xg.at[0], load_sem.at[0])
    start_load = pltpu.make_async_copy(x_hbm, xg.at[1], load_sem.at[1])
    first_owner = jnp.logical_and(owner, group == 0)

    def weight_loads(j):
        rows = w.shape[1] // PIECES
        return [
            pltpu.make_async_copy(
                w_hbm.at[j, pl.ds(n * rows, rows)], w.at[j, pl.ds(n * rows, rows)],
                weight_sem.at[j, n],
            )
            for n in range(PIECES)
        ]

    @pl.when(p == 0)
    def _():
        x_load.start()

    @pl.when(p > 0)
    def _():
        own_load.start()

    for load in weight_loads(0) + weight_loads(1):
        load.start()

    @pl.when(first_owner)
    def _():
        start_load.start()

    barrier = pltpu.get_barrier_semaphore()

    def greet(by, cond):
        @pl.when(cond)
        def _():
            pl.semaphore_signal(
                barrier, inc=1, device_id={"layer": p + by},
                device_id_type=pl.DeviceIdType.MESH,
            )
        return cond.astype(jnp.int32)

    has_next = p < devices - 1
    lead_next = jnp.logical_and(lead, p + 2 < devices)
    last_owner = p + COARSEN >= devices
    greeted = (
        greet(1, has_next) + greet(-1, p > 0)
        + greet(COARSEN - 1, jnp.logical_and(phase == 0, group > 0))
        + greet(1 - COARSEN, jnp.logical_and(owner, group > 0))
        + greet(2, lead_next) + greet(-2, jnp.logical_and(lead, p >= 2))
    )
    shares = jnp.logical_and(mate, p > 0)
    owner_shares = jnp.logical_and(owner, group > 0)
    changes = jnp.logical_and(phase == 0, group > 0)

    roles = [
        ("start", p == 0),
        ("lead_first", jnp.logical_and(group == 0, phase == 1)),
        ("mate_first", jnp.logical_and(group == 0, phase == 2)),
        ("owner_first", first_owner),
        ("head", changes),
        ("lead", jnp.logical_and(group > 0, phase == 1)),
        ("mate", jnp.logical_and(group > 0, phase == 2)),
        ("owner_last", jnp.logical_and(owner, jnp.logical_and(group > 0, last_owner))),
    ]
    listed = programs()

    def chosen(value_of):
        value = jnp.int32(value_of(listed["owner"]))
        for name, cond in roles:
            value = jnp.where(cond, jnp.int32(value_of(listed[name])), value)
        return value

    count = chosen(len)
    words = {
        field: [
            chosen(lambda steps: packed([s[field] for s in steps])[half]) for half in (0, 1)
        ]
        for field in FIELDS
    }

    def entry(field, i):
        low, high = words[field]
        word = jnp.where(i < 8, low, high)
        return jnp.bitwise_and(
            lax.shift_right_logical(word, 4 * jnp.bitwise_and(i, 7)), 15
        )

    def remote(src, dst, ssem, rsem, by):
        return pltpu.make_async_remote_copy(
            src_ref=src, dst_ref=dst, send_sem=ssem, recv_sem=rsem,
            device_id={"layer": p + by}, device_id_type=pl.DeviceIdType.MESH,
        )

    def inner(slot):
        return rounded.at[slot, pl.ds(WIDTH, cells)]

    def landing(slot):
        return jnp.where(slot == TO_RHS, RHS, slot - (TO_LEFT - LEFT))

    def message(slot, by):
        to = landing(slot)
        return remote(inner(slot), inner(to), send_sem.at[slot - TO_LEFT], recv_sem.at[to], by)

    def relay_of(slot):
        return remote(inner(slot), inner(slot), relay_sem.at[slot - LEFT], recv_sem.at[slot], -1)

    back = jnp.where(p > 0, -1, 1)

    def arrived(slot):
        remote(inner(slot), inner(slot), extra_sem.at[0], recv_sem.at[slot], back).wait_recv()

    def weight_to(by):
        return remote(w.at[0], w.at[COARSEN], extra_sem.at[0], recv_sem.at[WEIGHT], by)

    def special(slot, to, by):
        return remote(inner(slot), inner(to), send_sem.at[slot - TO_LEFT], recv_sem.at[to], by)

    def rounded_store(slot, value):
        rounded[slot, WIDTH:WIDTH + cells, :] = value.astype(bf16)

    def distance(code):
        return jnp.where(code == BY_TWO, 2, 1)

    half = chans // 2
    rounded[:, 0:WIDTH, :] = jnp.zeros((ROUNDED, WIDTH, chans), bf16)
    rounded[:, WIDTH + cells:, :] = jnp.zeros((ROUNDED, WIDTH, chans), bf16)
    part[:, :, 0:8, :] = jnp.zeros((2, 2, 8, half), f32)
    part[:, :, 8 + cells:, :] = jnp.zeros((2, 2, 8, half), f32)
    st[ZERO] = jnp.zeros((cells, chans), f32)

    def put(n):
        o_ref[n] = st[OUT].T

    own_load.wait()
    for load in weight_loads(2):
        load.start()
    loaded = xg[0].T
    st[LF] = loaded
    st[CP] = loaded
    rounded_store(CPB, loaded)

    @pl.when(first_owner)
    def _():
        start_load.wait()
        start = xg[1].T
        st[TMP] = start
        rounded_store(TMPB, start)

    def finish_owner(xy):
        cc = st[CC]
        second = st[RH] - (cc - st[PSI])
        solved = st[XZ] + ((cc - st[xy]) + second)

        @pl.when(lead_next)
        def _():
            rounded_store(TO_FINAL, solved)
            special(TO_FINAL, FINAL, 2).start()
            rounded_store(TO_SECOND, cc)
            special(TO_SECOND, SECOND, 2).start()

        st[CC] = solved

    rows_of = cells // BLOCKS
    col = lax.rem(lax.broadcasted_iota(jnp.int32, (rows_of, chans), 0), WIDTH)
    order = [
        [(1, 0), (0, 0), (2, 0), (0, 1), (1, 1)],
        [(1, 2), (0, 2), (2, 2), (2, 1), (1, 1)],
    ]

    def push(which, k, m):
        dy, dx = order[m][k]
        tap = 3 * dy + dx
        pltpu.matmul_push_rhs(
            w[which, :, tap * chans:(tap + 1) * chans], k % 2, m, transpose=True
        )

    def wait_weights(j):
        for load in weight_loads(j):
            load.wait()

    def fields_of(i):
        return tuple(entry(field, i) for field in FIELDS)

    def run(sides, middles, i, fields):
        f = dict(zip(FIELDS, fields))

        @pl.when(i == 1)
        def _():
            pl.semaphore_wait(barrier, greeted)

            @pl.when(shares)
            def _():
                weight_to(1).start()

            @pl.when(owner_shares)
            def _():
                weight_to(1 - COARSEN).start()

        received = f["recv"] != NONE

        @pl.when(received)
        def _():
            arrived(f["recv"])

            @pl.when(f["relay"] == 1)
            def _():
                relay_of(f["recv"]).start()

        source = f["rsrc"]

        def lhs(dy, r):
            return rounded[source, WIDTH * dy + r * rows_of:WIDTH * dy + (r + 1) * rows_of, :]

        def stream(k):
            for m in (0, 1):
                dy = order[m][k][0]
                total = sides[m] if k < 3 else middles[m]
                taken = range(BLOCKS) if k < 4 else range(m, BLOCKS, 2)
                for n, r in enumerate(taken):
                    pltpu.matmul_acc_lhs(total[r], lhs(dy, r), k % 2 if n == 0 else None)

        for m in (0, 1):
            push(f["w"], 1, m)
        stream(0)
        later = fields_of(i + 1)
        following = dict(zip(FIELDS, later))
        next_weight = jnp.logical_and(i + 1 < count, following["need"] > 0)

        @pl.when(received)
        def _():
            st[f["src"]] = rounded[source, WIDTH:WIDTH + cells, :].astype(f32)

        @pl.when(jnp.logical_or(i < COARSEN - 1, jnp.logical_or(next_weight, f["need"] > 0)))
        def _():
            @pl.when(i < COARSEN - 1)
            def _():
                wait_weights(i + 1)

            @pl.when(next_weight)
            def _():
                remote(w.at[0], w.at[COARSEN], extra_sem.at[0], recv_sem.at[WEIGHT], back).wait_recv()

            @pl.when(f["need"] == 1)
            def _():
                arrived(RHS)
                st[RHM] = rounded[RHS, WIDTH:WIDTH + cells, :].astype(f32)

        for k in range(1, 5):
            for m in (0, 1):
                if k < 4:
                    push(f["w"], k + 1, m)
            stream(k)
        for m in (0, 1):
            push(following["w"], 0, m)
        for r in range(BLOCKS):
            for m in (0, 1):
                t = pltpu.matmul_pop(sides[m][r])
                t = jnp.where(col == (0 if m else WIDTH - 1), 0.0, t)
                for h in (0, 1):
                    part[m, h, 8 + r * rows_of:8 + (r + 1) * rows_of, :] = t[:, h * half:(h + 1) * half]
        base[...] = st[f["src"]] + st[f["add"]]

        factor = jnp.where(f["factor"] == QUARTER, 0.25, jnp.where(f["factor"] == WHOLE, 1.0, 4.0))
        for r in range(BLOCKS):
            at = slice(r * rows_of, (r + 1) * rows_of)
            middle = pltpu.matmul_pop(middles[0][r]) + pltpu.matmul_pop(middles[1][r])
            side = jnp.concatenate([
                part[0, h, 7 + r * rows_of:7 + (r + 1) * rows_of, :]
                + part[1, h, 9 + r * rows_of:9 + (r + 1) * rows_of, :] for h in (0, 1)
            ], 1)
            new = base[at] + factor * jnp.tanh(middle + side)
            st[f["dst"], at] = new
            rounded[f["rdst"], WIDTH + r * rows_of:WIDTH + (r + 1) * rows_of, :] = new.astype(bf16)

        @pl.when(jnp.logical_and(f["rdst"] > UNSENT, has_next))
        def _():
            message(f["rdst"], distance(f["by"])).start()

        op = f["op"]

        @pl.when(op != NOTHING)
        def _():
            @pl.when(op == PSI_OF_LEFT)
            def _():
                psi = st[LF] + 4.0 * (st[CC] - base[...])
                st[PSI] = psi
                st[QQ] = (st[CP] - psi) - st[CP]

            @pl.when(op == KEEP)
            def _():
                st[TT] = 4.0 * (st[CP] - base[...])

            @pl.when(op == START)
            def _():
                psi = st[LF] + st[TT]
                rhs = st[CP] + ((st[CP] - psi) - st[CP])
                first = psi + rhs
                st[CC] = first
                rounded_store(TO_FIRST, first)
                special(TO_FIRST, FIRST, 1).start()

            @pl.when(op == FIRST_POINT)
            def _():
                rounded_store(TO_FIRST, st[PSI] + st[RH])
                special(TO_FIRST, FIRST, 1).start()

            @pl.when(op == OWNER_0)
            def _():
                t = st[CC] - base[...]
                st[TT] = t
                st[PSI] = st[LF] + t
                finish_owner(XZ)

            @pl.when(jnp.logical_or(op == PUT_0, jnp.logical_or(op == START, op == OWNER_0)))
            def _():
                t = jnp.where(op == PUT_0, st[f["dst"]] - base[...], st[TT])
                out = st[LF] + 0.25 * t
                st[OUT] = out
                rounded_store(OUTB, out)

            put_at = jnp.where(op == PUT_1, 1, jnp.where(op == PUT_2, 2, 0))

            @pl.when(jnp.logical_and(op >= START, op <= OWNER_0))
            def _():
                put(put_at)

            @pl.when(op == OWNER)
            def _():
                arrived(CHANGE)
                st[XZ] = rounded[CHANGE, WIDTH:WIDTH + cells, :].astype(f32)
                finish_owner(ZERO)

            @pl.when(op == CHANGES)
            def _():
                rounded_store(TO_CHANGE, st[XZ] - st[TMP])
                special(TO_CHANGE, CHANGE, COARSEN - 1).start()

        return later

    def loop(*totals):
        sides = (totals[:BLOCKS], totals[2 * BLOCKS:3 * BLOCKS])
        middles = (totals[BLOCKS:2 * BLOCKS], totals[3 * BLOCKS:])
        wait_weights(0)
        for load in weight_loads(3):
            load.start()
        for m in (0, 1):
            push(0, 0, m)
        lax.fori_loop(0, count, functools.partial(run, sides, middles), fields_of(0))
        for m in (0, 1):
            pltpu.matmul_acc_lhs(sides[m][0], rounded[CPB, 0:rows_of, :], 0)
            side_sum[0:rows_of, :] = pltpu.matmul_pop(sides[m][0])

    pl.run_scoped(
        loop, *[pltpu.ACC(m)((rows_of, chans), f32) for m in (0, 1) for _ in range(2 * BLOCKS)]
    )
    o_ref[COARSEN - 1] = st[CC].T

    def drain(copy, cond):
        @pl.when(cond)
        def _():
            copy.wait_send()

    relaxed = jnp.logical_or(
        jnp.logical_and(owner, lead_next), jnp.logical_and(phase == 1, group > 0)
    )
    drain(weight_to(back), jnp.logical_or(shares, owner_shares))
    drain(special(TO_LEFT, LEFT, back), has_next)
    drain(special(TO_RHS, RHS, back), shares)
    drain(special(TO_FIRST, FIRST, back), phase < 2)
    drain(special(TO_FINAL, FINAL, back), relaxed)
    drain(special(TO_SECOND, SECOND, back), relaxed)
    drain(special(TO_CHANGE, CHANGE, back), changes)
    drain(relay_of(FIRST), first_owner)
    drain(relay_of(FINAL), jnp.logical_and(lead, group > 0))
    drain(relay_of(SECOND), jnp.logical_and(phase == 1, group > 0))


def per_device(devices, inputs, guess, weights):
    chans, cells = inputs.shape
    return pl.pallas_call(
        functools.partial(kernel, devices),
        name="cycle",
        out_shape=pltpu.VMEM((COARSEN, chans, cells), jnp.float32),
        in_specs=[pl.BlockSpec(memory_space=pltpu.HBM)] * 3,
        out_specs=pl.BlockSpec(memory_space=pltpu.VMEM),
        scratch_shapes=[
            pltpu.VMEM((2, chans, cells), jnp.float32),
            pltpu.VMEM((COARSEN + 1,) + weights.shape[1:], jnp.bfloat16),
            pltpu.VMEM((STATES, cells, chans), jnp.float32),
            pltpu.VMEM((ROUNDED, cells + 2 * WIDTH, chans), jnp.bfloat16),
            pltpu.VMEM((2, 2, cells + 16, chans // 2), jnp.float32),
            pltpu.VMEM((cells, chans), jnp.float32),
            pltpu.VMEM((cells, chans), jnp.float32),
            pltpu.SemaphoreType.DMA((TO_RHS - TO_LEFT + 1,)),
            pltpu.SemaphoreType.DMA((FINAL - LEFT + 1,)),
            pltpu.SemaphoreType.DMA((1,)),
            pltpu.SemaphoreType.DMA((ROUNDED + 1,)),
            pltpu.SemaphoreType.DMA((2,)),
            pltpu.SemaphoreType.DMA((COARSEN, PIECES)),
        ],
        compiler_params=pltpu.CompilerParams(
            collective_id=0, has_side_effects=True, vmem_limit_bytes=56 * 2**20,
        ),
    )(*[pltpu.with_memory_space_constraint(a, pltpu.HBM) for a in (inputs, guess, weights)])


def solution(mesh):
    return jax.shard_map(
        functools.partial(per_device, mesh.shape["layer"]),
        mesh=mesh,
        in_specs=(P(None, "batch"), P("layer", None, "batch"), P("layer", None, None)),
        out_specs=P("layer", None, "batch"),
        check_vma=False,
    )
```

```python
import functools

import jax
import jax.numpy as jnp
from jax import lax
from jax.experimental import pallas as pl
from jax.experimental.pallas import tpu as pltpu
from jax.sharding import PartitionSpec as P

WIDTH = 16
COARSEN = 4
NONE = 15
PIECES = 2
BLOCKS = 8
ROWS = 128
ZERO, CP, LF, CC, RH, RHM, TT, PSI, QQ, XZ, OUT, TMP, DUMP = range(13)
STATES = 13
CPB, LFB, OUTB, CCB, TMPB, LEFT, FIRST, SECOND, FINAL, UNSENT = range(10)
TO_LEFT, TO_FIRST, TO_SECOND, TO_FINAL, TO_CHANGE, TO_RHS, CHANGE, RHS = range(10, 18)
ROUNDED = 18
WEIGHT = ROUNDED
NOTHING, PSI_OF_LEFT, FIRST_POINT, CHANGES, KEEP, START, PUT_0, OWNER_0, PUT_1, PUT_2, PUT_LAST, OWNER = range(12)
FIELDS = ("src", "dst", "w", "add", "factor", "rsrc", "rdst", "by", "recv", "relay", "need", "op")
BY_ONE, BY_TWO = 0, 1
QUARTER, WHOLE, FOUR = 0, 1, 2
ROUNDED_OF = {CP: CPB, LF: LFB, CC: CCB, OUT: OUTB, TMP: TMPB}


def step(src, dst, w, add=ZERO, factor=QUARTER, send=UNSENT, by=BY_ONE,
         recv=NONE, relay=0, need=0, op=NOTHING, rsrc=None):
    if rsrc is None:
        rsrc = ROUNDED_OF[src] if recv == NONE else recv
    rdst = ROUNDED_OF.get(dst, UNSENT) if send == UNSENT else send
    return dict(src=src, dst=dst, w=w, add=add, factor=factor, rsrc=rsrc, rdst=rdst,
                by=by, recv=recv, relay=relay, need=need, op=op)


def programs():
    def fine(send=UNSENT, first=NOTHING, op=NOTHING):
        return [step(CP, CP, 0, op=first), step(CP, CP, 1), step(CP, CP, 2),
                step(CP, CP, 3, send=send, op=op)]

    def again(send=UNSENT, op=NOTHING):
        return [step(LF, CC, 0, recv=LEFT, op=PSI_OF_LEFT), step(CC, CC, 1),
                step(CC, CC, 2), step(CC, RH, 3, add=QQ, send=send, op=op)]

    def whole(recv, dst, relay=0, need=0):
        return step(TMP, dst, COARSEN, add=RHM, factor=WHOLE, recv=recv, relay=relay, need=need)

    def own(src, dst, **kw):
        return step(src, dst, 0, add=RH, factor=WHOLE, **kw)

    last = [step(OUT, OUT, 1, op=PUT_1), step(OUT, OUT, 2, op=PUT_LAST)]
    early = [step(OUT, OUT, 1, op=PUT_1), step(OUT, OUT, 2, op=PUT_2)]
    body = fine(TO_LEFT) + again()
    mate = fine(TO_LEFT) + again(TO_RHS)
    final = [whole(FINAL, LF, relay=1)]
    owner_second = [whole(SECOND, TMP), step(TMP, PSI, 0, factor=WHOLE, op=OWNER)]
    relaxed = [whole(FIRST, TMP, need=1), own(TMP, CC)] + final + [
        step(LF, DUMP, 0, factor=WHOLE, op=PUT_0)]
    return {
        "start": fine(TO_LEFT, KEEP, START) + last,
        "lead_first": body + [own(LF, CC, recv=FIRST, send=TO_FIRST, by=BY_TWO, op=PUT_0)] + last,
        "mate_first": mate + [own(LF, CC, recv=FIRST, op=PUT_0)] + last,
        "owner_first": body + [
            step(TMP, XZ, 0, factor=FOUR), whole(FIRST, LF, relay=1, need=1),
            own(LF, CC, op=OWNER_0)] + last,
        "head": fine(TO_LEFT) + again(TO_RHS, FIRST_POINT) + [
            own(LF, CC, recv=FINAL, op=PUT_0)] + last + [
            step(LF, XZ, COARSEN, factor=FOUR, need=2, rsrc=FINAL),
            step(TMP, TMP, COARSEN, factor=FOUR, recv=SECOND, op=CHANGES)],
        "lead": body + [
            own(LF, TMP, recv=FIRST, send=TO_FIRST, by=BY_TWO),
            whole(FINAL, LF, relay=1, need=1),
            own(LF, CC, send=TO_FINAL, by=BY_TWO, op=PUT_0),
            whole(SECOND, TMP, relay=1),
            own(TMP, TMP, send=TO_SECOND, by=BY_TWO)] + last,
        "mate": mate + [own(LF, CC, recv=FINAL, op=PUT_0)] + last,
        "owner": body + relaxed + owner_second + last,
        "owner_last": body + relaxed + early + owner_second,
    }


def packed(values):
    words = []
    for start in (0, 8):
        word = sum(v << (4 * k) for k, v in enumerate(values[start:start + 8]))
        words.append(word - 2**32 if word >= 2**31 else word)
    return words


def kernel(
    devices, x_hbm, g_hbm, w_hbm, o_ref,
    xg, w, st, rounded, part, side_sum, base,
    send_sem, relay_sem, extra_sem, recv_sem, load_sem, weight_sem,
):
    f32, bf16 = jnp.float32, jnp.bfloat16
    p = lax.axis_index("layer")
    phase = lax.rem(p, COARSEN)
    owner = phase == COARSEN - 1
    group = lax.div(p, COARSEN)
    lead = lax.rem(p, 2) == 1
    mate = jnp.logical_not(lead)
    _, cells, chans = st.shape

    own_load = pltpu.make_async_copy(g_hbm.at[0], xg.at[0], load_sem.at[0])
    x_load = pltpu.make_async_copy(x_hbm, xg.at[0], load_sem.at[0])
    start_load = pltpu.make_async_copy(x_hbm, xg.at[1], load_sem.at[1])
    first_owner = jnp.logical_and(owner, group == 0)

    def weight_loads(j):
        rows = w.shape[1] // PIECES
        return [
            pltpu.make_async_copy(
                w_hbm.at[j, pl.ds(n * rows, rows)], w.at[j, pl.ds(n * rows, rows)],
                weight_sem.at[j, n],
            )
            for n in range(PIECES)
        ]

    @pl.when(p == 0)
    def _():
        x_load.start()

    @pl.when(p > 0)
    def _():
        own_load.start()

    for load in weight_loads(0) + weight_loads(1):
        load.start()

    @pl.when(first_owner)
    def _():
        start_load.start()

    barrier = pltpu.get_barrier_semaphore()

    def greet(by, cond):
        @pl.when(cond)
        def _():
            pl.semaphore_signal(
                barrier, inc=1, device_id={"layer": p + by},
                device_id_type=pl.DeviceIdType.MESH,
            )
        return cond.astype(jnp.int32)

    has_next = p < devices - 1
    lead_next = jnp.logical_and(lead, p + 2 < devices)
    last_owner = p + COARSEN >= devices
    greeted = (
        greet(1, has_next) + greet(-1, p > 0)
        + greet(COARSEN - 1, jnp.logical_and(phase == 0, group > 0))
        + greet(1 - COARSEN, jnp.logical_and(owner, group > 0))
        + greet(2, lead_next) + greet(-2, jnp.logical_and(lead, p >= 2))
    )
    shares = jnp.logical_and(mate, p > 0)
    owner_shares = jnp.logical_and(owner, group > 0)
    changes = jnp.logical_and(phase == 0, group > 0)

    roles = [
        ("start", p == 0),
        ("lead_first", jnp.logical_and(group == 0, phase == 1)),
        ("mate_first", jnp.logical_and(group == 0, phase == 2)),
        ("owner_first", first_owner),
        ("head", changes),
        ("lead", jnp.logical_and(group > 0, phase == 1)),
        ("mate", jnp.logical_and(group > 0, phase == 2)),
        ("owner_last", jnp.logical_and(owner, jnp.logical_and(group > 0, last_owner))),
    ]
    listed = programs()

    def chosen(value_of):
        value = jnp.int32(value_of(listed["owner"]))
        for name, cond in roles:
            value = jnp.where(cond, jnp.int32(value_of(listed[name])), value)
        return value

    count = chosen(len)
    words = {
        field: [
            chosen(lambda steps: packed([s[field] for s in steps])[half]) for half in (0, 1)
        ]
        for field in FIELDS
    }

    def entry(field, i):
        low, high = words[field]
        word = jnp.where(i < 8, low, high)
        return jnp.bitwise_and(
            lax.shift_right_logical(word, 4 * jnp.bitwise_and(i, 7)), 15
        )

    def remote(src, dst, ssem, rsem, by):
        return pltpu.make_async_remote_copy(
            src_ref=src, dst_ref=dst, send_sem=ssem, recv_sem=rsem,
            device_id={"layer": p + by}, device_id_type=pl.DeviceIdType.MESH,
        )

    def inner(slot):
        return rounded.at[slot, pl.ds(WIDTH, cells)]

    def landing(slot):
        return jnp.where(slot == TO_RHS, RHS, slot - (TO_LEFT - LEFT))

    def message(slot, by):
        to = landing(slot)
        return remote(inner(slot), inner(to), send_sem.at[slot - TO_LEFT], recv_sem.at[to], by)

    def relay_of(slot):
        return remote(inner(slot), inner(slot), relay_sem.at[slot - LEFT], recv_sem.at[slot], -1)

    back = jnp.where(p > 0, -1, 1)

    def arrived(slot):
        remote(inner(slot), inner(slot), extra_sem.at[0], recv_sem.at[slot], back).wait_recv()

    def weight_to(by):
        return remote(w.at[0], w.at[COARSEN], extra_sem.at[0], recv_sem.at[WEIGHT], by)

    def special(slot, to, by):
        return remote(inner(slot), inner(to), send_sem.at[slot - TO_LEFT], recv_sem.at[to], by)

    def rounded_store(slot, value):
        rounded[slot, WIDTH:WIDTH + cells, :] = value.astype(bf16)

    def distance(code):
        return jnp.where(code == BY_TWO, 2, 1)

    half = chans // 2
    rounded[:, 0:WIDTH, :] = jnp.zeros((ROUNDED, WIDTH, chans), bf16)
    rounded[:, WIDTH + cells:, :] = jnp.zeros((ROUNDED, WIDTH, chans), bf16)
    part[:, :, 0:8, :] = jnp.zeros((2, 2, 8, half), f32)
    part[:, :, 8 + cells:, :] = jnp.zeros((2, 2, 8, half), f32)
    st[ZERO] = jnp.zeros((cells, chans), f32)

    def put(slot, n):
        o_ref[n] = st[slot].T

    def by_rows(body):
        def rows(r, _):
            first = pl.multiple_of(r * ROWS, ROWS)
            body(pl.ds(first, ROWS), pl.ds(WIDTH + first, ROWS))
            return 0

        lax.fori_loop(0, cells // ROWS, rows, 0)

    own_load.wait()
    for load in weight_loads(2):
        load.start()
    loaded = xg[0].T
    st[LF] = loaded
    st[CP] = loaded
    rounded_store(CPB, loaded)

    @pl.when(first_owner)
    def _():
        start_load.wait()
        start = xg[1].T
        st[TMP] = start
        rounded_store(TMPB, start)

    def send_solved():
        @pl.when(lead_next)
        def _():
            special(TO_FINAL, FINAL, 2).start()
            special(TO_SECOND, SECOND, 2).start()

    def solve(at, inner_at, psi, xz, xy):
        cc = st[CC, at]
        second = st[RH, at] - (cc - psi)
        solved = xz + ((cc - xy) + second)
        rounded[TO_FINAL, inner_at] = solved.astype(bf16)
        rounded[TO_SECOND, inner_at] = cc.astype(bf16)
        st[CC, at] = solved

    rows_of = cells // BLOCKS
    col = lax.rem(lax.broadcasted_iota(jnp.int32, (rows_of, chans), 0), WIDTH)
    order = [
        [(1, 0), (0, 0), (2, 0), (0, 1), (1, 1)],
        [(1, 2), (0, 2), (2, 2), (2, 1), (1, 1)],
    ]

    def push(which, k, m):
        dy, dx = order[m][k]
        tap = 3 * dy + dx
        pltpu.matmul_push_rhs(
            w[which, :, tap * chans:(tap + 1) * chans], k % 2, m, transpose=True
        )

    def wait_weights(j):
        for load in weight_loads(j):
            load.wait()

    def fields_of(i):
        return tuple(entry(field, i) for field in FIELDS)

    def run(sides, middles, i, fields):
        f = dict(zip(FIELDS, fields))

        @pl.when(i == 1)
        def _():
            pl.semaphore_wait(barrier, greeted)

            @pl.when(shares)
            def _():
                weight_to(1).start()

            @pl.when(owner_shares)
            def _():
                weight_to(1 - COARSEN).start()

        received = f["recv"] != NONE

        @pl.when(received)
        def _():
            arrived(f["recv"])

            @pl.when(f["relay"] == 1)
            def _():
                relay_of(f["recv"]).start()

        source = f["rsrc"]

        def lhs(dy, r):
            return rounded[source, WIDTH * dy + r * rows_of:WIDTH * dy + (r + 1) * rows_of, :]

        def stream(k):
            for m in (0, 1):
                dy = order[m][k][0]
                total = sides[m] if k < 3 else middles[m]
                taken = range(BLOCKS) if k < 4 else range(m, BLOCKS, 2)
                for n, r in enumerate(taken):
                    pltpu.matmul_acc_lhs(total[r], lhs(dy, r), k % 2 if n == 0 else None)

        for m in (0, 1):
            push(f["w"], 1, m)
        stream(0)
        later = fields_of(i + 1)
        following = dict(zip(FIELDS, later))
        next_weight = jnp.logical_and(i + 1 < count, following["need"] > 0)

        @pl.when(received)
        def _():
            st[f["src"]] = rounded[source, WIDTH:WIDTH + cells, :].astype(f32)

        @pl.when(jnp.logical_or(i < COARSEN - 1, jnp.logical_or(next_weight, f["need"] > 0)))
        def _():
            @pl.when(i < COARSEN - 1)
            def _():
                wait_weights(i + 1)

            @pl.when(next_weight)
            def _():
                remote(w.at[0], w.at[COARSEN], extra_sem.at[0], recv_sem.at[WEIGHT], back).wait_recv()

            @pl.when(f["need"] == 1)
            def _():
                arrived(RHS)
                st[RHM] = rounded[RHS, WIDTH:WIDTH + cells, :].astype(f32)

        for k in range(1, 5):
            for m in (0, 1):
                if k < 4:
                    push(f["w"], k + 1, m)
            stream(k)
        for m in (0, 1):
            push(following["w"], 0, m)
        for r in range(BLOCKS):
            for m in (0, 1):
                t = pltpu.matmul_pop(sides[m][r])
                t = jnp.where(col == (0 if m else WIDTH - 1), 0.0, t)
                for h in (0, 1):
                    part[m, h, 8 + r * rows_of:8 + (r + 1) * rows_of, :] = t[:, h * half:(h + 1) * half]
        base[...] = st[f["src"]] + st[f["add"]]

        factor = jnp.where(f["factor"] == QUARTER, 0.25, jnp.where(f["factor"] == WHOLE, 1.0, 4.0))
        for r in range(BLOCKS):
            at = slice(r * rows_of, (r + 1) * rows_of)
            middle = pltpu.matmul_pop(middles[0][r]) + pltpu.matmul_pop(middles[1][r])
            side = jnp.concatenate([
                part[0, h, 7 + r * rows_of:7 + (r + 1) * rows_of, :]
                + part[1, h, 9 + r * rows_of:9 + (r + 1) * rows_of, :] for h in (0, 1)
            ], 1)
            new = base[at] + factor * jnp.tanh(middle + side)
            st[f["dst"], at] = new
            rounded[f["rdst"], WIDTH + r * rows_of:WIDTH + (r + 1) * rows_of, :] = new.astype(bf16)

        @pl.when(jnp.logical_and(f["rdst"] > UNSENT, has_next))
        def _():
            message(f["rdst"], distance(f["by"])).start()

        op = f["op"]

        @pl.when(op != NOTHING)
        def _():
            @pl.when(op == PSI_OF_LEFT)
            def _():
                def rows(at, _):
                    psi = st[LF, at] + 4.0 * (st[CC, at] - base[at])
                    st[PSI, at] = psi
                    st[QQ, at] = (st[CP, at] - psi) - st[CP, at]

                by_rows(rows)

            @pl.when(op == KEEP)
            def _():
                def rows(at, _):
                    st[TT, at] = 4.0 * (st[CP, at] - base[at])

                by_rows(rows)

            @pl.when(op == START)
            def _():
                def rows(at, inner_at):
                    psi = st[LF, at] + st[TT, at]
                    rhs = st[CP, at] + ((st[CP, at] - psi) - st[CP, at])
                    first = psi + rhs
                    st[CC, at] = first
                    rounded[TO_FIRST, inner_at] = first.astype(bf16)

                by_rows(rows)
                special(TO_FIRST, FIRST, 1).start()

            @pl.when(op == FIRST_POINT)
            def _():
                def rows(at, inner_at):
                    rounded[TO_FIRST, inner_at] = (st[PSI, at] + st[RH, at]).astype(bf16)

                by_rows(rows)
                special(TO_FIRST, FIRST, 1).start()

            @pl.when(op == OWNER_0)
            def _():
                def rows(at, inner_at):
                    t = st[CC, at] - base[at]
                    st[TT, at] = t
                    solve(at, inner_at, st[LF, at] + t, st[XZ, at], st[XZ, at])

                by_rows(rows)
                send_solved()

            @pl.when(jnp.logical_and(op >= START, op <= OWNER_0))
            def _():
                def rows(at, inner_at):
                    t = jnp.where(op == PUT_0, st[f["dst"], at] - base[at], st[TT, at])
                    out = st[LF, at] + 0.25 * t
                    st[OUT, at] = out
                    rounded[OUTB, inner_at] = out.astype(bf16)

                by_rows(rows)

            @pl.when(op == OWNER)
            def _():
                arrived(CHANGE)

                def rows(at, inner_at):
                    change = rounded[CHANGE, inner_at].astype(f32)
                    solve(at, inner_at, st[PSI, at], change, st[ZERO, at])

                by_rows(rows)
                send_solved()

            @pl.when(op >= START)
            def _():
                whole_put = op == OWNER

                def one(n, _):
                    put_last = jnp.logical_or(whole_put, n == 1)
                    place = jnp.where(op >= PUT_1, op - PUT_1 + 1, 0)
                    put(
                        jnp.where(put_last, CC, OUT),
                        jnp.where(put_last, COARSEN - 1, jnp.minimum(place, COARSEN - 2)),
                    )
                    return 0

                lax.fori_loop(0, jnp.where(op == PUT_LAST, 2, 1), one, 0)

            @pl.when(op == CHANGES)
            def _():
                def rows(at, inner_at):
                    rounded[TO_CHANGE, inner_at] = (st[XZ, at] - st[TMP, at]).astype(bf16)

                by_rows(rows)
                special(TO_CHANGE, CHANGE, COARSEN - 1).start()

        return later

    def loop(*totals):
        sides = (totals[:BLOCKS], totals[2 * BLOCKS:3 * BLOCKS])
        middles = (totals[BLOCKS:2 * BLOCKS], totals[3 * BLOCKS:])
        wait_weights(0)
        for load in weight_loads(3):
            load.start()
        for m in (0, 1):
            push(0, 0, m)
        lax.fori_loop(0, count, functools.partial(run, sides, middles), fields_of(0))
        for m in (0, 1):
            pltpu.matmul_acc_lhs(sides[m][0], rounded[CPB, 0:rows_of, :], 0)
            side_sum[0:rows_of, :] = pltpu.matmul_pop(sides[m][0])

    pl.run_scoped(
        loop, *[pltpu.ACC(m)((rows_of, chans), f32) for m in (0, 1) for _ in range(2 * BLOCKS)]
    )

    def drain(copy, cond):
        @pl.when(cond)
        def _():
            copy.wait_send()

    relaxed = jnp.logical_or(
        jnp.logical_and(owner, lead_next), jnp.logical_and(phase == 1, group > 0)
    )
    drain(weight_to(back), jnp.logical_or(shares, owner_shares))
    drain(special(TO_LEFT, LEFT, back), has_next)
    drain(special(TO_RHS, RHS, back), shares)
    drain(special(TO_FIRST, FIRST, back), phase < 2)
    drain(special(TO_FINAL, FINAL, back), relaxed)
    drain(special(TO_SECOND, SECOND, back), relaxed)
    drain(special(TO_CHANGE, CHANGE, back), changes)
    drain(relay_of(FIRST), first_owner)
    drain(relay_of(FINAL), jnp.logical_and(lead, group > 0))
    drain(relay_of(SECOND), jnp.logical_and(phase == 1, group > 0))


def per_device(devices, inputs, guess, weights):
    chans, cells = inputs.shape
    return pl.pallas_call(
        functools.partial(kernel, devices),
        name="cycle",
        out_shape=pltpu.VMEM((COARSEN, chans, cells), jnp.float32),
        in_specs=[pl.BlockSpec(memory_space=pltpu.HBM)] * 3,
        out_specs=pl.BlockSpec(memory_space=pltpu.VMEM),
        scratch_shapes=[
            pltpu.VMEM((2, chans, cells), jnp.float32),
            pltpu.VMEM((COARSEN + 1,) + weights.shape[1:], jnp.bfloat16),
            pltpu.VMEM((STATES, cells, chans), jnp.float32),
            pltpu.VMEM((ROUNDED, cells + 2 * WIDTH, chans), jnp.bfloat16),
            pltpu.VMEM((2, 2, cells + 16, chans // 2), jnp.float32),
            pltpu.VMEM((cells, chans), jnp.float32),
            pltpu.VMEM((cells, chans), jnp.float32),
            pltpu.SemaphoreType.DMA((TO_RHS - TO_LEFT + 1,)),
            pltpu.SemaphoreType.DMA((FINAL - LEFT + 1,)),
            pltpu.SemaphoreType.DMA((1,)),
            pltpu.SemaphoreType.DMA((ROUNDED + 1,)),
            pltpu.SemaphoreType.DMA((2,)),
            pltpu.SemaphoreType.DMA((COARSEN, PIECES)),
        ],
        compiler_params=pltpu.CompilerParams(
            collective_id=0, has_side_effects=True, vmem_limit_bytes=56 * 2**20,
        ),
    )(*[pltpu.with_memory_space_constraint(a, pltpu.HBM) for a in (inputs, guess, weights)])


def solution(mesh):
    return jax.shard_map(
        functools.partial(per_device, mesh.shape["layer"]),
        mesh=mesh,
        in_specs=(P(None, "batch"), P("layer", None, "batch"), P("layer", None, None)),
        out_specs=P("layer", None, "batch"),
        check_vma=False,
    )
```

```python
import functools

import jax
import jax.numpy as jnp
from jax import lax
from jax.experimental import pallas as pl
from jax.experimental.pallas import tpu as pltpu
from jax.sharding import PartitionSpec as P

WIDTH = 16
COARSEN = 4
NONE = 15
PIECES = 2
BLOCKS = 8
ROWS = 128
ZERO, CP, LF, CC, RH, RHM, TT, PSI, QQ, XZ, OUT, TMP, DUMP = range(13)
STATES = 13
CPB, LFB, OUTB, CCB, TMPB, LEFT, FIRST, SECOND, FINAL, UNSENT = range(10)
TO_LEFT, TO_FIRST, TO_SECOND, TO_FINAL, TO_CHANGE, TO_RHS, CHANGE, RHS = range(10, 18)
ROUNDED = 18
WEIGHT = ROUNDED
NOTHING, PSI_OF_LEFT, FIRST_POINT, CHANGES, KEEP, START, PUT_0, OWNER_0, PUT_1, PUT_2, OWNER = range(11)
FIELDS = ("src", "dst", "w", "add", "factor", "rsrc", "rdst", "by", "recv", "relay", "need", "op")
BY_ONE, BY_TWO = 0, 1
QUARTER, WHOLE, FOUR = 0, 1, 2
ROUNDED_OF = {CP: CPB, LF: LFB, CC: CCB, OUT: OUTB, TMP: TMPB}


def step(src, dst, w, add=ZERO, factor=QUARTER, send=UNSENT, by=BY_ONE,
         recv=NONE, relay=0, need=0, op=NOTHING, rsrc=None):
    if rsrc is None:
        rsrc = ROUNDED_OF[src] if recv == NONE else recv
    rdst = ROUNDED_OF.get(dst, UNSENT) if send == UNSENT else send
    return dict(src=src, dst=dst, w=w, add=add, factor=factor, rsrc=rsrc, rdst=rdst,
                by=by, recv=recv, relay=relay, need=need, op=op)


def programs():
    def fine(send=UNSENT, first=NOTHING, op=NOTHING):
        return [step(CP, CP, 0, op=first), step(CP, CP, 1), step(CP, CP, 2),
                step(CP, CP, 3, send=send, op=op)]

    def again(send=UNSENT, op=NOTHING):
        return [step(LF, CC, 0, recv=LEFT, op=PSI_OF_LEFT), step(CC, CC, 1),
                step(CC, CC, 2), step(CC, RH, 3, add=QQ, send=send, op=op)]

    def whole(recv, dst, relay=0, need=0):
        return step(TMP, dst, COARSEN, add=RHM, factor=WHOLE, recv=recv, relay=relay, need=need)

    def own(src, dst, **kw):
        return step(src, dst, 0, add=RH, factor=WHOLE, **kw)

    last = [step(OUT, OUT, 1, op=PUT_1), step(OUT, OUT, 2, op=PUT_2)]
    body = fine(TO_LEFT) + again()
    mate = fine(TO_LEFT) + again(TO_RHS)
    final = [whole(FINAL, LF, relay=1)]
    owner_second = [whole(SECOND, TMP), step(TMP, PSI, 0, factor=WHOLE, op=OWNER)]
    relaxed = [whole(FIRST, TMP, need=1), own(TMP, CC)] + final + [
        step(LF, DUMP, 0, factor=WHOLE, op=PUT_0)]
    return {
        "start": fine(TO_LEFT, KEEP, START) + last,
        "lead_first": body + [own(LF, CC, recv=FIRST, send=TO_FIRST, by=BY_TWO, op=PUT_0)] + last,
        "mate_first": mate + [own(LF, CC, recv=FIRST, op=PUT_0)] + last,
        "owner_first": body + [
            step(TMP, XZ, 0, factor=FOUR), whole(FIRST, LF, relay=1, need=1),
            own(LF, CC, op=OWNER_0)] + last,
        "head": fine(TO_LEFT) + again(TO_RHS, FIRST_POINT) + [
            own(LF, CC, recv=FINAL, op=PUT_0)] + last + [
            step(LF, XZ, COARSEN, factor=FOUR, need=2, rsrc=FINAL),
            step(TMP, TMP, COARSEN, factor=FOUR, recv=SECOND, op=CHANGES)],
        "lead": body + [
            own(LF, TMP, recv=FIRST, send=TO_FIRST, by=BY_TWO),
            whole(FINAL, LF, relay=1, need=1),
            own(LF, CC, send=TO_FINAL, by=BY_TWO, op=PUT_0),
            whole(SECOND, TMP, relay=1),
            own(TMP, TMP, send=TO_SECOND, by=BY_TWO)] + last,
        "mate": mate + [own(LF, CC, recv=FINAL, op=PUT_0)] + last,
        "owner": body + relaxed + owner_second + last,
        "owner_last": body + relaxed + last + owner_second,
    }


def packed(values):
    words = []
    for start in (0, 8):
        word = sum(v << (4 * k) for k, v in enumerate(values[start:start + 8]))
        words.append(word - 2**32 if word >= 2**31 else word)
    return words


def kernel(
    devices, x_hbm, g_hbm, w_hbm, o_ref,
    xg, w, st, rounded, part, side_sum, base,
    send_sem, relay_sem, extra_sem, recv_sem, load_sem, weight_sem,
):
    f32, bf16 = jnp.float32, jnp.bfloat16
    p = lax.axis_index("layer")
    phase = lax.rem(p, COARSEN)
    owner = phase == COARSEN - 1
    group = lax.div(p, COARSEN)
    lead = lax.rem(p, 2) == 1
    mate = jnp.logical_not(lead)
    _, cells, chans = st.shape

    own_load = pltpu.make_async_copy(g_hbm.at[0], xg.at[0], load_sem.at[0])
    x_load = pltpu.make_async_copy(x_hbm, xg.at[0], load_sem.at[0])
    start_load = pltpu.make_async_copy(x_hbm, xg.at[1], load_sem.at[1])
    first_owner = jnp.logical_and(owner, group == 0)

    def weight_loads(j):
        rows = w.shape[1] // PIECES
        return [
            pltpu.make_async_copy(
                w_hbm.at[j, pl.ds(n * rows, rows)], w.at[j, pl.ds(n * rows, rows)],
                weight_sem.at[j, n],
            )
            for n in range(PIECES)
        ]

    @pl.when(p == 0)
    def _():
        x_load.start()

    @pl.when(p > 0)
    def _():
        own_load.start()

    for load in weight_loads(0) + weight_loads(1):
        load.start()

    @pl.when(first_owner)
    def _():
        start_load.start()

    barrier = pltpu.get_barrier_semaphore()

    def greet(by, cond):
        @pl.when(cond)
        def _():
            pl.semaphore_signal(
                barrier, inc=1, device_id={"layer": p + by},
                device_id_type=pl.DeviceIdType.MESH,
            )
        return cond.astype(jnp.int32)

    has_next = p < devices - 1
    lead_next = jnp.logical_and(lead, p + 2 < devices)
    last_owner = p + COARSEN >= devices
    greeted = (
        greet(1, has_next) + greet(-1, p > 0)
        + greet(COARSEN - 1, jnp.logical_and(phase == 0, group > 0))
        + greet(1 - COARSEN, jnp.logical_and(owner, group > 0))
        + greet(2, lead_next) + greet(-2, jnp.logical_and(lead, p >= 2))
    )
    shares = jnp.logical_and(mate, p > 0)
    owner_shares = jnp.logical_and(owner, group > 0)
    changes = jnp.logical_and(phase == 0, group > 0)

    roles = [
        ("start", p == 0),
        ("lead_first", jnp.logical_and(group == 0, phase == 1)),
        ("mate_first", jnp.logical_and(group == 0, phase == 2)),
        ("owner_first", first_owner),
        ("head", changes),
        ("lead", jnp.logical_and(group > 0, phase == 1)),
        ("mate", jnp.logical_and(group > 0, phase == 2)),
        ("owner_last", jnp.logical_and(owner, jnp.logical_and(group > 0, last_owner))),
    ]
    listed = programs()

    def chosen(value_of):
        value = jnp.int32(value_of(listed["owner"]))
        for name, cond in roles:
            value = jnp.where(cond, jnp.int32(value_of(listed[name])), value)
        return value

    count = chosen(len)
    words = {
        field: [
            chosen(lambda steps: packed([s[field] for s in steps])[half]) for half in (0, 1)
        ]
        for field in FIELDS
    }

    def entry(field, i):
        low, high = words[field]
        word = jnp.where(i < 8, low, high)
        return jnp.bitwise_and(
            lax.shift_right_logical(word, 4 * jnp.bitwise_and(i, 7)), 15
        )

    def remote(src, dst, ssem, rsem, by):
        return pltpu.make_async_remote_copy(
            src_ref=src, dst_ref=dst, send_sem=ssem, recv_sem=rsem,
            device_id={"layer": p + by}, device_id_type=pl.DeviceIdType.MESH,
        )

    def inner(slot):
        return rounded.at[slot, pl.ds(WIDTH, cells)]

    def landing(slot):
        return jnp.where(slot == TO_RHS, RHS, slot - (TO_LEFT - LEFT))

    def message(slot, by):
        to = landing(slot)
        return remote(inner(slot), inner(to), send_sem.at[slot - TO_LEFT], recv_sem.at[to], by)

    def relay_of(slot):
        return remote(inner(slot), inner(slot), relay_sem.at[slot - LEFT], recv_sem.at[slot], -1)

    back = jnp.where(p > 0, -1, 1)

    def arrived(slot):
        remote(inner(slot), inner(slot), extra_sem.at[0], recv_sem.at[slot], back).wait_recv()

    def weight_to(by):
        return remote(w.at[0], w.at[COARSEN], extra_sem.at[0], recv_sem.at[WEIGHT], by)

    def special(slot, to, by):
        return remote(inner(slot), inner(to), send_sem.at[slot - TO_LEFT], recv_sem.at[to], by)

    def rounded_store(slot, value):
        rounded[slot, WIDTH:WIDTH + cells, :] = value.astype(bf16)

    def distance(code):
        return jnp.where(code == BY_TWO, 2, 1)

    half = chans // 2
    rounded[:, 0:WIDTH, :] = jnp.zeros((ROUNDED, WIDTH, chans), bf16)
    rounded[:, WIDTH + cells:, :] = jnp.zeros((ROUNDED, WIDTH, chans), bf16)
    part[:, :, 0:8, :] = jnp.zeros((2, 2, 8, half), f32)
    part[:, :, 8 + cells:, :] = jnp.zeros((2, 2, 8, half), f32)
    st[ZERO] = jnp.zeros((cells, chans), f32)

    def by_rows(body):
        def rows(r, _):
            first = pl.multiple_of(r * ROWS, ROWS)
            body(pl.ds(first, ROWS), pl.ds(WIDTH + first, ROWS))
            return 0

        lax.fori_loop(0, cells // ROWS, rows, 0)

    own_load.wait()
    for load in weight_loads(2):
        load.start()
    loaded = xg[0].T
    st[LF] = loaded
    st[CP] = loaded
    rounded_store(CPB, loaded)

    @pl.when(first_owner)
    def _():
        start_load.wait()
        start = xg[1].T
        st[TMP] = start
        rounded_store(TMPB, start)

    def send_solved():
        @pl.when(lead_next)
        def _():
            special(TO_FINAL, FINAL, 2).start()
            special(TO_SECOND, SECOND, 2).start()

    def solve(at, inner_at, psi, xz, xy):
        cc = st[CC, at]
        second = st[RH, at] - (cc - psi)
        solved = xz + ((cc - xy) + second)
        rounded[TO_FINAL, inner_at] = solved.astype(bf16)
        rounded[TO_SECOND, inner_at] = cc.astype(bf16)
        st[CC, at] = solved
        o_ref[COARSEN - 1, at] = solved

    rows_of = cells // BLOCKS
    col = lax.rem(lax.broadcasted_iota(jnp.int32, (rows_of, chans), 0), WIDTH)
    order = [
        [(1, 0), (0, 0), (2, 0), (0, 1), (1, 1)],
        [(1, 2), (0, 2), (2, 2), (2, 1), (1, 1)],
    ]

    def push(which, k, m):
        dy, dx = order[m][k]
        tap = 3 * dy + dx
        pltpu.matmul_push_rhs(
            w[which, :, tap * chans:(tap + 1) * chans], k % 2, m, transpose=True
        )

    def wait_weights(j):
        for load in weight_loads(j):
            load.wait()

    def fields_of(i):
        return tuple(entry(field, i) for field in FIELDS)

    def run(sides, middles, i, fields):
        f = dict(zip(FIELDS, fields))

        @pl.when(i == 1)
        def _():
            pl.semaphore_wait(barrier, greeted)

            @pl.when(shares)
            def _():
                weight_to(1).start()

            @pl.when(owner_shares)
            def _():
                weight_to(1 - COARSEN).start()

        received = f["recv"] != NONE

        @pl.when(received)
        def _():
            arrived(f["recv"])

            @pl.when(f["relay"] == 1)
            def _():
                relay_of(f["recv"]).start()

        source = f["rsrc"]

        def lhs(dy, r):
            return rounded[source, WIDTH * dy + r * rows_of:WIDTH * dy + (r + 1) * rows_of, :]

        def stream(k):
            for m in (0, 1):
                dy = order[m][k][0]
                total = sides[m] if k < 3 else middles[m]
                taken = range(BLOCKS) if k < 4 else range(m, BLOCKS, 2)
                for n, r in enumerate(taken):
                    pltpu.matmul_acc_lhs(total[r], lhs(dy, r), k % 2 if n == 0 else None)

        for m in (0, 1):
            push(f["w"], 1, m)
        stream(0)
        later = fields_of(i + 1)
        following = dict(zip(FIELDS, later))
        next_weight = jnp.logical_and(i + 1 < count, following["need"] > 0)

        @pl.when(received)
        def _():
            st[f["src"]] = rounded[source, WIDTH:WIDTH + cells, :].astype(f32)

        @pl.when(jnp.logical_or(i < COARSEN - 1, jnp.logical_or(next_weight, f["need"] > 0)))
        def _():
            @pl.when(i < COARSEN - 1)
            def _():
                wait_weights(i + 1)

            @pl.when(next_weight)
            def _():
                remote(w.at[0], w.at[COARSEN], extra_sem.at[0], recv_sem.at[WEIGHT], back).wait_recv()

            @pl.when(f["need"] == 1)
            def _():
                arrived(RHS)
                st[RHM] = rounded[RHS, WIDTH:WIDTH + cells, :].astype(f32)

        for k in range(1, 5):
            for m in (0, 1):
                if k < 4:
                    push(f["w"], k + 1, m)
            stream(k)
        for m in (0, 1):
            push(following["w"], 0, m)
        for r in range(BLOCKS):
            for m in (0, 1):
                t = pltpu.matmul_pop(sides[m][r])
                t = jnp.where(col == (0 if m else WIDTH - 1), 0.0, t)
                for h in (0, 1):
                    part[m, h, 8 + r * rows_of:8 + (r + 1) * rows_of, :] = t[:, h * half:(h + 1) * half]
        base[...] = st[f["src"]] + st[f["add"]]

        factor = jnp.where(f["factor"] == QUARTER, 0.25, jnp.where(f["factor"] == WHOLE, 1.0, 4.0))
        for r in range(BLOCKS):
            at = slice(r * rows_of, (r + 1) * rows_of)
            middle = pltpu.matmul_pop(middles[0][r]) + pltpu.matmul_pop(middles[1][r])
            side = jnp.concatenate([
                part[0, h, 7 + r * rows_of:7 + (r + 1) * rows_of, :]
                + part[1, h, 9 + r * rows_of:9 + (r + 1) * rows_of, :] for h in (0, 1)
            ], 1)
            new = base[at] + factor * jnp.tanh(middle + side)
            st[f["dst"], at] = new
            rounded[f["rdst"], WIDTH + r * rows_of:WIDTH + (r + 1) * rows_of, :] = new.astype(bf16)

        @pl.when(jnp.logical_and(f["rdst"] > UNSENT, has_next))
        def _():
            message(f["rdst"], distance(f["by"])).start()

        op = f["op"]

        @pl.when(op != NOTHING)
        def _():
            @pl.when(op == PSI_OF_LEFT)
            def _():
                def rows(at, _):
                    psi = st[LF, at] + 4.0 * (st[CC, at] - base[at])
                    st[PSI, at] = psi
                    st[QQ, at] = (st[CP, at] - psi) - st[CP, at]

                by_rows(rows)

            @pl.when(op == KEEP)
            def _():
                def rows(at, _):
                    st[TT, at] = 4.0 * (st[CP, at] - base[at])

                by_rows(rows)

            @pl.when(op == START)
            def _():
                def rows(at, inner_at):
                    psi = st[LF, at] + st[TT, at]
                    rhs = st[CP, at] + ((st[CP, at] - psi) - st[CP, at])
                    first = psi + rhs
                    st[CC, at] = first
                    rounded[TO_FIRST, inner_at] = first.astype(bf16)

                by_rows(rows)
                special(TO_FIRST, FIRST, 1).start()

            @pl.when(op == FIRST_POINT)
            def _():
                def rows(at, inner_at):
                    rounded[TO_FIRST, inner_at] = (st[PSI, at] + st[RH, at]).astype(bf16)

                by_rows(rows)
                special(TO_FIRST, FIRST, 1).start()

            @pl.when(op == OWNER_0)
            def _():
                def rows(at, inner_at):
                    t = st[CC, at] - base[at]
                    st[TT, at] = t
                    solve(at, inner_at, st[LF, at] + t, st[XZ, at], st[XZ, at])

                by_rows(rows)
                send_solved()

            @pl.when(jnp.logical_and(op >= START, op <= OWNER_0))
            def _():
                def rows(at, inner_at):
                    t = jnp.where(op == PUT_0, st[f["dst"], at] - base[at], st[TT, at])
                    out = st[LF, at] + 0.25 * t
                    st[OUT, at] = out
                    o_ref[0, at] = out
                    o_ref[COARSEN - 1, at] = st[CC, at]
                    rounded[OUTB, inner_at] = out.astype(bf16)

                by_rows(rows)

            @pl.when(op == OWNER)
            def _():
                arrived(CHANGE)

                def rows(at, inner_at):
                    change = rounded[CHANGE, inner_at].astype(f32)
                    solve(at, inner_at, st[PSI, at], change, st[ZERO, at])

                by_rows(rows)
                send_solved()

            @pl.when(jnp.logical_or(op == PUT_1, op == PUT_2))
            def _():
                o_ref[op - PUT_1 + 1] = st[OUT]

            @pl.when(op == CHANGES)
            def _():
                def rows(at, inner_at):
                    rounded[TO_CHANGE, inner_at] = (st[XZ, at] - st[TMP, at]).astype(bf16)

                by_rows(rows)
                special(TO_CHANGE, CHANGE, COARSEN - 1).start()

        return later

    def loop(*totals):
        sides = (totals[:BLOCKS], totals[2 * BLOCKS:3 * BLOCKS])
        middles = (totals[BLOCKS:2 * BLOCKS], totals[3 * BLOCKS:])
        wait_weights(0)
        for load in weight_loads(3):
            load.start()
        for m in (0, 1):
            push(0, 0, m)
        lax.fori_loop(0, count, functools.partial(run, sides, middles), fields_of(0))
        for m in (0, 1):
            pltpu.matmul_acc_lhs(sides[m][0], rounded[CPB, 0:rows_of, :], 0)
            side_sum[0:rows_of, :] = pltpu.matmul_pop(sides[m][0])

    pl.run_scoped(
        loop, *[pltpu.ACC(m)((rows_of, chans), f32) for m in (0, 1) for _ in range(2 * BLOCKS)]
    )

    def drain(copy, cond):
        @pl.when(cond)
        def _():
            copy.wait_send()

    relaxed = jnp.logical_or(
        jnp.logical_and(owner, lead_next), jnp.logical_and(phase == 1, group > 0)
    )
    drain(weight_to(back), jnp.logical_or(shares, owner_shares))
    drain(special(TO_LEFT, LEFT, back), has_next)
    drain(special(TO_RHS, RHS, back), shares)
    drain(special(TO_FIRST, FIRST, back), phase < 2)
    drain(special(TO_FINAL, FINAL, back), relaxed)
    drain(special(TO_SECOND, SECOND, back), relaxed)
    drain(special(TO_CHANGE, CHANGE, back), changes)
    drain(relay_of(FIRST), first_owner)
    drain(relay_of(FINAL), jnp.logical_and(lead, group > 0))
    drain(relay_of(SECOND), jnp.logical_and(phase == 1, group > 0))


def per_device(devices, inputs, guess, weights):
    chans, cells = inputs.shape
    states = pl.pallas_call(
        functools.partial(kernel, devices),
        name="cycle",
        out_shape=pltpu.VMEM((COARSEN, cells, chans), jnp.float32),
        in_specs=[pl.BlockSpec(memory_space=pltpu.HBM)] * 3,
        out_specs=pl.BlockSpec(memory_space=pltpu.VMEM),
        scratch_shapes=[
            pltpu.VMEM((2, chans, cells), jnp.float32),
            pltpu.VMEM((COARSEN + 1,) + weights.shape[1:], jnp.bfloat16),
            pltpu.VMEM((STATES, cells, chans), jnp.float32),
            pltpu.VMEM((ROUNDED, cells + 2 * WIDTH, chans), jnp.bfloat16),
            pltpu.VMEM((2, 2, cells + 16, chans // 2), jnp.float32),
            pltpu.VMEM((cells, chans), jnp.float32),
            pltpu.VMEM((cells, chans), jnp.float32),
            pltpu.SemaphoreType.DMA((TO_RHS - TO_LEFT + 1,)),
            pltpu.SemaphoreType.DMA((FINAL - LEFT + 1,)),
            pltpu.SemaphoreType.DMA((1,)),
            pltpu.SemaphoreType.DMA((ROUNDED + 1,)),
            pltpu.SemaphoreType.DMA((2,)),
            pltpu.SemaphoreType.DMA((COARSEN, PIECES)),
        ],
        compiler_params=pltpu.CompilerParams(
            collective_id=0, has_side_effects=True, vmem_limit_bytes=56 * 2**20,
        ),
    )(*[pltpu.with_memory_space_constraint(a, pltpu.HBM) for a in (inputs, guess, weights)])
    return jnp.swapaxes(states, 1, 2)


def solution(mesh):
    return jax.shard_map(
        functools.partial(per_device, mesh.shape["layer"]),
        mesh=mesh,
        in_specs=(P(None, "batch"), P("layer", None, "batch"), P("layer", None, None)),
        out_specs=P("layer", None, "batch"),
        check_vma=False,
    )
```

```python
import functools

import jax
import jax.numpy as jnp
from jax import lax
from jax.experimental import pallas as pl
from jax.experimental.pallas import tpu as pltpu
from jax.sharding import PartitionSpec as P

WIDTH = 16
COARSEN = 4
NONE = 15
PIECES = 2
BLOCKS = 8
ZERO, CP, LF, CC, RH, RHM, TT, PSI, QQ, XZ, OUT, TMP, DUMP = range(13)
STATES = 13
CPB, LFB, OUTB, CCB, TMPB, LEFT, FIRST, SECOND, FINAL, UNSENT = range(10)
TO_LEFT, TO_FIRST, TO_SECOND, TO_FINAL, TO_CHANGE, TO_RHS, CHANGE, RHS = range(10, 18)
ROUNDED = 18
WEIGHT = ROUNDED
NOTHING, PSI_OF_LEFT, FIRST_POINT, START, PUT_0, PUT_1, PUT_2, OWNER_0, OWNER, CHANGES, KEEP = range(11)
FIELDS = ("src", "dst", "w", "add", "factor", "rsrc", "rdst", "by", "recv", "relay", "need", "op")
BY_ONE, BY_TWO = 0, 1
QUARTER, WHOLE, FOUR = 0, 1, 2
ROUNDED_OF = {CP: CPB, LF: LFB, CC: CCB, OUT: OUTB, TMP: TMPB}


def step(src, dst, w, add=ZERO, factor=QUARTER, send=UNSENT, by=BY_ONE,
         recv=NONE, relay=0, need=0, op=NOTHING, rsrc=None):
    if rsrc is None:
        rsrc = ROUNDED_OF[src] if recv == NONE else recv
    rdst = ROUNDED_OF.get(dst, UNSENT) if send == UNSENT else send
    return dict(src=src, dst=dst, w=w, add=add, factor=factor, rsrc=rsrc, rdst=rdst,
                by=by, recv=recv, relay=relay, need=need, op=op)


def programs():
    def fine(send=UNSENT, first=NOTHING, op=NOTHING):
        return [step(CP, CP, 0, op=first), step(CP, CP, 1), step(CP, CP, 2),
                step(CP, CP, 3, send=send, op=op)]

    def again(send=UNSENT, op=NOTHING):
        return [step(LF, CC, 0, recv=LEFT, op=PSI_OF_LEFT), step(CC, CC, 1),
                step(CC, CC, 2), step(CC, RH, 3, add=QQ, send=send, op=op)]

    def whole(recv, dst, relay=0, need=0):
        return step(TMP, dst, COARSEN, add=RHM, factor=WHOLE, recv=recv, relay=relay, need=need)

    def own(src, dst, **kw):
        return step(src, dst, 0, add=RH, factor=WHOLE, **kw)

    last = [step(OUT, OUT, 1, op=PUT_1), step(OUT, OUT, 2, op=PUT_2)]
    body = fine(TO_LEFT) + again()
    mate = fine(TO_LEFT) + again(TO_RHS)
    final = [whole(FINAL, LF, relay=1)]
    owner_second = [whole(SECOND, TMP), step(TMP, PSI, 0, factor=WHOLE, op=OWNER)]
    relaxed = [whole(FIRST, TMP, need=1), own(TMP, CC)] + final + [
        step(LF, DUMP, 0, factor=WHOLE, op=PUT_0)]
    return {
        "start": fine(TO_LEFT, KEEP, START) + last,
        "lead_first": body + [own(LF, CC, recv=FIRST, send=TO_FIRST, by=BY_TWO, op=PUT_0)] + last,
        "mate_first": mate + [own(LF, CC, recv=FIRST, op=PUT_0)] + last,
        "owner_first": body + [
            step(TMP, XZ, 0, factor=FOUR), whole(FIRST, LF, relay=1, need=1),
            own(LF, CC, op=OWNER_0)] + last,
        "head": fine(TO_LEFT) + again(TO_RHS, FIRST_POINT) + [
            own(LF, CC, recv=FINAL, op=PUT_0),
            step(LF, XZ, COARSEN, factor=FOUR, need=2, rsrc=FINAL),
            step(TMP, TMP, COARSEN, factor=FOUR, recv=SECOND, op=CHANGES)] + last,
        "lead": body + [
            own(LF, TMP, recv=FIRST, send=TO_FIRST, by=BY_TWO),
            whole(FINAL, LF, relay=1, need=1),
            own(LF, CC, send=TO_FINAL, by=BY_TWO, op=PUT_0),
            whole(SECOND, TMP, relay=1),
            own(TMP, TMP, send=TO_SECOND, by=BY_TWO)] + last,
        "mate": mate + [own(LF, CC, recv=FINAL, op=PUT_0)] + last,
        "owner": body + relaxed + owner_second + last,
        "owner_last": body + relaxed + last + owner_second,
    }


def packed(values):
    words = []
    for start in (0, 8):
        word = sum(v << (4 * k) for k, v in enumerate(values[start:start + 8]))
        words.append(word - 2**32 if word >= 2**31 else word)
    return words


def kernel(
    devices, x_hbm, g_hbm, w_hbm, o_ref,
    xg, w, st, rounded, part, side_sum, base,
    send_sem, relay_sem, extra_sem, recv_sem, load_sem, weight_sem,
):
    f32, bf16 = jnp.float32, jnp.bfloat16
    p = lax.axis_index("layer")
    phase = lax.rem(p, COARSEN)
    owner = phase == COARSEN - 1
    group = lax.div(p, COARSEN)
    lead = lax.rem(p, 2) == 1
    mate = jnp.logical_not(lead)
    _, cells, chans = st.shape

    own_load = pltpu.make_async_copy(g_hbm.at[0], xg.at[0], load_sem.at[0])
    x_load = pltpu.make_async_copy(x_hbm, xg.at[0], load_sem.at[0])
    start_load = pltpu.make_async_copy(x_hbm, xg.at[1], load_sem.at[1])
    first_owner = jnp.logical_and(owner, group == 0)

    def weight_loads(j):
        rows = w.shape[1] // PIECES
        return [
            pltpu.make_async_copy(
                w_hbm.at[j, pl.ds(n * rows, rows)], w.at[j, pl.ds(n * rows, rows)],
                weight_sem.at[j, n],
            )
            for n in range(PIECES)
        ]

    @pl.when(p == 0)
    def _():
        x_load.start()

    @pl.when(p > 0)
    def _():
        own_load.start()

    for load in weight_loads(0) + weight_loads(1):
        load.start()

    @pl.when(first_owner)
    def _():
        start_load.start()

    barrier = pltpu.get_barrier_semaphore()

    def greet(by, cond):
        @pl.when(cond)
        def _():
            pl.semaphore_signal(
                barrier, inc=1, device_id={"layer": p + by},
                device_id_type=pl.DeviceIdType.MESH,
            )
        return cond.astype(jnp.int32)

    has_next = p < devices - 1
    lead_next = jnp.logical_and(lead, p + 2 < devices)
    last_owner = p + COARSEN >= devices
    greeted = (
        greet(1, has_next) + greet(-1, p > 0)
        + greet(COARSEN - 1, jnp.logical_and(phase == 0, group > 0))
        + greet(1 - COARSEN, jnp.logical_and(owner, group > 0))
        + greet(2, lead_next) + greet(-2, jnp.logical_and(lead, p >= 2))
    )
    shares = jnp.logical_and(mate, p > 0)
    owner_shares = jnp.logical_and(owner, group > 0)
    changes = jnp.logical_and(phase == 0, group > 0)

    roles = [
        ("start", p == 0),
        ("lead_first", jnp.logical_and(group == 0, phase == 1)),
        ("mate_first", jnp.logical_and(group == 0, phase == 2)),
        ("owner_first", first_owner),
        ("head", changes),
        ("lead", jnp.logical_and(group > 0, phase == 1)),
        ("mate", jnp.logical_and(group > 0, phase == 2)),
        ("owner_last", jnp.logical_and(owner, jnp.logical_and(group > 0, last_owner))),
    ]
    listed = programs()

    def chosen(value_of):
        value = jnp.int32(value_of(listed["owner"]))
        for name, cond in roles:
            value = jnp.where(cond, jnp.int32(value_of(listed[name])), value)
        return value

    count = chosen(len)
    words = {
        field: [
            chosen(lambda steps: packed([s[field] for s in steps])[half]) for half in (0, 1)
        ]
        for field in FIELDS
    }

    def entry(field, i):
        low, high = words[field]
        word = jnp.where(i < 8, low, high)
        return jnp.bitwise_and(
            lax.shift_right_logical(word, 4 * jnp.bitwise_and(i, 7)), 15
        )

    def remote(src, dst, ssem, rsem, by):
        return pltpu.make_async_remote_copy(
            src_ref=src, dst_ref=dst, send_sem=ssem, recv_sem=rsem,
            device_id={"layer": p + by}, device_id_type=pl.DeviceIdType.MESH,
        )

    def inner(slot):
        return rounded.at[slot, pl.ds(WIDTH, cells)]

    def landing(slot):
        return jnp.where(slot == TO_RHS, RHS, slot - (TO_LEFT - LEFT))

    def message(slot, by):
        to = landing(slot)
        return remote(inner(slot), inner(to), send_sem.at[slot - TO_LEFT], recv_sem.at[to], by)

    def relay_of(slot):
        return remote(inner(slot), inner(slot), relay_sem.at[slot - LEFT], recv_sem.at[slot], -1)

    back = jnp.where(p > 0, -1, 1)

    def arrived(slot):
        remote(inner(slot), inner(slot), extra_sem.at[0], recv_sem.at[slot], back).wait_recv()

    def weight_to(by):
        return remote(w_hbm.at[0], w.at[COARSEN], extra_sem.at[0], recv_sem.at[WEIGHT], by)

    def special(slot, to, by):
        return remote(inner(slot), inner(to), send_sem.at[slot - TO_LEFT], recv_sem.at[to], by)

    def rounded_store(slot, value):
        rounded[slot, WIDTH:WIDTH + cells, :] = value.astype(bf16)

    def distance(code):
        return jnp.where(code == BY_TWO, 2, 1)

    half = chans // 2
    rounded[:, 0:WIDTH, :] = jnp.zeros((ROUNDED, WIDTH, chans), bf16)
    rounded[:, WIDTH + cells:, :] = jnp.zeros((ROUNDED, WIDTH, chans), bf16)
    part[:, :, 0:8, :] = jnp.zeros((2, 2, 8, half), f32)
    part[:, :, 8 + cells:, :] = jnp.zeros((2, 2, 8, half), f32)
    st[ZERO] = jnp.zeros((cells, chans), f32)

    def put(n):
        o_ref[n] = st[OUT].T

    own_load.wait()
    for load in weight_loads(2):
        load.start()
    loaded = xg[0].T
    st[LF] = loaded
    st[CP] = loaded
    rounded_store(CPB, loaded)

    @pl.when(first_owner)
    def _():
        start_load.wait()
        start = xg[1].T
        st[TMP] = start
        rounded_store(TMPB, start)

    def finish_owner(xy):
        cc = st[CC]
        second = st[RH] - (cc - st[PSI])
        solved = st[XZ] + ((cc - st[xy]) + second)

        @pl.when(lead_next)
        def _():
            rounded_store(TO_FINAL, solved)
            special(TO_FINAL, FINAL, 2).start()
            rounded_store(TO_SECOND, cc)
            special(TO_SECOND, SECOND, 2).start()

        st[CC] = solved

    pl.semaphore_wait(barrier, greeted)

    @pl.when(shares)
    def _():
        weight_to(1).start()

    @pl.when(owner_shares)
    def _():
        weight_to(1 - COARSEN).start()

    rows_of = cells // BLOCKS
    col = lax.rem(lax.broadcasted_iota(jnp.int32, (rows_of, chans), 0), WIDTH)
    order = [
        [(1, 0), (0, 0), (2, 0), (0, 1), (1, 1)],
        [(1, 2), (0, 2), (2, 2), (2, 1), (1, 1)],
    ]

    def push(which, k, m):
        dy, dx = order[m][k]
        tap = 3 * dy + dx
        pltpu.matmul_push_rhs(
            w[which, :, tap * chans:(tap + 1) * chans], k % 2, m, transpose=True
        )

    def wait_weights(j):
        for load in weight_loads(j):
            load.wait()

    def fields_of(i):
        return tuple(entry(field, i) for field in FIELDS)

    def run(sides, middles, i, fields):
        f = dict(zip(FIELDS, fields))

        received = f["recv"] != NONE

        @pl.when(received)
        def _():
            arrived(f["recv"])

            @pl.when(f["relay"] == 1)
            def _():
                relay_of(f["recv"]).start()

        source = f["rsrc"]

        def lhs(dy, r):
            return rounded[source, WIDTH * dy + r * rows_of:WIDTH * dy + (r + 1) * rows_of, :]

        def stream(k):
            for m in (0, 1):
                dy = order[m][k][0]
                total = sides[m] if k < 3 else middles[m]
                taken = range(BLOCKS) if k < 4 else range(m, BLOCKS, 2)
                for n, r in enumerate(taken):
                    pltpu.matmul_acc_lhs(total[r], lhs(dy, r), k % 2 if n == 0 else None)

        for m in (0, 1):
            push(f["w"], 1, m)
        stream(0)
        later = fields_of(i + 1)
        following = dict(zip(FIELDS, later))
        next_weight = jnp.logical_and(i + 1 < count, following["need"] > 0)

        @pl.when(received)
        def _():
            st[f["src"]] = rounded[source, WIDTH:WIDTH + cells, :].astype(f32)

        @pl.when(jnp.logical_or(i < COARSEN - 1, jnp.logical_or(next_weight, f["need"] > 0)))
        def _():
            @pl.when(i < COARSEN - 1)
            def _():
                wait_weights(i + 1)

            @pl.when(next_weight)
            def _():
                remote(w.at[0], w.at[COARSEN], extra_sem.at[0], recv_sem.at[WEIGHT], back).wait_recv()

            @pl.when(f["need"] == 1)
            def _():
                arrived(RHS)
                st[RHM] = rounded[RHS, WIDTH:WIDTH + cells, :].astype(f32)

        for k in range(1, 5):
            for m in (0, 1):
                if k < 4:
                    push(f["w"], k + 1, m)
            stream(k)
        for m in (0, 1):
            push(following["w"], 0, m)
        for r in range(BLOCKS):
            for m in (0, 1):
                t = pltpu.matmul_pop(sides[m][r])
                t = jnp.where(col == (0 if m else WIDTH - 1), 0.0, t)
                for h in (0, 1):
                    part[m, h, 8 + r * rows_of:8 + (r + 1) * rows_of, :] = t[:, h * half:(h + 1) * half]
        base[...] = st[f["src"]] + st[f["add"]]

        factor = jnp.where(f["factor"] == QUARTER, 0.25, jnp.where(f["factor"] == WHOLE, 1.0, 4.0))
        for r in range(BLOCKS):
            at = slice(r * rows_of, (r + 1) * rows_of)
            middle = pltpu.matmul_pop(middles[0][r]) + pltpu.matmul_pop(middles[1][r])
            side = jnp.concatenate([
                part[0, h, 7 + r * rows_of:7 + (r + 1) * rows_of, :]
                + part[1, h, 9 + r * rows_of:9 + (r + 1) * rows_of, :] for h in (0, 1)
            ], 1)
            new = base[at] + factor * jnp.tanh(middle + side)
            st[f["dst"], at] = new
            rounded[f["rdst"], WIDTH + r * rows_of:WIDTH + (r + 1) * rows_of, :] = new.astype(bf16)

        @pl.when(jnp.logical_and(f["rdst"] > UNSENT, has_next))
        def _():
            message(f["rdst"], distance(f["by"])).start()

        op = f["op"]

        @pl.when(op != NOTHING)
        def _():
            @pl.when(op == PSI_OF_LEFT)
            def _():
                psi = st[LF] + 4.0 * (st[CC] - base[...])
                st[PSI] = psi
                st[QQ] = (st[CP] - psi) - st[CP]

            @pl.when(op == KEEP)
            def _():
                st[TT] = 4.0 * (st[CP] - base[...])

            @pl.when(op == START)
            def _():
                psi = st[LF] + st[TT]
                rhs = st[CP] + ((st[CP] - psi) - st[CP])
                first = psi + rhs
                st[CC] = first
                rounded_store(TO_FIRST, first)
                special(TO_FIRST, FIRST, 1).start()

            @pl.when(op == FIRST_POINT)
            def _():
                rounded_store(TO_FIRST, st[PSI] + st[RH])
                special(TO_FIRST, FIRST, 1).start()

            @pl.when(op == OWNER_0)
            def _():
                t = st[CC] - base[...]
                st[TT] = t
                st[PSI] = st[LF] + t
                finish_owner(XZ)

            @pl.when(jnp.logical_or(op == PUT_0, jnp.logical_or(op == START, op == OWNER_0)))
            def _():
                t = jnp.where(op == PUT_0, st[f["dst"]] - base[...], st[TT])
                out = st[LF] + 0.25 * t
                st[OUT] = out
                rounded_store(OUTB, out)

            put_at = jnp.where(op == PUT_1, 1, jnp.where(op == PUT_2, 2, 0))

            @pl.when(jnp.logical_and(op >= START, op <= OWNER_0))
            def _():
                put(put_at)

            @pl.when(op == OWNER)
            def _():
                arrived(CHANGE)
                st[XZ] = rounded[CHANGE, WIDTH:WIDTH + cells, :].astype(f32)
                finish_owner(ZERO)

            @pl.when(op == CHANGES)
            def _():
                rounded_store(TO_CHANGE, st[XZ] - st[TMP])
                special(TO_CHANGE, CHANGE, COARSEN - 1).start()

        return later

    def loop(*totals):
        sides = (totals[:BLOCKS], totals[2 * BLOCKS:3 * BLOCKS])
        middles = (totals[BLOCKS:2 * BLOCKS], totals[3 * BLOCKS:])
        wait_weights(0)
        for load in weight_loads(3):
            load.start()
        for m in (0, 1):
            push(0, 0, m)
        lax.fori_loop(0, count, functools.partial(run, sides, middles), fields_of(0))
        for m in (0, 1):
            pltpu.matmul_acc_lhs(sides[m][0], rounded[CPB, 0:rows_of, :], 0)
            side_sum[0:rows_of, :] = pltpu.matmul_pop(sides[m][0])

    pl.run_scoped(
        loop, *[pltpu.ACC(m)((rows_of, chans), f32) for m in (0, 1) for _ in range(2 * BLOCKS)]
    )
    o_ref[COARSEN - 1] = st[CC].T

    def drain(copy, cond):
        @pl.when(cond)
        def _():
            copy.wait_send()

    relaxed = jnp.logical_or(
        jnp.logical_and(owner, lead_next), jnp.logical_and(phase == 1, group > 0)
    )
    drain(weight_to(back), jnp.logical_or(shares, owner_shares))
    drain(special(TO_LEFT, LEFT, back), has_next)
    drain(special(TO_RHS, RHS, back), shares)
    drain(special(TO_FIRST, FIRST, back), phase < 2)
    drain(special(TO_FINAL, FINAL, back), relaxed)
    drain(special(TO_SECOND, SECOND, back), relaxed)
    drain(special(TO_CHANGE, CHANGE, back), changes)
    drain(relay_of(FIRST), first_owner)
    drain(relay_of(FINAL), jnp.logical_and(lead, group > 0))
    drain(relay_of(SECOND), jnp.logical_and(phase == 1, group > 0))


def per_device(devices, inputs, guess, weights):
    chans, cells = inputs.shape
    return pl.pallas_call(
        functools.partial(kernel, devices),
        name="cycle",
        out_shape=pltpu.VMEM((COARSEN, chans, cells), jnp.float32),
        in_specs=[pl.BlockSpec(memory_space=pltpu.HBM)] * 3,
        out_specs=pl.BlockSpec(memory_space=pltpu.VMEM),
        scratch_shapes=[
            pltpu.VMEM((2, chans, cells), jnp.float32),
            pltpu.VMEM((COARSEN + 1,) + weights.shape[1:], jnp.bfloat16),
            pltpu.VMEM((STATES, cells, chans), jnp.float32),
            pltpu.VMEM((ROUNDED, cells + 2 * WIDTH, chans), jnp.bfloat16),
            pltpu.VMEM((2, 2, cells + 16, chans // 2), jnp.float32),
            pltpu.VMEM((cells, chans), jnp.float32),
            pltpu.VMEM((cells, chans), jnp.float32),
            pltpu.SemaphoreType.DMA((TO_RHS - TO_LEFT + 1,)),
            pltpu.SemaphoreType.DMA((FINAL - LEFT + 1,)),
            pltpu.SemaphoreType.DMA((1,)),
            pltpu.SemaphoreType.DMA((ROUNDED + 1,)),
            pltpu.SemaphoreType.DMA((2,)),
            pltpu.SemaphoreType.DMA((COARSEN, PIECES)),
        ],
        compiler_params=pltpu.CompilerParams(
            collective_id=0, has_side_effects=True, vmem_limit_bytes=56 * 2**20,
        ),
    )(*[pltpu.with_memory_space_constraint(a, pltpu.HBM) for a in (inputs, guess, weights)])


def solution(mesh):
    return jax.shard_map(
        functools.partial(per_device, mesh.shape["layer"]),
        mesh=mesh,
        in_specs=(P(None, "batch"), P("layer", None, "batch"), P("layer", None, None)),
        out_specs=P("layer", None, "batch"),
        check_vma=False,
    )
```

```python
import functools

import jax
import jax.numpy as jnp
from jax import lax
from jax.experimental import pallas as pl
from jax.experimental.pallas import tpu as pltpu
from jax.sharding import PartitionSpec as P

WIDTH = 16
COARSEN = 4
NONE = 15
PIECES = 2
BLOCKS = 8
ROWS = 128
ZERO, CP, LF, CC, RH, RHM, TT, PSI, QQ, XZ, OUT, TMP, DUMP = range(13)
STATES = 13
CPB, LFB, OUTB, CCB, TMPB, LEFT, FIRST, SECOND, FINAL, UNSENT = range(10)
TO_LEFT, TO_FIRST, TO_SECOND, TO_FINAL, TO_CHANGE, TO_RHS, CHANGE, RHS = range(10, 18)
ROUNDED = 18
WEIGHT = ROUNDED
NOTHING, PSI_OF_LEFT, FIRST_POINT, CHANGES, KEEP, START, PUT_0, OWNER_0, PUT_1, PUT_2, PUT_LAST, OWNER = range(12)
FIELDS = ("src", "dst", "w", "add", "factor", "rsrc", "rdst", "by", "recv", "relay", "need", "op")
BY_ONE, BY_TWO = 0, 1
QUARTER, WHOLE, FOUR = 0, 1, 2
ROUNDED_OF = {CP: CPB, LF: LFB, CC: CCB, OUT: OUTB, TMP: TMPB}


def step(src, dst, w, add=ZERO, factor=QUARTER, send=UNSENT, by=BY_ONE,
         recv=NONE, relay=0, need=0, op=NOTHING, rsrc=None):
    if rsrc is None:
        rsrc = ROUNDED_OF[src] if recv == NONE else recv
    rdst = ROUNDED_OF.get(dst, UNSENT) if send == UNSENT else send
    return dict(src=src, dst=dst, w=w, add=add, factor=factor, rsrc=rsrc, rdst=rdst,
                by=by, recv=recv, relay=relay, need=need, op=op)


def programs():
    def fine(send=UNSENT, first=NOTHING, op=NOTHING):
        return [step(CP, CP, 0, op=first), step(CP, CP, 1), step(CP, CP, 2),
                step(CP, CP, 3, send=send, op=op)]

    def again(send=UNSENT, op=NOTHING):
        return [step(LF, CC, 0, recv=LEFT, op=PSI_OF_LEFT), step(CC, CC, 1),
                step(CC, CC, 2), step(CC, RH, 3, add=QQ, send=send, op=op)]

    def whole(recv, dst, relay=0, need=0):
        return step(TMP, dst, COARSEN, add=RHM, factor=WHOLE, recv=recv, relay=relay, need=need)

    def own(src, dst, **kw):
        return step(src, dst, 0, add=RH, factor=WHOLE, **kw)

    last = [step(OUT, OUT, 1, op=PUT_1), step(OUT, OUT, 2, op=PUT_LAST)]
    early = [step(OUT, OUT, 1, op=PUT_1), step(OUT, OUT, 2, op=PUT_2)]
    body = fine(TO_LEFT) + again()
    mate = fine(TO_LEFT) + again(TO_RHS)
    final = [whole(FINAL, LF, relay=1)]
    owner_second = [whole(SECOND, TMP), step(TMP, PSI, 0, factor=WHOLE, op=OWNER)]
    relaxed = [whole(FIRST, TMP, need=1), own(TMP, CC)] + final + [
        step(LF, DUMP, 0, factor=WHOLE, op=PUT_0)]
    return {
        "start": fine(TO_LEFT, KEEP, START) + last,
        "lead_first": body + [own(LF, CC, recv=FIRST, send=TO_FIRST, by=BY_TWO, op=PUT_0)] + last,
        "mate_first": mate + [own(LF, CC, recv=FIRST, op=PUT_0)] + last,
        "owner_first": body + [
            step(TMP, XZ, 0, factor=FOUR), whole(FIRST, LF, relay=1, need=1),
            own(LF, CC, op=OWNER_0)] + last,
        "head": fine(TO_LEFT) + again(TO_RHS, FIRST_POINT) + [
            own(LF, CC, recv=FINAL, op=PUT_0),
            step(LF, XZ, COARSEN, factor=FOUR, need=2, rsrc=FINAL),
            step(TMP, TMP, COARSEN, factor=FOUR, recv=SECOND, op=CHANGES)] + last,
        "lead": body + [
            own(LF, TMP, recv=FIRST, send=TO_FIRST, by=BY_TWO),
            whole(FINAL, LF, relay=1, need=1),
            own(LF, CC, send=TO_FINAL, by=BY_TWO, op=PUT_0),
            whole(SECOND, TMP, relay=1),
            own(TMP, TMP, send=TO_SECOND, by=BY_TWO)] + last,
        "mate": mate + [own(LF, CC, recv=FINAL, op=PUT_0)] + last,
        "owner": body + relaxed + owner_second + last,
        "owner_last": body + relaxed + early + owner_second,
    }


def packed(values):
    words = []
    for start in (0, 8):
        word = sum(v << (4 * k) for k, v in enumerate(values[start:start + 8]))
        words.append(word - 2**32 if word >= 2**31 else word)
    return words


def kernel(
    devices, x_hbm, g_hbm, w_hbm, o_ref,
    xg, w, st, rounded, part, side_sum, base,
    send_sem, relay_sem, extra_sem, recv_sem, load_sem, weight_sem,
):
    f32, bf16 = jnp.float32, jnp.bfloat16
    p = lax.axis_index("layer")
    phase = lax.rem(p, COARSEN)
    owner = phase == COARSEN - 1
    group = lax.div(p, COARSEN)
    lead = lax.rem(p, 2) == 1
    mate = jnp.logical_not(lead)
    _, cells, chans = st.shape

    own_load = pltpu.make_async_copy(g_hbm.at[0], xg.at[0], load_sem.at[0])
    x_load = pltpu.make_async_copy(x_hbm, xg.at[0], load_sem.at[0])
    start_load = pltpu.make_async_copy(x_hbm, xg.at[1], load_sem.at[1])
    first_owner = jnp.logical_and(owner, group == 0)

    def weight_loads(j):
        rows = w.shape[1] // PIECES
        return [
            pltpu.make_async_copy(
                w_hbm.at[j, pl.ds(n * rows, rows)], w.at[j, pl.ds(n * rows, rows)],
                weight_sem.at[j, n],
            )
            for n in range(PIECES)
        ]

    @pl.when(p == 0)
    def _():
        x_load.start()

    @pl.when(p > 0)
    def _():
        own_load.start()

    for load in weight_loads(0) + weight_loads(1):
        load.start()

    @pl.when(first_owner)
    def _():
        start_load.start()

    barrier = pltpu.get_barrier_semaphore()

    def greet(by, cond):
        @pl.when(cond)
        def _():
            pl.semaphore_signal(
                barrier, inc=1, device_id={"layer": p + by},
                device_id_type=pl.DeviceIdType.MESH,
            )
        return cond.astype(jnp.int32)

    has_next = p < devices - 1
    lead_next = jnp.logical_and(lead, p + 2 < devices)
    last_owner = p + COARSEN >= devices
    greeted = (
        greet(1, has_next) + greet(-1, p > 0)
        + greet(COARSEN - 1, jnp.logical_and(phase == 0, group > 0))
        + greet(1 - COARSEN, jnp.logical_and(owner, group > 0))
        + greet(2, lead_next) + greet(-2, jnp.logical_and(lead, p >= 2))
    )
    shares = jnp.logical_and(mate, p > 0)
    owner_shares = jnp.logical_and(owner, group > 0)
    changes = jnp.logical_and(phase == 0, group > 0)

    roles = [
        ("start", p == 0),
        ("lead_first", jnp.logical_and(group == 0, phase == 1)),
        ("mate_first", jnp.logical_and(group == 0, phase == 2)),
        ("owner_first", first_owner),
        ("head", changes),
        ("lead", jnp.logical_and(group > 0, phase == 1)),
        ("mate", jnp.logical_and(group > 0, phase == 2)),
        ("owner_last", jnp.logical_and(owner, jnp.logical_and(group > 0, last_owner))),
    ]
    listed = programs()

    def chosen(value_of):
        value = jnp.int32(value_of(listed["owner"]))
        for name, cond in roles:
            value = jnp.where(cond, jnp.int32(value_of(listed[name])), value)
        return value

    count = chosen(len)
    words = {
        field: [
            chosen(lambda steps: packed([s[field] for s in steps])[half]) for half in (0, 1)
        ]
        for field in FIELDS
    }

    def entry(field, i):
        low, high = words[field]
        word = jnp.where(i < 8, low, high)
        return jnp.bitwise_and(
            lax.shift_right_logical(word, 4 * jnp.bitwise_and(i, 7)), 15
        )

    def remote(src, dst, ssem, rsem, by):
        return pltpu.make_async_remote_copy(
            src_ref=src, dst_ref=dst, send_sem=ssem, recv_sem=rsem,
            device_id={"layer": p + by}, device_id_type=pl.DeviceIdType.MESH,
        )

    def inner(slot):
        return rounded.at[slot, pl.ds(WIDTH, cells)]

    def landing(slot):
        return jnp.where(slot == TO_RHS, RHS, slot - (TO_LEFT - LEFT))

    def message(slot, by):
        to = landing(slot)
        return remote(inner(slot), inner(to), send_sem.at[slot - TO_LEFT], recv_sem.at[to], by)

    def relay_of(slot):
        return remote(inner(slot), inner(slot), relay_sem.at[slot - LEFT], recv_sem.at[slot], -1)

    back = jnp.where(p > 0, -1, 1)

    def arrived(slot):
        remote(inner(slot), inner(slot), extra_sem.at[0], recv_sem.at[slot], back).wait_recv()

    def weight_to(by):
        return remote(w_hbm.at[0], w.at[COARSEN], extra_sem.at[0], recv_sem.at[WEIGHT], by)

    def special(slot, to, by):
        return remote(inner(slot), inner(to), send_sem.at[slot - TO_LEFT], recv_sem.at[to], by)

    def rounded_store(slot, value):
        rounded[slot, WIDTH:WIDTH + cells, :] = value.astype(bf16)

    def distance(code):
        return jnp.where(code == BY_TWO, 2, 1)

    half = chans // 2
    rounded[:, 0:WIDTH, :] = jnp.zeros((ROUNDED, WIDTH, chans), bf16)
    rounded[:, WIDTH + cells:, :] = jnp.zeros((ROUNDED, WIDTH, chans), bf16)
    part[:, :, 0:8, :] = jnp.zeros((2, 2, 8, half), f32)
    part[:, :, 8 + cells:, :] = jnp.zeros((2, 2, 8, half), f32)
    st[ZERO] = jnp.zeros((cells, chans), f32)

    def put(slot, n):
        o_ref[n] = st[slot].T

    def by_rows(body):
        def rows(r, _):
            first = pl.multiple_of(r * ROWS, ROWS)
            body(pl.ds(first, ROWS), pl.ds(WIDTH + first, ROWS))
            return 0

        lax.fori_loop(0, cells // ROWS, rows, 0)

    own_load.wait()
    for load in weight_loads(2):
        load.start()
    loaded = xg[0].T
    st[LF] = loaded
    st[CP] = loaded
    rounded_store(CPB, loaded)

    @pl.when(first_owner)
    def _():
        start_load.wait()
        start = xg[1].T
        st[TMP] = start
        rounded_store(TMPB, start)

    def send_solved():
        @pl.when(lead_next)
        def _():
            special(TO_FINAL, FINAL, 2).start()
            special(TO_SECOND, SECOND, 2).start()

    def solve(at, inner_at, psi, xz, xy):
        cc = st[CC, at]
        second = st[RH, at] - (cc - psi)
        solved = xz + ((cc - xy) + second)
        rounded[TO_FINAL, inner_at] = solved.astype(bf16)
        rounded[TO_SECOND, inner_at] = cc.astype(bf16)
        st[CC, at] = solved

    pl.semaphore_wait(barrier, greeted)

    @pl.when(owner_shares)
    def _():
        weight_to(1 - COARSEN).start()

    rows_of = cells // BLOCKS
    col = lax.rem(lax.broadcasted_iota(jnp.int32, (rows_of, chans), 0), WIDTH)
    order = [
        [(1, 0), (0, 0), (2, 0), (0, 1), (1, 1)],
        [(1, 2), (0, 2), (2, 2), (2, 1), (1, 1)],
    ]

    def push(which, k, m):
        dy, dx = order[m][k]
        tap = 3 * dy + dx
        pltpu.matmul_push_rhs(
            w[which, :, tap * chans:(tap + 1) * chans], k % 2, m, transpose=True
        )

    def wait_weights(j):
        for load in weight_loads(j):
            load.wait()

    def fields_of(i):
        return tuple(entry(field, i) for field in FIELDS)

    def run(sides, middles, i, fields):
        f = dict(zip(FIELDS, fields))

        @pl.when(jnp.logical_and(i == 1, shares))
        def _():
            weight_to(1).start()

        received = f["recv"] != NONE

        @pl.when(received)
        def _():
            arrived(f["recv"])

            @pl.when(f["relay"] == 1)
            def _():
                relay_of(f["recv"]).start()

        source = f["rsrc"]

        def lhs(dy, r):
            return rounded[source, WIDTH * dy + r * rows_of:WIDTH * dy + (r + 1) * rows_of, :]

        def stream(k):
            for m in (0, 1):
                dy = order[m][k][0]
                total = sides[m] if k < 3 else middles[m]
                taken = range(BLOCKS) if k < 4 else range(m, BLOCKS, 2)
                for n, r in enumerate(taken):
                    pltpu.matmul_acc_lhs(total[r], lhs(dy, r), k % 2 if n == 0 else None)

        for m in (0, 1):
            push(f["w"], 1, m)
        stream(0)
        later = fields_of(i + 1)
        following = dict(zip(FIELDS, later))
        next_weight = jnp.logical_and(i + 1 < count, following["need"] > 0)

        @pl.when(received)
        def _():
            st[f["src"]] = rounded[source, WIDTH:WIDTH + cells, :].astype(f32)

        @pl.when(jnp.logical_or(i < COARSEN - 1, jnp.logical_or(next_weight, f["need"] > 0)))
        def _():
            @pl.when(i < COARSEN - 1)
            def _():
                wait_weights(i + 1)

            @pl.when(next_weight)
            def _():
                remote(w.at[0], w.at[COARSEN], extra_sem.at[0], recv_sem.at[WEIGHT], back).wait_recv()

            @pl.when(f["need"] == 1)
            def _():
                arrived(RHS)
                st[RHM] = rounded[RHS, WIDTH:WIDTH + cells, :].astype(f32)

        for k in range(1, 5):
            for m in (0, 1):
                if k < 4:
                    push(f["w"], k + 1, m)
            stream(k)
        for m in (0, 1):
            push(following["w"], 0, m)
        for r in range(BLOCKS):
            for m in (0, 1):
                t = pltpu.matmul_pop(sides[m][r])
                t = jnp.where(col == (0 if m else WIDTH - 1), 0.0, t)
                for h in (0, 1):
                    part[m, h, 8 + r * rows_of:8 + (r + 1) * rows_of, :] = t[:, h * half:(h + 1) * half]
        base[...] = st[f["src"]] + st[f["add"]]

        factor = jnp.where(f["factor"] == QUARTER, 0.25, jnp.where(f["factor"] == WHOLE, 1.0, 4.0))
        for r in range(BLOCKS):
            at = slice(r * rows_of, (r + 1) * rows_of)
            middle = pltpu.matmul_pop(middles[0][r]) + pltpu.matmul_pop(middles[1][r])
            side = jnp.concatenate([
                part[0, h, 7 + r * rows_of:7 + (r + 1) * rows_of, :]
                + part[1, h, 9 + r * rows_of:9 + (r + 1) * rows_of, :] for h in (0, 1)
            ], 1)
            new = base[at] + factor * jnp.tanh(middle + side)
            st[f["dst"], at] = new
            rounded[f["rdst"], WIDTH + r * rows_of:WIDTH + (r + 1) * rows_of, :] = new.astype(bf16)

        @pl.when(jnp.logical_and(f["rdst"] > UNSENT, has_next))
        def _():
            message(f["rdst"], distance(f["by"])).start()

        op = f["op"]

        @pl.when(op != NOTHING)
        def _():
            @pl.when(op == PSI_OF_LEFT)
            def _():
                def rows(at, _):
                    psi = st[LF, at] + 4.0 * (st[CC, at] - base[at])
                    st[PSI, at] = psi
                    st[QQ, at] = (st[CP, at] - psi) - st[CP, at]

                by_rows(rows)

            @pl.when(op == KEEP)
            def _():
                def rows(at, _):
                    st[TT, at] = 4.0 * (st[CP, at] - base[at])

                by_rows(rows)

            @pl.when(op == START)
            def _():
                def rows(at, inner_at):
                    psi = st[LF, at] + st[TT, at]
                    rhs = st[CP, at] + ((st[CP, at] - psi) - st[CP, at])
                    first = psi + rhs
                    st[CC, at] = first
                    rounded[TO_FIRST, inner_at] = first.astype(bf16)

                by_rows(rows)
                special(TO_FIRST, FIRST, 1).start()

            @pl.when(op == FIRST_POINT)
            def _():
                def rows(at, inner_at):
                    rounded[TO_FIRST, inner_at] = (st[PSI, at] + st[RH, at]).astype(bf16)

                by_rows(rows)
                special(TO_FIRST, FIRST, 1).start()

            @pl.when(op == OWNER_0)
            def _():
                def rows(at, inner_at):
                    t = st[CC, at] - base[at]
                    st[TT, at] = t
                    solve(at, inner_at, st[LF, at] + t, st[XZ, at], st[XZ, at])

                by_rows(rows)
                send_solved()

            @pl.when(jnp.logical_and(op >= START, op <= OWNER_0))
            def _():
                def rows(at, inner_at):
                    t = jnp.where(op == PUT_0, st[f["dst"], at] - base[at], st[TT, at])
                    out = st[LF, at] + 0.25 * t
                    st[OUT, at] = out
                    rounded[OUTB, inner_at] = out.astype(bf16)

                by_rows(rows)

            @pl.when(op == OWNER)
            def _():
                arrived(CHANGE)

                def rows(at, inner_at):
                    change = rounded[CHANGE, inner_at].astype(f32)
                    solve(at, inner_at, st[PSI, at], change, st[ZERO, at])

                by_rows(rows)
                send_solved()

            @pl.when(op >= START)
            def _():
                whole_put = op == OWNER

                def one(n, _):
                    put_last = jnp.logical_or(whole_put, n == 1)
                    place = jnp.where(op >= PUT_1, op - PUT_1 + 1, 0)
                    put(
                        jnp.where(put_last, CC, OUT),
                        jnp.where(put_last, COARSEN - 1, jnp.minimum(place, COARSEN - 2)),
                    )
                    return 0

                lax.fori_loop(0, jnp.where(op == PUT_LAST, 2, 1), one, 0)

            @pl.when(op == CHANGES)
            def _():
                def rows(at, inner_at):
                    rounded[TO_CHANGE, inner_at] = (st[XZ, at] - st[TMP, at]).astype(bf16)

                by_rows(rows)
                special(TO_CHANGE, CHANGE, COARSEN - 1).start()

        return later

    def loop(*totals):
        sides = (totals[:BLOCKS], totals[2 * BLOCKS:3 * BLOCKS])
        middles = (totals[BLOCKS:2 * BLOCKS], totals[3 * BLOCKS:])
        wait_weights(0)
        for load in weight_loads(3):
            load.start()
        for m in (0, 1):
            push(0, 0, m)
        lax.fori_loop(0, count, functools.partial(run, sides, middles), fields_of(0))
        for m in (0, 1):
            pltpu.matmul_acc_lhs(sides[m][0], rounded[CPB, 0:rows_of, :], 0)
            side_sum[0:rows_of, :] = pltpu.matmul_pop(sides[m][0])

    pl.run_scoped(
        loop, *[pltpu.ACC(m)((rows_of, chans), f32) for m in (0, 1) for _ in range(2 * BLOCKS)]
    )

    def drain(copy, cond):
        @pl.when(cond)
        def _():
            copy.wait_send()

    relaxed = jnp.logical_or(
        jnp.logical_and(owner, lead_next), jnp.logical_and(phase == 1, group > 0)
    )
    drain(weight_to(back), jnp.logical_or(shares, owner_shares))
    drain(special(TO_LEFT, LEFT, back), has_next)
    drain(special(TO_RHS, RHS, back), shares)
    drain(special(TO_FIRST, FIRST, back), phase < 2)
    drain(special(TO_FINAL, FINAL, back), relaxed)
    drain(special(TO_SECOND, SECOND, back), relaxed)
    drain(special(TO_CHANGE, CHANGE, back), changes)
    drain(relay_of(FIRST), first_owner)
    drain(relay_of(FINAL), jnp.logical_and(lead, group > 0))
    drain(relay_of(SECOND), jnp.logical_and(phase == 1, group > 0))


def per_device(devices, inputs, guess, weights):
    chans, cells = inputs.shape
    return pl.pallas_call(
        functools.partial(kernel, devices),
        name="cycle",
        out_shape=pltpu.VMEM((COARSEN, chans, cells), jnp.float32),
        in_specs=[pl.BlockSpec(memory_space=pltpu.HBM)] * 3,
        out_specs=pl.BlockSpec(memory_space=pltpu.VMEM),
        scratch_shapes=[
            pltpu.VMEM((2, chans, cells), jnp.float32),
            pltpu.VMEM((COARSEN + 1,) + weights.shape[1:], jnp.bfloat16),
            pltpu.VMEM((STATES, cells, chans), jnp.float32),
            pltpu.VMEM((ROUNDED, cells + 2 * WIDTH, chans), jnp.bfloat16),
            pltpu.VMEM((2, 2, cells + 16, chans // 2), jnp.float32),
            pltpu.VMEM((cells, chans), jnp.float32),
            pltpu.VMEM((cells, chans), jnp.float32),
            pltpu.SemaphoreType.DMA((TO_RHS - TO_LEFT + 1,)),
            pltpu.SemaphoreType.DMA((FINAL - LEFT + 1,)),
            pltpu.SemaphoreType.DMA((1,)),
            pltpu.SemaphoreType.DMA((ROUNDED + 1,)),
            pltpu.SemaphoreType.DMA((2,)),
            pltpu.SemaphoreType.DMA((COARSEN, PIECES)),
        ],
        compiler_params=pltpu.CompilerParams(
            collective_id=0, has_side_effects=True, vmem_limit_bytes=56 * 2**20,
        ),
    )(*[pltpu.with_memory_space_constraint(a, pltpu.HBM) for a in (inputs, guess, weights)])


def solution(mesh):
    return jax.shard_map(
        functools.partial(per_device, mesh.shape["layer"]),
        mesh=mesh,
        in_specs=(P(None, "batch"), P("layer", None, "batch"), P("layer", None, None)),
        out_specs=P("layer", None, "batch"),
        check_vma=False,
    )
```

```python
import functools

import jax
import jax.numpy as jnp
from jax import lax
from jax.experimental import pallas as pl
from jax.experimental.pallas import tpu as pltpu
from jax.sharding import PartitionSpec as P

WIDTH = 16
COARSEN = 4
NONE = 15
PIECES = 2
BLOCKS = 8
ZERO, CP, LF, CC, RH, RHM, TT, PSI, QQ, XZ, OUT, TMP, DUMP = range(13)
STATES = 13
CPB, LFB, OUTB, CCB, TMPB, LEFT, FIRST, SECOND, FINAL, UNSENT = range(10)
TO_LEFT, TO_FIRST, TO_SECOND, TO_FINAL, TO_CHANGE, TO_RHS, CHANGE, RHS = range(10, 18)
ROUNDED = 18
WEIGHT = ROUNDED
NOTHING, PSI_OF_LEFT, FIRST_POINT, START, PUT_0, PUT_1, PUT_2, PUT_OUT, OWNER_0, OWNER, CHANGES, KEEP = range(12)
FIELDS = ("src", "dst", "w", "add", "factor", "rsrc", "rdst", "by", "recv", "relay", "need", "op")
BY_ONE, BY_TWO = 0, 1
QUARTER, WHOLE, FOUR = 0, 1, 2
ROUNDED_OF = {CP: CPB, LF: LFB, CC: CCB, OUT: OUTB, TMP: TMPB}


def step(src, dst, w, add=ZERO, factor=QUARTER, send=UNSENT, by=BY_ONE,
         recv=NONE, relay=0, need=0, op=NOTHING, rsrc=None):
    if rsrc is None:
        rsrc = ROUNDED_OF[src] if recv == NONE else recv
    rdst = ROUNDED_OF.get(dst, UNSENT) if send == UNSENT else send
    return dict(src=src, dst=dst, w=w, add=add, factor=factor, rsrc=rsrc, rdst=rdst,
                by=by, recv=recv, relay=relay, need=need, op=op)


def programs():
    def fine(send=UNSENT, first=NOTHING, op=NOTHING):
        return [step(CP, CP, 0, op=first), step(CP, CP, 1), step(CP, CP, 2),
                step(CP, CP, 3, send=send, op=op)]

    def again(send=UNSENT, op=NOTHING):
        return [step(LF, CC, 0, recv=LEFT, op=PSI_OF_LEFT), step(CC, CC, 1),
                step(CC, CC, 2), step(CC, RH, 3, add=QQ, send=send, op=op)]

    def whole(recv, dst, relay=0, need=0):
        return step(TMP, dst, COARSEN, add=RHM, factor=WHOLE, recv=recv, relay=relay, need=need)

    def own(src, dst, **kw):
        return step(src, dst, 0, add=RH, factor=WHOLE, **kw)

    last = [step(OUT, OUT, 1, op=PUT_1), step(OUT, OUT, 2, op=PUT_2)]
    body = fine(TO_LEFT) + again()
    mate = fine(TO_LEFT) + again(TO_RHS)
    final = [whole(FINAL, LF, relay=1)]
    owner_second = [whole(SECOND, TMP), step(TMP, PSI, 0, factor=WHOLE, op=OWNER)]
    relaxed = [whole(FIRST, TMP, need=1), own(TMP, CC)] + final + [
        step(LF, OUT, 0, op=PUT_OUT)]
    return {
        "start": fine(TO_LEFT, KEEP, START) + last,
        "lead_first": body + [own(LF, CC, recv=FIRST, send=TO_FIRST, by=BY_TWO, op=PUT_0)] + last,
        "mate_first": mate + [own(LF, CC, recv=FIRST, op=PUT_0)] + last,
        "owner_first": body + [
            step(TMP, XZ, 0, factor=FOUR), whole(FIRST, LF, relay=1, need=1),
            own(LF, CC, send=TO_SECOND, op=OWNER_0)] + last,
        "head": fine(TO_LEFT) + again(TO_RHS, FIRST_POINT) + [
            own(LF, CC, recv=FINAL, op=PUT_0),
            step(LF, XZ, COARSEN, factor=FOUR, need=2, rsrc=FINAL),
            step(TMP, TMP, COARSEN, factor=FOUR, recv=SECOND, op=CHANGES)] + last,
        "lead": body + [
            own(LF, TMP, recv=FIRST, send=TO_FIRST, by=BY_TWO),
            whole(FINAL, LF, relay=1, need=1),
            own(LF, CC, send=TO_FINAL, by=BY_TWO, op=PUT_0),
            whole(SECOND, TMP, relay=1),
            own(TMP, TMP, send=TO_SECOND, by=BY_TWO)] + last,
        "mate": mate + [own(LF, CC, recv=FINAL, op=PUT_0)] + last,
        "owner": body + relaxed + owner_second + last,
        "owner_last": body + relaxed + last + owner_second,
    }


def packed(values):
    words = []
    for start in (0, 8):
        word = sum(v << (4 * k) for k, v in enumerate(values[start:start + 8]))
        words.append(word - 2**32 if word >= 2**31 else word)
    return words


def kernel(
    devices, x_hbm, g_hbm, w_hbm, o_ref,
    xg, w, st, rounded, part, side_sum, base,
    send_sem, relay_sem, extra_sem, recv_sem, load_sem, weight_sem,
):
    f32, bf16 = jnp.float32, jnp.bfloat16
    p = lax.axis_index("layer")
    phase = lax.rem(p, COARSEN)
    owner = phase == COARSEN - 1
    group = lax.div(p, COARSEN)
    lead = lax.rem(p, 2) == 1
    mate = jnp.logical_not(lead)
    _, cells, chans = st.shape

    own_load = pltpu.make_async_copy(g_hbm.at[0], xg.at[0], load_sem.at[0])
    x_load = pltpu.make_async_copy(x_hbm, xg.at[0], load_sem.at[0])
    start_load = pltpu.make_async_copy(x_hbm, xg.at[1], load_sem.at[1])
    first_owner = jnp.logical_and(owner, group == 0)

    def weight_loads(j):
        rows = w.shape[1] // PIECES
        return [
            pltpu.make_async_copy(
                w_hbm.at[j, pl.ds(n * rows, rows)], w.at[j, pl.ds(n * rows, rows)],
                weight_sem.at[j, n],
            )
            for n in range(PIECES)
        ]

    @pl.when(p == 0)
    def _():
        x_load.start()

    @pl.when(p > 0)
    def _():
        own_load.start()

    for load in weight_loads(0) + weight_loads(1):
        load.start()

    @pl.when(first_owner)
    def _():
        start_load.start()

    barrier = pltpu.get_barrier_semaphore()

    def greet(by, cond):
        @pl.when(cond)
        def _():
            pl.semaphore_signal(
                barrier, inc=1, device_id={"layer": p + by},
                device_id_type=pl.DeviceIdType.MESH,
            )
        return cond.astype(jnp.int32)

    has_next = p < devices - 1
    lead_next = jnp.logical_and(lead, p + 2 < devices)
    last_owner = p + COARSEN >= devices
    greeted = (
        greet(1, has_next) + greet(-1, p > 0)
        + greet(COARSEN - 1, jnp.logical_and(phase == 0, group > 0))
        + greet(1 - COARSEN, jnp.logical_and(owner, group > 0))
        + greet(2, lead_next) + greet(-2, jnp.logical_and(lead, p >= 2))
    )
    shares = jnp.logical_and(mate, p > 0)
    owner_shares = jnp.logical_and(owner, group > 0)
    changes = jnp.logical_and(phase == 0, group > 0)

    roles = [
        ("start", p == 0),
        ("lead_first", jnp.logical_and(group == 0, phase == 1)),
        ("mate_first", jnp.logical_and(group == 0, phase == 2)),
        ("owner_first", first_owner),
        ("head", changes),
        ("lead", jnp.logical_and(group > 0, phase == 1)),
        ("mate", jnp.logical_and(group > 0, phase == 2)),
        ("owner_last", jnp.logical_and(owner, jnp.logical_and(group > 0, last_owner))),
    ]
    listed = programs()

    def chosen(value_of):
        value = jnp.int32(value_of(listed["owner"]))
        for name, cond in roles:
            value = jnp.where(cond, jnp.int32(value_of(listed[name])), value)
        return value

    count = chosen(len)
    words = {
        field: [
            chosen(lambda steps: packed([s[field] for s in steps])[half]) for half in (0, 1)
        ]
        for field in FIELDS
    }

    def entry(field, i):
        low, high = words[field]
        word = jnp.where(i < 8, low, high)
        return jnp.bitwise_and(
            lax.shift_right_logical(word, 4 * jnp.bitwise_and(i, 7)), 15
        )

    def remote(src, dst, ssem, rsem, by):
        return pltpu.make_async_remote_copy(
            src_ref=src, dst_ref=dst, send_sem=ssem, recv_sem=rsem,
            device_id={"layer": p + by}, device_id_type=pl.DeviceIdType.MESH,
        )

    def inner(slot):
        return rounded.at[slot, pl.ds(WIDTH, cells)]

    def landing(slot):
        return jnp.where(slot == TO_RHS, RHS, slot - (TO_LEFT - LEFT))

    def message(slot, by):
        to = landing(slot)
        return remote(inner(slot), inner(to), send_sem.at[slot - TO_LEFT], recv_sem.at[to], by)

    def relay_of(slot):
        return remote(inner(slot), inner(slot), relay_sem.at[slot - LEFT], recv_sem.at[slot], -1)

    back = jnp.where(p > 0, -1, 1)

    def arrived(slot):
        remote(inner(slot), inner(slot), extra_sem.at[0], recv_sem.at[slot], back).wait_recv()

    def weight_to(by):
        return remote(w_hbm.at[0], w.at[COARSEN], extra_sem.at[0], recv_sem.at[WEIGHT], by)

    def special(slot, to, by):
        return remote(inner(slot), inner(to), send_sem.at[slot - TO_LEFT], recv_sem.at[to], by)

    def rounded_store(slot, value):
        rounded[slot, WIDTH:WIDTH + cells, :] = value.astype(bf16)

    def distance(code):
        return jnp.where(code == BY_TWO, 2, 1)

    half = chans // 2
    rounded[:, 0:WIDTH, :] = jnp.zeros((ROUNDED, WIDTH, chans), bf16)
    rounded[:, WIDTH + cells:, :] = jnp.zeros((ROUNDED, WIDTH, chans), bf16)
    part[:, :, 0:8, :] = jnp.zeros((2, 2, 8, half), f32)
    part[:, :, 8 + cells:, :] = jnp.zeros((2, 2, 8, half), f32)
    st[ZERO] = jnp.zeros((cells, chans), f32)

    def put(n):
        o_ref[n] = st[OUT].T

    own_load.wait()
    for load in weight_loads(2):
        load.start()
    loaded = xg[0].T
    st[LF] = loaded
    st[CP] = loaded
    rounded_store(CPB, loaded)

    @pl.when(first_owner)
    def _():
        start_load.wait()
        start = xg[1].T
        st[TMP] = start
        rounded_store(TMPB, start)

    def send_solved():
        @pl.when(lead_next)
        def _():
            special(TO_FINAL, FINAL, 2).start()
            special(TO_SECOND, SECOND, 2).start()

    pl.semaphore_wait(barrier, greeted)

    @pl.when(shares)
    def _():
        weight_to(1).start()

    @pl.when(owner_shares)
    def _():
        weight_to(1 - COARSEN).start()

    rows_of = cells // BLOCKS
    col = lax.rem(lax.broadcasted_iota(jnp.int32, (rows_of, chans), 0), WIDTH)
    order = [
        [(1, 0), (0, 0), (2, 0), (0, 1), (1, 1)],
        [(1, 2), (0, 2), (2, 2), (2, 1), (1, 1)],
    ]

    def push(which, k, m):
        dy, dx = order[m][k]
        tap = 3 * dy + dx
        pltpu.matmul_push_rhs(
            w[which, :, tap * chans:(tap + 1) * chans], k % 2, m, transpose=True
        )

    def wait_weights(j):
        for load in weight_loads(j):
            load.wait()

    def fields_of(i):
        return tuple(entry(field, i) for field in FIELDS)

    def run(sides, middles, i, fields):
        f = dict(zip(FIELDS, fields))

        received = f["recv"] != NONE

        @pl.when(received)
        def _():
            arrived(f["recv"])

            @pl.when(f["relay"] == 1)
            def _():
                relay_of(f["recv"]).start()

        source = f["rsrc"]

        def lhs(dy, r):
            return rounded[source, WIDTH * dy + r * rows_of:WIDTH * dy + (r + 1) * rows_of, :]

        def stream(k):
            for m in (0, 1):
                dy = order[m][k][0]
                total = sides[m] if k < 3 else middles[m]
                taken = range(BLOCKS) if k < 4 else range(m, BLOCKS, 2)
                for n, r in enumerate(taken):
                    pltpu.matmul_acc_lhs(total[r], lhs(dy, r), k % 2 if n == 0 else None)

        for m in (0, 1):
            push(f["w"], 1, m)
        stream(0)
        later = fields_of(i + 1)
        following = dict(zip(FIELDS, later))
        next_weight = jnp.logical_and(i + 1 < count, following["need"] > 0)

        @pl.when(received)
        def _():
            st[f["src"]] = rounded[source, WIDTH:WIDTH + cells, :].astype(f32)

        @pl.when(jnp.logical_or(i < COARSEN - 1, jnp.logical_or(next_weight, f["need"] > 0)))
        def _():
            @pl.when(i < COARSEN - 1)
            def _():
                wait_weights(i + 1)

            @pl.when(next_weight)
            def _():
                remote(w.at[0], w.at[COARSEN], extra_sem.at[0], recv_sem.at[WEIGHT], back).wait_recv()

            @pl.when(f["need"] == 1)
            def _():
                arrived(RHS)
                st[RHM] = rounded[RHS, WIDTH:WIDTH + cells, :].astype(f32)

        for k in range(1, 5):
            for m in (0, 1):
                if k < 4:
                    push(f["w"], k + 1, m)
            stream(k)
        for m in (0, 1):
            push(following["w"], 0, m)
        for r in range(BLOCKS):
            for m in (0, 1):
                t = pltpu.matmul_pop(sides[m][r])
                t = jnp.where(col == (0 if m else WIDTH - 1), 0.0, t)
                for h in (0, 1):
                    part[m, h, 8 + r * rows_of:8 + (r + 1) * rows_of, :] = t[:, h * half:(h + 1) * half]
        base[...] = st[f["src"]] + st[f["add"]]

        factor = jnp.where(f["factor"] == QUARTER, 0.25, jnp.where(f["factor"] == WHOLE, 1.0, 4.0))
        for r in range(BLOCKS):
            at = slice(r * rows_of, (r + 1) * rows_of)
            middle = pltpu.matmul_pop(middles[0][r]) + pltpu.matmul_pop(middles[1][r])
            side = jnp.concatenate([
                part[0, h, 7 + r * rows_of:7 + (r + 1) * rows_of, :]
                + part[1, h, 9 + r * rows_of:9 + (r + 1) * rows_of, :] for h in (0, 1)
            ], 1)
            new = base[at] + factor * jnp.tanh(middle + side)
            st[f["dst"], at] = new
            rounded[f["rdst"], WIDTH + r * rows_of:WIDTH + (r + 1) * rows_of, :] = new.astype(bf16)

        @pl.when(jnp.logical_and(
            jnp.logical_and(f["rdst"] > UNSENT, has_next), f["op"] != OWNER_0
        ))
        def _():
            message(f["rdst"], distance(f["by"])).start()

        op = f["op"]

        @pl.when(op != NOTHING)
        def _():
            @pl.when(op == PSI_OF_LEFT)
            def _():
                psi = st[LF] + 4.0 * (st[CC] - base[...])
                st[PSI] = psi
                st[QQ] = (st[CP] - psi) - st[CP]

            @pl.when(op == KEEP)
            def _():
                st[TT] = 4.0 * (st[CP] - base[...])

            @pl.when(op == START)
            def _():
                psi = st[LF] + st[TT]
                rhs = st[CP] + ((st[CP] - psi) - st[CP])
                first = psi + rhs
                st[CC] = first
                rounded_store(TO_FIRST, first)
                special(TO_FIRST, FIRST, 1).start()

            @pl.when(op == FIRST_POINT)
            def _():
                rounded_store(TO_FIRST, st[PSI] + st[RH])
                special(TO_FIRST, FIRST, 1).start()

            @pl.when(op == OWNER_0)
            def _():
                for r in range(4):
                    at = slice(r * cells // 4, (r + 1) * cells // 4)
                    cc, xi = st[CC, at], st[XZ, at]
                    psi = st[LF, at] + (cc - base[at])
                    solved = xi + ((cc - xi) + (st[RH, at] - (cc - psi)))
                    rounded[TO_FINAL, WIDTH + at.start:WIDTH + at.stop, :] = solved.astype(bf16)
                    st[PSI, at] = solved
                send_solved()
                for r in range(4):
                    at = slice(r * cells // 4, (r + 1) * cells // 4)
                    st[TT, at] = st[CC, at] - base[at]
                    st[CC, at] = st[PSI, at]

            @pl.when(jnp.logical_or(op == PUT_0, jnp.logical_or(op == START, op == OWNER_0)))
            def _():
                t = jnp.where(op == PUT_0, st[f["dst"]] - base[...], st[TT])
                out = st[LF] + 0.25 * t
                st[OUT] = out
                rounded_store(OUTB, out)

            put_at = jnp.where(op == PUT_1, 1, jnp.where(op == PUT_2, 2, 0))

            @pl.when(jnp.logical_and(op >= START, op <= OWNER_0))
            def _():
                put(put_at)

            @pl.when(op == OWNER)
            def _():
                arrived(CHANGE)
                for r in range(4):
                    at = slice(r * cells // 4, (r + 1) * cells // 4)
                    inner_at = slice(WIDTH + at.start, WIDTH + at.stop)
                    cc = st[CC, at]
                    change = rounded[CHANGE, inner_at, :].astype(f32)
                    second = st[RH, at] - (cc - st[PSI, at])
                    solved = change + ((cc - st[ZERO, at]) + second)
                    rounded[TO_SECOND, inner_at, :] = cc.astype(bf16)
                    rounded[TO_FINAL, inner_at, :] = solved.astype(bf16)
                    st[CC, at] = solved
                send_solved()

            @pl.when(op == CHANGES)
            def _():
                rounded_store(TO_CHANGE, st[XZ] - st[TMP])
                special(TO_CHANGE, CHANGE, COARSEN - 1).start()

        return later

    def loop(*totals):
        sides = (totals[:BLOCKS], totals[2 * BLOCKS:3 * BLOCKS])
        middles = (totals[BLOCKS:2 * BLOCKS], totals[3 * BLOCKS:])
        wait_weights(0)
        for load in weight_loads(3):
            load.start()
        for m in (0, 1):
            push(0, 0, m)
        lax.fori_loop(0, count, functools.partial(run, sides, middles), fields_of(0))
        for m in (0, 1):
            pltpu.matmul_acc_lhs(sides[m][0], rounded[CPB, 0:rows_of, :], 0)
            side_sum[0:rows_of, :] = pltpu.matmul_pop(sides[m][0])

    pl.run_scoped(
        loop, *[pltpu.ACC(m)((rows_of, chans), f32) for m in (0, 1) for _ in range(2 * BLOCKS)]
    )
    o_ref[COARSEN - 1] = st[CC].T

    def drain(copy, cond):
        @pl.when(cond)
        def _():
            copy.wait_send()

    relaxed = jnp.logical_or(
        jnp.logical_and(owner, lead_next), jnp.logical_and(phase == 1, group > 0)
    )
    drain(weight_to(back), jnp.logical_or(shares, owner_shares))
    drain(special(TO_LEFT, LEFT, back), has_next)
    drain(special(TO_RHS, RHS, back), shares)
    drain(special(TO_FIRST, FIRST, back), phase < 2)
    drain(special(TO_FINAL, FINAL, back), relaxed)
    drain(special(TO_SECOND, SECOND, back), relaxed)
    drain(special(TO_CHANGE, CHANGE, back), changes)
    drain(relay_of(FIRST), first_owner)
    drain(relay_of(FINAL), jnp.logical_and(lead, group > 0))
    drain(relay_of(SECOND), jnp.logical_and(phase == 1, group > 0))


def per_device(devices, inputs, guess, weights):
    chans, cells = inputs.shape
    return pl.pallas_call(
        functools.partial(kernel, devices),
        name="cycle",
        out_shape=pltpu.VMEM((COARSEN, chans, cells), jnp.float32),
        in_specs=[pl.BlockSpec(memory_space=pltpu.HBM)] * 3,
        out_specs=pl.BlockSpec(memory_space=pltpu.VMEM),
        scratch_shapes=[
            pltpu.VMEM((2, chans, cells), jnp.float32),
            pltpu.VMEM((COARSEN + 1,) + weights.shape[1:], jnp.bfloat16),
            pltpu.VMEM((STATES, cells, chans), jnp.float32),
            pltpu.VMEM((ROUNDED, cells + 2 * WIDTH, chans), jnp.bfloat16),
            pltpu.VMEM((2, 2, cells + 16, chans // 2), jnp.float32),
            pltpu.VMEM((cells, chans), jnp.float32),
            pltpu.VMEM((cells, chans), jnp.float32),
            pltpu.SemaphoreType.DMA((TO_RHS - TO_LEFT + 1,)),
            pltpu.SemaphoreType.DMA((FINAL - LEFT + 1,)),
            pltpu.SemaphoreType.DMA((1,)),
            pltpu.SemaphoreType.DMA((ROUNDED + 1,)),
            pltpu.SemaphoreType.DMA((2,)),
            pltpu.SemaphoreType.DMA((COARSEN, PIECES)),
        ],
        compiler_params=pltpu.CompilerParams(
            collective_id=0, has_side_effects=True, vmem_limit_bytes=56 * 2**20,
        ),
    )(*[pltpu.with_memory_space_constraint(a, pltpu.HBM) for a in (inputs, guess, weights)])


def solution(mesh):
    return jax.shard_map(
        functools.partial(per_device, mesh.shape["layer"]),
        mesh=mesh,
        in_specs=(P(None, "batch"), P("layer", None, "batch"), P("layer", None, None)),
        out_specs=P("layer", None, "batch"),
        check_vma=False,
    )
```

```python
import functools

import jax
import jax.numpy as jnp
from jax import lax
from jax.experimental import pallas as pl
from jax.experimental.pallas import tpu as pltpu
from jax.sharding import PartitionSpec as P

WIDTH = 16
COARSEN = 4
NONE = 15
PIECES = 2
BLOCKS = 8
ZERO, CP, LF, CC, RH, RHM, TT, PSI, QQ, XZ, OUT, TMP, DUMP = range(13)
STATES = 13
CPB, LFB, OUTB, CCB, TMPB, LEFT, FIRST, SECOND, FINAL, UNSENT = range(10)
TO_LEFT, TO_FIRST, TO_SECOND, TO_FINAL, TO_CHANGE, TO_RHS, CHANGE, RHS = range(10, 18)
ROUNDED = 18
WEIGHT = ROUNDED
NOTHING, PSI_OF_LEFT, FIRST_POINT, START, PUT_0, PUT_1, PUT_2, PUT_OUT, OWNER_0, OWNER, CHANGES, KEEP = range(12)
FIELDS = ("src", "dst", "w", "add", "factor", "rsrc", "rdst", "by", "recv", "relay", "need", "op")
BY_ONE, BY_TWO = 0, 1
QUARTER, WHOLE, FOUR = 0, 1, 2
ROUNDED_OF = {CP: CPB, LF: LFB, CC: CCB, OUT: OUTB, TMP: TMPB}


def step(src, dst, w, add=ZERO, factor=QUARTER, send=UNSENT, by=BY_ONE,
         recv=NONE, relay=0, need=0, op=NOTHING, rsrc=None):
    if rsrc is None:
        rsrc = ROUNDED_OF[src] if recv == NONE else recv
    rdst = ROUNDED_OF.get(dst, UNSENT) if send == UNSENT else send
    return dict(src=src, dst=dst, w=w, add=add, factor=factor, rsrc=rsrc, rdst=rdst,
                by=by, recv=recv, relay=relay, need=need, op=op)


def programs():
    def fine(send=UNSENT, first=NOTHING, op=NOTHING):
        return [step(CP, CP, 0, op=first), step(CP, CP, 1), step(CP, CP, 2),
                step(CP, CP, 3, send=send, op=op)]

    def again(send=UNSENT, op=NOTHING):
        return [step(LF, CC, 0, recv=LEFT, op=PSI_OF_LEFT), step(CC, CC, 1),
                step(CC, CC, 2), step(CC, RH, 3, add=QQ, send=send, op=op)]

    def whole(recv, dst, relay=0, need=0):
        return step(TMP, dst, COARSEN, add=RHM, factor=WHOLE, recv=recv, relay=relay, need=need)

    def own(src, dst, **kw):
        return step(src, dst, 0, add=RH, factor=WHOLE, **kw)

    last = [step(OUT, OUT, 1, op=PUT_1), step(OUT, OUT, 2, op=PUT_2)]
    body = fine(TO_LEFT) + again()
    mate = fine(TO_LEFT) + again(TO_RHS)
    final = [whole(FINAL, LF, relay=1)]
    owner_second = [whole(SECOND, TMP), step(TMP, PSI, 0, factor=WHOLE, op=OWNER)]
    relaxed = [whole(FIRST, TMP, need=1), own(TMP, CC)] + final + [
        step(LF, OUT, 0, op=PUT_OUT)]
    return {
        "start": fine(TO_LEFT, KEEP, START) + last,
        "lead_first": body + [own(LF, CC, recv=FIRST, send=TO_FIRST, by=BY_TWO, op=PUT_0)] + last,
        "mate_first": mate + [own(LF, CC, recv=FIRST, op=PUT_0)] + last,
        "owner_first": body + [
            step(TMP, XZ, 0, factor=FOUR), whole(FIRST, LF, relay=1, need=1),
            own(LF, CC, send=TO_SECOND, op=OWNER_0)] + last,
        "head": fine(TO_LEFT) + again(TO_RHS, FIRST_POINT) + [
            own(LF, CC, recv=FINAL, op=PUT_0),
            step(LF, XZ, COARSEN, factor=FOUR, need=2, rsrc=FINAL),
            step(TMP, TMP, COARSEN, factor=FOUR, recv=SECOND, op=CHANGES)] + last,
        "lead": body + [
            own(LF, TMP, recv=FIRST, send=TO_FIRST, by=BY_TWO),
            whole(FINAL, LF, relay=1, need=1),
            own(LF, CC, send=TO_FINAL, by=BY_TWO, op=PUT_0),
            whole(SECOND, TMP, relay=1),
            own(TMP, TMP, send=TO_SECOND, by=BY_TWO)] + last,
        "mate": mate + [own(LF, CC, recv=FINAL, op=PUT_0)] + last,
        "owner": body + relaxed + owner_second + last,
        "owner_last": body + relaxed + last + owner_second,
    }


def packed(values):
    words = []
    for start in (0, 8):
        word = sum(v << (4 * k) for k, v in enumerate(values[start:start + 8]))
        words.append(word - 2**32 if word >= 2**31 else word)
    return words


def kernel(
    devices, x_hbm, g_hbm, w_hbm, o_ref,
    xg, w, st, rounded, part, side_sum, base,
    send_sem, relay_sem, extra_sem, recv_sem, load_sem, weight_sem,
):
    f32, bf16 = jnp.float32, jnp.bfloat16
    p = lax.axis_index("layer")
    phase = lax.rem(p, COARSEN)
    owner = phase == COARSEN - 1
    group = lax.div(p, COARSEN)
    lead = lax.rem(p, 2) == 1
    mate = jnp.logical_not(lead)
    _, cells, chans = st.shape

    own_load = pltpu.make_async_copy(g_hbm.at[0], xg.at[0], load_sem.at[0])
    x_load = pltpu.make_async_copy(x_hbm, xg.at[0], load_sem.at[0])
    start_load = pltpu.make_async_copy(x_hbm, xg.at[1], load_sem.at[1])
    first_owner = jnp.logical_and(owner, group == 0)

    def weight_loads(j):
        rows = w.shape[1] // PIECES
        return [
            pltpu.make_async_copy(
                w_hbm.at[j, pl.ds(n * rows, rows)], w.at[j, pl.ds(n * rows, rows)],
                weight_sem.at[j, n],
            )
            for n in range(PIECES)
        ]

    @pl.when(p == 0)
    def _():
        x_load.start()

    @pl.when(p > 0)
    def _():
        own_load.start()

    for load in weight_loads(0) + weight_loads(1):
        load.start()

    @pl.when(first_owner)
    def _():
        start_load.start()

    barrier = pltpu.get_barrier_semaphore()

    def greet(by, cond):
        @pl.when(cond)
        def _():
            pl.semaphore_signal(
                barrier, inc=1, device_id={"layer": p + by},
                device_id_type=pl.DeviceIdType.MESH,
            )
        return cond.astype(jnp.int32)

    has_next = p < devices - 1
    lead_next = jnp.logical_and(lead, p + 2 < devices)
    last_owner = p + COARSEN >= devices
    greeted = (
        greet(1, has_next) + greet(-1, p > 0)
        + greet(COARSEN - 1, jnp.logical_and(phase == 0, group > 0))
        + greet(1 - COARSEN, jnp.logical_and(owner, group > 0))
        + greet(2, lead_next) + greet(-2, jnp.logical_and(lead, p >= 2))
    )
    shares = jnp.logical_and(mate, p > 0)
    owner_shares = jnp.logical_and(owner, group > 0)
    changes = jnp.logical_and(phase == 0, group > 0)

    roles = [
        ("start", p == 0),
        ("lead_first", jnp.logical_and(group == 0, phase == 1)),
        ("mate_first", jnp.logical_and(group == 0, phase == 2)),
        ("owner_first", first_owner),
        ("head", changes),
        ("lead", jnp.logical_and(group > 0, phase == 1)),
        ("mate", jnp.logical_and(group > 0, phase == 2)),
        ("owner_last", jnp.logical_and(owner, jnp.logical_and(group > 0, last_owner))),
    ]
    listed = programs()

    def chosen(value_of):
        value = jnp.int32(value_of(listed["owner"]))
        for name, cond in roles:
            value = jnp.where(cond, jnp.int32(value_of(listed[name])), value)
        return value

    count = chosen(len)
    words = {
        field: [
            chosen(lambda steps: packed([s[field] for s in steps])[half]) for half in (0, 1)
        ]
        for field in FIELDS
    }

    def entry(field, i):
        low, high = words[field]
        word = jnp.where(i < 8, low, high)
        return jnp.bitwise_and(
            lax.shift_right_logical(word, 4 * jnp.bitwise_and(i, 7)), 15
        )

    def remote(src, dst, ssem, rsem, by):
        return pltpu.make_async_remote_copy(
            src_ref=src, dst_ref=dst, send_sem=ssem, recv_sem=rsem,
            device_id={"layer": p + by}, device_id_type=pl.DeviceIdType.MESH,
        )

    def inner(slot):
        return rounded.at[slot, pl.ds(WIDTH, cells)]

    def landing(slot):
        return jnp.where(slot == TO_RHS, RHS, slot - (TO_LEFT - LEFT))

    def message(slot, by):
        to = landing(slot)
        return remote(inner(slot), inner(to), send_sem.at[slot - TO_LEFT], recv_sem.at[to], by)

    def relay_of(slot):
        return remote(inner(slot), inner(slot), relay_sem.at[slot - LEFT], recv_sem.at[slot], -1)

    back = jnp.where(p > 0, -1, 1)

    def arrived(slot):
        remote(inner(slot), inner(slot), extra_sem.at[0], recv_sem.at[slot], back).wait_recv()

    def weight_to(by):
        return remote(w_hbm.at[0], w.at[COARSEN], extra_sem.at[0], recv_sem.at[WEIGHT], by)

    def special(slot, to, by):
        return remote(inner(slot), inner(to), send_sem.at[slot - TO_LEFT], recv_sem.at[to], by)

    def rounded_store(slot, value):
        rounded[slot, WIDTH:WIDTH + cells, :] = value.astype(bf16)

    def distance(code):
        return jnp.where(code == BY_TWO, 2, 1)

    half = chans // 2
    rounded[:, 0:WIDTH, :] = jnp.zeros((ROUNDED, WIDTH, chans), bf16)
    rounded[:, WIDTH + cells:, :] = jnp.zeros((ROUNDED, WIDTH, chans), bf16)
    part[:, :, 0:8, :] = jnp.zeros((2, 2, 8, half), f32)
    part[:, :, 8 + cells:, :] = jnp.zeros((2, 2, 8, half), f32)
    st[ZERO] = jnp.zeros((cells, chans), f32)

    def put(slot, n):
        o_ref[n] = st[slot].T

    own_load.wait()
    for load in weight_loads(2):
        load.start()
    loaded = xg[0].T
    st[LF] = loaded
    st[CP] = loaded
    rounded_store(CPB, loaded)

    @pl.when(first_owner)
    def _():
        start_load.wait()
        start = xg[1].T
        st[TMP] = start
        rounded_store(TMPB, start)

    def send_solved():
        @pl.when(lead_next)
        def _():
            special(TO_FINAL, FINAL, 2).start()
            special(TO_SECOND, SECOND, 2).start()

    pl.semaphore_wait(barrier, greeted)

    @pl.when(shares)
    def _():
        weight_to(1).start()

    @pl.when(owner_shares)
    def _():
        weight_to(1 - COARSEN).start()

    rows_of = cells // BLOCKS
    col = lax.rem(lax.broadcasted_iota(jnp.int32, (rows_of, chans), 0), WIDTH)
    order = [
        [(1, 0), (0, 0), (2, 0), (0, 1), (1, 1)],
        [(1, 2), (0, 2), (2, 2), (2, 1), (1, 1)],
    ]

    def push(which, k, m):
        dy, dx = order[m][k]
        tap = 3 * dy + dx
        pltpu.matmul_push_rhs(
            w[which, :, tap * chans:(tap + 1) * chans], k % 2, m, transpose=True
        )

    def wait_weights(j):
        for load in weight_loads(j):
            load.wait()

    def fields_of(i):
        return tuple(entry(field, i) for field in FIELDS)

    def run(sides, middles, i, fields):
        f = dict(zip(FIELDS, fields))

        received = f["recv"] != NONE

        @pl.when(received)
        def _():
            arrived(f["recv"])

            @pl.when(f["relay"] == 1)
            def _():
                relay_of(f["recv"]).start()

        source = f["rsrc"]

        def lhs(dy, r):
            return rounded[source, WIDTH * dy + r * rows_of:WIDTH * dy + (r + 1) * rows_of, :]

        def stream(k):
            for m in (0, 1):
                dy = order[m][k][0]
                total = sides[m] if k < 3 else middles[m]
                taken = range(BLOCKS) if k < 4 else range(m, BLOCKS, 2)
                for n, r in enumerate(taken):
                    pltpu.matmul_acc_lhs(total[r], lhs(dy, r), k % 2 if n == 0 else None)

        for m in (0, 1):
            push(f["w"], 1, m)
        stream(0)
        later = fields_of(i + 1)
        following = dict(zip(FIELDS, later))
        next_weight = jnp.logical_and(i + 1 < count, following["need"] > 0)

        @pl.when(received)
        def _():
            st[f["src"]] = rounded[source, WIDTH:WIDTH + cells, :].astype(f32)

        @pl.when(jnp.logical_or(i < COARSEN - 1, jnp.logical_or(next_weight, f["need"] > 0)))
        def _():
            @pl.when(i < COARSEN - 1)
            def _():
                wait_weights(i + 1)

            @pl.when(next_weight)
            def _():
                remote(w.at[0], w.at[COARSEN], extra_sem.at[0], recv_sem.at[WEIGHT], back).wait_recv()

            @pl.when(f["need"] == 1)
            def _():
                arrived(RHS)
                st[RHM] = rounded[RHS, WIDTH:WIDTH + cells, :].astype(f32)

        for k in range(1, 5):
            for m in (0, 1):
                if k < 4:
                    push(f["w"], k + 1, m)
            stream(k)
        for m in (0, 1):
            push(following["w"], 0, m)
        for r in range(BLOCKS):
            for m in (0, 1):
                t = pltpu.matmul_pop(sides[m][r])
                t = jnp.where(col == (0 if m else WIDTH - 1), 0.0, t)
                for h in (0, 1):
                    part[m, h, 8 + r * rows_of:8 + (r + 1) * rows_of, :] = t[:, h * half:(h + 1) * half]
        base[...] = st[f["src"]] + st[f["add"]]

        factor = jnp.where(f["factor"] == QUARTER, 0.25, jnp.where(f["factor"] == WHOLE, 1.0, 4.0))
        for r in range(BLOCKS):
            at = slice(r * rows_of, (r + 1) * rows_of)
            middle = pltpu.matmul_pop(middles[0][r]) + pltpu.matmul_pop(middles[1][r])
            side = jnp.concatenate([
                part[0, h, 7 + r * rows_of:7 + (r + 1) * rows_of, :]
                + part[1, h, 9 + r * rows_of:9 + (r + 1) * rows_of, :] for h in (0, 1)
            ], 1)
            new = base[at] + factor * jnp.tanh(middle + side)
            st[f["dst"], at] = new
            rounded[f["rdst"], WIDTH + r * rows_of:WIDTH + (r + 1) * rows_of, :] = new.astype(bf16)

        @pl.when(jnp.logical_and(
            jnp.logical_and(f["rdst"] > UNSENT, has_next), f["op"] != OWNER_0
        ))
        def _():
            message(f["rdst"], distance(f["by"])).start()

        op = f["op"]

        @pl.when(op != NOTHING)
        def _():
            @pl.when(op == PSI_OF_LEFT)
            def _():
                psi = st[LF] + 4.0 * (st[CC] - base[...])
                st[PSI] = psi
                st[QQ] = (st[CP] - psi) - st[CP]

            @pl.when(op == KEEP)
            def _():
                st[TT] = 4.0 * (st[CP] - base[...])

            @pl.when(op == START)
            def _():
                psi = st[LF] + st[TT]
                rhs = st[CP] + ((st[CP] - psi) - st[CP])
                first = psi + rhs
                st[CC] = first
                rounded_store(TO_FIRST, first)
                special(TO_FIRST, FIRST, 1).start()

            @pl.when(op == FIRST_POINT)
            def _():
                rounded_store(TO_FIRST, st[PSI] + st[RH])
                special(TO_FIRST, FIRST, 1).start()

            @pl.when(op == OWNER_0)
            def _():
                for r in range(4):
                    at = slice(r * cells // 4, (r + 1) * cells // 4)
                    cc, xi = st[CC, at], st[XZ, at]
                    psi = st[LF, at] + (cc - base[at])
                    solved = xi + ((cc - xi) + (st[RH, at] - (cc - psi)))
                    rounded[TO_FINAL, WIDTH + at.start:WIDTH + at.stop, :] = solved.astype(bf16)
                    st[PSI, at] = solved
                send_solved()
                for r in range(4):
                    at = slice(r * cells // 4, (r + 1) * cells // 4)
                    st[TT, at] = st[CC, at] - base[at]
                    st[CC, at] = st[PSI, at]

            @pl.when(jnp.logical_or(op == PUT_0, jnp.logical_or(op == START, op == OWNER_0)))
            def _():
                t = jnp.where(op == PUT_0, st[f["dst"]] - base[...], st[TT])
                out = st[LF] + 0.25 * t
                st[OUT] = out
                rounded_store(OUTB, out)

            @pl.when(op == OWNER)
            def _():
                arrived(CHANGE)
                for r in range(4):
                    at = slice(r * cells // 4, (r + 1) * cells // 4)
                    inner_at = slice(WIDTH + at.start, WIDTH + at.stop)
                    cc = st[CC, at]
                    change = rounded[CHANGE, inner_at, :].astype(f32)
                    second = st[RH, at] - (cc - st[PSI, at])
                    solved = change + ((cc - st[ZERO, at]) + second)
                    rounded[TO_SECOND, inner_at, :] = cc.astype(bf16)
                    rounded[TO_FINAL, inner_at, :] = solved.astype(bf16)
                    st[CC, at] = solved
                send_solved()

            put_at = jnp.where(
                op == OWNER, COARSEN - 1, jnp.where(op == PUT_1, 1, jnp.where(op == PUT_2, 2, 0))
            )

            @pl.when(jnp.logical_and(op >= START, op <= OWNER))
            def _():
                put(jnp.where(op == OWNER, CC, OUT), put_at)

            @pl.when(op == CHANGES)
            def _():
                rounded_store(TO_CHANGE, st[XZ] - st[TMP])
                special(TO_CHANGE, CHANGE, COARSEN - 1).start()

        return later

    def loop(*totals):
        sides = (totals[:BLOCKS], totals[2 * BLOCKS:3 * BLOCKS])
        middles = (totals[BLOCKS:2 * BLOCKS], totals[3 * BLOCKS:])
        wait_weights(0)
        for load in weight_loads(3):
            load.start()
        for m in (0, 1):
            push(0, 0, m)
        lax.fori_loop(0, count, functools.partial(run, sides, middles), fields_of(0))
        for m in (0, 1):
            pltpu.matmul_acc_lhs(sides[m][0], rounded[CPB, 0:rows_of, :], 0)
        finish()
        for m in (0, 1):
            side_sum[0:rows_of, :] = pltpu.matmul_pop(sides[m][0])

    def finish():
        @pl.when(jnp.logical_not(jnp.logical_and(owner_shares, last_owner)))
        def _():
            put(CC, COARSEN - 1)

        def drain(copy, cond):
            @pl.when(cond)
            def _():
                copy.wait_send()

        relaxed = jnp.logical_or(
            jnp.logical_and(owner, lead_next), jnp.logical_and(phase == 1, group > 0)
        )
        drain(weight_to(back), jnp.logical_or(shares, owner_shares))
        drain(special(TO_LEFT, LEFT, back), has_next)
        drain(special(TO_RHS, RHS, back), shares)
        drain(special(TO_FIRST, FIRST, back), phase < 2)
        drain(special(TO_FINAL, FINAL, back), relaxed)
        drain(special(TO_SECOND, SECOND, back), relaxed)
        drain(special(TO_CHANGE, CHANGE, back), changes)
        drain(relay_of(FIRST), first_owner)
        drain(relay_of(FINAL), jnp.logical_and(lead, group > 0))
        drain(relay_of(SECOND), jnp.logical_and(phase == 1, group > 0))

    pl.run_scoped(
        loop, *[pltpu.ACC(m)((rows_of, chans), f32) for m in (0, 1) for _ in range(2 * BLOCKS)]
    )


def per_device(devices, inputs, guess, weights):
    chans, cells = inputs.shape
    return pl.pallas_call(
        functools.partial(kernel, devices),
        name="cycle",
        out_shape=pltpu.VMEM((COARSEN, chans, cells), jnp.float32),
        in_specs=[pl.BlockSpec(memory_space=pltpu.HBM)] * 3,
        out_specs=pl.BlockSpec(memory_space=pltpu.VMEM),
        scratch_shapes=[
            pltpu.VMEM((2, chans, cells), jnp.float32),
            pltpu.VMEM((COARSEN + 1,) + weights.shape[1:], jnp.bfloat16),
            pltpu.VMEM((STATES, cells, chans), jnp.float32),
            pltpu.VMEM((ROUNDED, cells + 2 * WIDTH, chans), jnp.bfloat16),
            pltpu.VMEM((2, 2, cells + 16, chans // 2), jnp.float32),
            pltpu.VMEM((cells, chans), jnp.float32),
            pltpu.VMEM((cells, chans), jnp.float32),
            pltpu.SemaphoreType.DMA((TO_RHS - TO_LEFT + 1,)),
            pltpu.SemaphoreType.DMA((FINAL - LEFT + 1,)),
            pltpu.SemaphoreType.DMA((1,)),
            pltpu.SemaphoreType.DMA((ROUNDED + 1,)),
            pltpu.SemaphoreType.DMA((2,)),
            pltpu.SemaphoreType.DMA((COARSEN, PIECES)),
        ],
        compiler_params=pltpu.CompilerParams(
            collective_id=0, has_side_effects=True, vmem_limit_bytes=56 * 2**20,
        ),
    )(*[pltpu.with_memory_space_constraint(a, pltpu.HBM) for a in (inputs, guess, weights)])


def solution(mesh):
    return jax.shard_map(
        functools.partial(per_device, mesh.shape["layer"]),
        mesh=mesh,
        in_specs=(P(None, "batch"), P("layer", None, "batch"), P("layer", None, None)),
        out_specs=P("layer", None, "batch"),
        check_vma=False,
    )
```

```python
import functools

import jax
import jax.numpy as jnp
from jax import lax
from jax.experimental import pallas as pl
from jax.experimental.pallas import tpu as pltpu
from jax.sharding import PartitionSpec as P

WIDTH = 16
COARSEN = 4
NONE = 15
PIECES = 2
BLOCKS = 8
ZERO, CP, LF, CC, RH, RHM, TT, PSI, QQ, XZ, OUT, TMP, DUMP = range(13)
STATES = 13
CPB, LFB, OUTB, CCB, TMPB, LEFT, FIRST, SECOND, FINAL, UNSENT = range(10)
TO_LEFT, TO_FIRST, TO_SECOND, TO_FINAL, TO_CHANGE, TO_RHS, CHANGE, RHS = range(10, 18)
ROUNDED = 18
WEIGHT = ROUNDED
NOTHING, PSI_OF_LEFT, FIRST_POINT, START, PUT_0, PUT_1, PUT_2, PUT_OUT, OWNER_0, OWNER, CHANGES, KEEP = range(12)
FIELDS = ("src", "dst", "w", "add", "factor", "rsrc", "rdst", "by", "recv", "relay", "need", "op")
BY_ONE, BY_TWO = 0, 1
QUARTER, WHOLE, FOUR = 0, 1, 2
ROUNDED_OF = {CP: CPB, LF: LFB, CC: CCB, OUT: OUTB, TMP: TMPB}


def step(src, dst, w, add=ZERO, factor=QUARTER, send=UNSENT, by=BY_ONE,
         recv=NONE, relay=0, need=0, op=NOTHING, rsrc=None):
    if rsrc is None:
        rsrc = ROUNDED_OF[src] if recv == NONE else recv
    rdst = ROUNDED_OF.get(dst, UNSENT) if send == UNSENT else send
    return dict(src=src, dst=dst, w=w, add=add, factor=factor, rsrc=rsrc, rdst=rdst,
                by=by, recv=recv, relay=relay, need=need, op=op)


def programs():
    def fine(send=UNSENT, first=NOTHING, op=NOTHING):
        return [step(CP, CP, 0, op=first), step(CP, CP, 1), step(CP, CP, 2),
                step(CP, CP, 3, send=send, op=op)]

    def again(send=UNSENT, op=NOTHING):
        return [step(LF, CC, 0, recv=LEFT, op=PSI_OF_LEFT), step(CC, CC, 1),
                step(CC, CC, 2), step(CC, RH, 3, add=QQ, send=send, op=op)]

    def whole(recv, dst, relay=0, need=0):
        return step(TMP, dst, COARSEN, add=RHM, factor=WHOLE, recv=recv, relay=relay, need=need)

    def own(src, dst, **kw):
        return step(src, dst, 0, add=RH, factor=WHOLE, **kw)

    last = [step(OUT, OUT, 1, op=PUT_1), step(OUT, OUT, 2, op=PUT_2)]
    body = fine(TO_LEFT) + again()
    mate = fine(TO_LEFT) + again(TO_RHS)
    final = [whole(FINAL, LF, relay=1)]
    owner_second = [whole(SECOND, TMP), step(TMP, PSI, 0, factor=WHOLE, op=OWNER)]
    relaxed = [whole(FIRST, TMP, need=1), own(TMP, CC)] + final + [
        step(LF, OUT, 0, op=PUT_OUT)]
    return {
        "start": fine(TO_LEFT, KEEP, START) + last,
        "lead_first": body + [own(LF, CC, recv=FIRST, send=TO_FIRST, by=BY_TWO, op=PUT_0)] + last,
        "mate_first": mate + [own(LF, CC, recv=FIRST, op=PUT_0)] + last,
        "owner_first": body + [
            step(TMP, XZ, 0, factor=FOUR), whole(FIRST, LF, relay=1, need=1),
            own(LF, CC, send=TO_SECOND, op=OWNER_0)] + last,
        "head": fine(TO_LEFT) + again(TO_RHS, FIRST_POINT) + [
            own(LF, CC, recv=FINAL),
            step(LF, XZ, COARSEN, factor=FOUR, need=2, rsrc=FINAL),
            step(TMP, TMP, COARSEN, factor=FOUR, recv=SECOND, op=CHANGES),
            step(LF, OUT, 0, rsrc=FINAL, op=PUT_OUT)] + last,
        "lead": body + [
            own(LF, TMP, recv=FIRST, send=TO_FIRST, by=BY_TWO),
            whole(FINAL, LF, relay=1, need=1),
            own(LF, CC, send=TO_FINAL, by=BY_TWO, op=PUT_0),
            whole(SECOND, TMP, relay=1),
            own(TMP, TMP, send=TO_SECOND, by=BY_TWO)] + last,
        "mate": mate + [own(LF, CC, recv=FINAL, op=PUT_0)] + last,
        "owner": body + relaxed + owner_second + last,
        "owner_last": body + relaxed + last + owner_second,
    }


def packed(values):
    words = []
    for start in (0, 8):
        word = sum(v << (4 * k) for k, v in enumerate(values[start:start + 8]))
        words.append(word - 2**32 if word >= 2**31 else word)
    return words


def kernel(
    devices, x_hbm, g_hbm, w_hbm, o_ref,
    xg, w, st, rounded, part, side_sum, base,
    send_sem, relay_sem, extra_sem, recv_sem, load_sem, weight_sem,
):
    f32, bf16 = jnp.float32, jnp.bfloat16
    p = lax.axis_index("layer")
    phase = lax.rem(p, COARSEN)
    owner = phase == COARSEN - 1
    group = lax.div(p, COARSEN)
    lead = lax.rem(p, 2) == 1
    mate = jnp.logical_not(lead)
    _, cells, chans = st.shape

    own_load = pltpu.make_async_copy(g_hbm.at[0], xg.at[0], load_sem.at[0])
    x_load = pltpu.make_async_copy(x_hbm, xg.at[0], load_sem.at[0])
    start_load = pltpu.make_async_copy(x_hbm, xg.at[1], load_sem.at[1])
    first_owner = jnp.logical_and(owner, group == 0)

    def weight_loads(j):
        rows = w.shape[1] // PIECES
        return [
            pltpu.make_async_copy(
                w_hbm.at[j, pl.ds(n * rows, rows)], w.at[j, pl.ds(n * rows, rows)],
                weight_sem.at[j, n],
            )
            for n in range(PIECES)
        ]

    @pl.when(p == 0)
    def _():
        x_load.start()

    @pl.when(p > 0)
    def _():
        own_load.start()

    for load in weight_loads(0) + weight_loads(1):
        load.start()

    @pl.when(first_owner)
    def _():
        start_load.start()

    barrier = pltpu.get_barrier_semaphore()

    def greet(by, cond):
        @pl.when(cond)
        def _():
            pl.semaphore_signal(
                barrier, inc=1, device_id={"layer": p + by},
                device_id_type=pl.DeviceIdType.MESH,
            )
        return cond.astype(jnp.int32)

    has_next = p < devices - 1
    lead_next = jnp.logical_and(lead, p + 2 < devices)
    last_owner = p + COARSEN >= devices
    greeted = (
        greet(1, has_next) + greet(-1, p > 0)
        + greet(COARSEN - 1, jnp.logical_and(phase == 0, group > 0))
        + greet(1 - COARSEN, jnp.logical_and(owner, group > 0))
        + greet(2, lead_next) + greet(-2, jnp.logical_and(lead, p >= 2))
    )
    shares = jnp.logical_and(mate, p > 0)
    owner_shares = jnp.logical_and(owner, group > 0)
    changes = jnp.logical_and(phase == 0, group > 0)

    roles = [
        ("start", p == 0),
        ("lead_first", jnp.logical_and(group == 0, phase == 1)),
        ("mate_first", jnp.logical_and(group == 0, phase == 2)),
        ("owner_first", first_owner),
        ("head", changes),
        ("lead", jnp.logical_and(group > 0, phase == 1)),
        ("mate", jnp.logical_and(group > 0, phase == 2)),
        ("owner_last", jnp.logical_and(owner, jnp.logical_and(group > 0, last_owner))),
    ]
    listed = programs()

    def chosen(value_of):
        value = jnp.int32(value_of(listed["owner"]))
        for name, cond in roles:
            value = jnp.where(cond, jnp.int32(value_of(listed[name])), value)
        return value

    count = chosen(len)
    words = {
        field: [
            chosen(lambda steps: packed([s[field] for s in steps])[half]) for half in (0, 1)
        ]
        for field in FIELDS
    }

    def entry(field, i):
        low, high = words[field]
        word = jnp.where(i < 8, low, high)
        return jnp.bitwise_and(
            lax.shift_right_logical(word, 4 * jnp.bitwise_and(i, 7)), 15
        )

    def remote(src, dst, ssem, rsem, by):
        return pltpu.make_async_remote_copy(
            src_ref=src, dst_ref=dst, send_sem=ssem, recv_sem=rsem,
            device_id={"layer": p + by}, device_id_type=pl.DeviceIdType.MESH,
        )

    def inner(slot):
        return rounded.at[slot, pl.ds(WIDTH, cells)]

    def landing(slot):
        return jnp.where(slot == TO_RHS, RHS, slot - (TO_LEFT - LEFT))

    def message(slot, by):
        to = landing(slot)
        return remote(inner(slot), inner(to), send_sem.at[slot - TO_LEFT], recv_sem.at[to], by)

    def relay_of(slot):
        return remote(inner(slot), inner(slot), relay_sem.at[slot - LEFT], recv_sem.at[slot], -1)

    back = jnp.where(p > 0, -1, 1)

    def arrived(slot):
        remote(inner(slot), inner(slot), extra_sem.at[0], recv_sem.at[slot], back).wait_recv()

    def weight_to(by):
        return remote(w_hbm.at[0], w.at[COARSEN], extra_sem.at[0], recv_sem.at[WEIGHT], by)

    def special(slot, to, by):
        return remote(inner(slot), inner(to), send_sem.at[slot - TO_LEFT], recv_sem.at[to], by)

    def rounded_store(slot, value):
        rounded[slot, WIDTH:WIDTH + cells, :] = value.astype(bf16)

    def distance(code):
        return jnp.where(code == BY_TWO, 2, 1)

    half = chans // 2
    rounded[:, 0:WIDTH, :] = jnp.zeros((ROUNDED, WIDTH, chans), bf16)
    rounded[:, WIDTH + cells:, :] = jnp.zeros((ROUNDED, WIDTH, chans), bf16)
    part[:, :, 0:8, :] = jnp.zeros((2, 2, 8, half), f32)
    part[:, :, 8 + cells:, :] = jnp.zeros((2, 2, 8, half), f32)
    st[ZERO] = jnp.zeros((cells, chans), f32)

    def put(slot, n):
        o_ref[n] = st[slot].T

    pl.semaphore_wait(barrier, greeted)

    @pl.when(owner_shares)
    def _():
        weight_to(1 - COARSEN).start()

    own_load.wait()
    for load in weight_loads(2):
        load.start()
    loaded = xg[0].T
    st[LF] = loaded
    st[CP] = loaded
    rounded_store(CPB, loaded)

    @pl.when(first_owner)
    def _():
        start_load.wait()
        start = xg[1].T
        st[TMP] = start
        rounded_store(TMPB, start)

    def send_solved():
        @pl.when(lead_next)
        def _():
            special(TO_FINAL, FINAL, 2).start()
            special(TO_SECOND, SECOND, 2).start()

    @pl.when(shares)
    def _():
        weight_to(1).start()

    rows_of = cells // BLOCKS
    col = lax.rem(lax.broadcasted_iota(jnp.int32, (rows_of, chans), 0), WIDTH)
    order = [
        [(1, 0), (0, 0), (2, 0), (0, 1), (1, 1)],
        [(1, 2), (0, 2), (2, 2), (2, 1), (1, 1)],
    ]

    def push(which, k, m):
        dy, dx = order[m][k]
        tap = 3 * dy + dx
        pltpu.matmul_push_rhs(
            w[which, :, tap * chans:(tap + 1) * chans], k % 2, m, transpose=True
        )

    def wait_weights(j):
        for load in weight_loads(j):
            load.wait()

    def fields_of(i):
        return tuple(entry(field, i) for field in FIELDS)

    def run(sides, middles, i, fields):
        f = dict(zip(FIELDS, fields))

        received = f["recv"] != NONE

        @pl.when(received)
        def _():
            arrived(f["recv"])

            @pl.when(f["relay"] == 1)
            def _():
                relay_of(f["recv"]).start()

        source = f["rsrc"]

        def lhs(dy, r):
            return rounded[source, WIDTH * dy + r * rows_of:WIDTH * dy + (r + 1) * rows_of, :]

        def stream(k):
            for m in (0, 1):
                dy = order[m][k][0]
                total = sides[m] if k < 3 else middles[m]
                taken = range(BLOCKS) if k < 4 else range(m, BLOCKS, 2)
                for n, r in enumerate(taken):
                    pltpu.matmul_acc_lhs(total[r], lhs(dy, r), k % 2 if n == 0 else None)

        for m in (0, 1):
            push(f["w"], 1, m)
        stream(0)
        later = fields_of(i + 1)
        following = dict(zip(FIELDS, later))
        next_weight = jnp.logical_and(i + 1 < count, following["need"] > 0)

        @pl.when(received)
        def _():
            st[f["src"]] = rounded[source, WIDTH:WIDTH + cells, :].astype(f32)

        @pl.when(jnp.logical_or(i < COARSEN - 1, jnp.logical_or(next_weight, f["need"] > 0)))
        def _():
            @pl.when(i < COARSEN - 1)
            def _():
                wait_weights(i + 1)

            @pl.when(next_weight)
            def _():
                remote(w.at[0], w.at[COARSEN], extra_sem.at[0], recv_sem.at[WEIGHT], back).wait_recv()

            @pl.when(f["need"] == 1)
            def _():
                arrived(RHS)
                st[RHM] = rounded[RHS, WIDTH:WIDTH + cells, :].astype(f32)

        for k in range(1, 5):
            for m in (0, 1):
                if k < 4:
                    push(f["w"], k + 1, m)
            stream(k)
        for m in (0, 1):
            push(following["w"], 0, m)
        for r in range(BLOCKS):
            for m in (0, 1):
                t = pltpu.matmul_pop(sides[m][r])
                t = jnp.where(col == (0 if m else WIDTH - 1), 0.0, t)
                for h in (0, 1):
                    part[m, h, 8 + r * rows_of:8 + (r + 1) * rows_of, :] = t[:, h * half:(h + 1) * half]
        base[...] = st[f["src"]] + st[f["add"]]

        factor = jnp.where(f["factor"] == QUARTER, 0.25, jnp.where(f["factor"] == WHOLE, 1.0, 4.0))
        for r in range(BLOCKS):
            at = slice(r * rows_of, (r + 1) * rows_of)
            middle = pltpu.matmul_pop(middles[0][r]) + pltpu.matmul_pop(middles[1][r])
            side = jnp.concatenate([
                part[0, h, 7 + r * rows_of:7 + (r + 1) * rows_of, :]
                + part[1, h, 9 + r * rows_of:9 + (r + 1) * rows_of, :] for h in (0, 1)
            ], 1)
            new = base[at] + factor * jnp.tanh(middle + side)
            st[f["dst"], at] = new
            rounded[f["rdst"], WIDTH + r * rows_of:WIDTH + (r + 1) * rows_of, :] = new.astype(bf16)

        @pl.when(jnp.logical_and(
            jnp.logical_and(f["rdst"] > UNSENT, has_next), f["op"] != OWNER_0
        ))
        def _():
            message(f["rdst"], distance(f["by"])).start()

        op = f["op"]

        @pl.when(op != NOTHING)
        def _():
            @pl.when(op == PSI_OF_LEFT)
            def _():
                psi = st[LF] + 4.0 * (st[CC] - base[...])
                st[PSI] = psi
                st[QQ] = (st[CP] - psi) - st[CP]

            @pl.when(op == KEEP)
            def _():
                st[TT] = 4.0 * (st[CP] - base[...])

            @pl.when(op == START)
            def _():
                psi = st[LF] + st[TT]
                rhs = st[CP] + ((st[CP] - psi) - st[CP])
                first = psi + rhs
                st[CC] = first
                rounded_store(TO_FIRST, first)
                special(TO_FIRST, FIRST, 1).start()

            @pl.when(op == FIRST_POINT)
            def _():
                rounded_store(TO_FIRST, st[PSI] + st[RH])
                special(TO_FIRST, FIRST, 1).start()

            @pl.when(op == OWNER_0)
            def _():
                for r in range(4):
                    at = slice(r * cells // 4, (r + 1) * cells // 4)
                    cc, xi = st[CC, at], st[XZ, at]
                    psi = st[LF, at] + (cc - base[at])
                    solved = xi + ((cc - xi) + (st[RH, at] - (cc - psi)))
                    rounded[TO_FINAL, WIDTH + at.start:WIDTH + at.stop, :] = solved.astype(bf16)
                    st[PSI, at] = solved
                send_solved()
                for r in range(4):
                    at = slice(r * cells // 4, (r + 1) * cells // 4)
                    st[TT, at] = st[CC, at] - base[at]
                    st[CC, at] = st[PSI, at]

            @pl.when(jnp.logical_or(op == PUT_0, jnp.logical_or(op == START, op == OWNER_0)))
            def _():
                t = jnp.where(op == PUT_0, st[f["dst"]] - base[...], st[TT])
                out = st[LF] + 0.25 * t
                st[OUT] = out
                rounded_store(OUTB, out)

            @pl.when(op == OWNER)
            def _():
                arrived(CHANGE)
                for r in range(4):
                    at = slice(r * cells // 4, (r + 1) * cells // 4)
                    inner_at = slice(WIDTH + at.start, WIDTH + at.stop)
                    cc = st[CC, at]
                    change = rounded[CHANGE, inner_at, :].astype(f32)
                    second = st[RH, at] - (cc - st[PSI, at])
                    solved = change + ((cc - st[ZERO, at]) + second)
                    rounded[TO_SECOND, inner_at, :] = cc.astype(bf16)
                    rounded[TO_FINAL, inner_at, :] = solved.astype(bf16)
                    st[CC, at] = solved
                send_solved()

            put_at = jnp.where(
                op == OWNER, COARSEN - 1, jnp.where(op == PUT_1, 1, jnp.where(op == PUT_2, 2, 0))
            )

            @pl.when(jnp.logical_and(op >= START, op <= OWNER))
            def _():
                put(jnp.where(op == OWNER, CC, OUT), put_at)

            @pl.when(op == CHANGES)
            def _():
                rounded_store(TO_CHANGE, st[XZ] - st[TMP])
                special(TO_CHANGE, CHANGE, COARSEN - 1).start()

        return later

    def loop(*totals):
        sides = (totals[:BLOCKS], totals[2 * BLOCKS:3 * BLOCKS])
        middles = (totals[BLOCKS:2 * BLOCKS], totals[3 * BLOCKS:])
        wait_weights(0)
        for load in weight_loads(3):
            load.start()
        for m in (0, 1):
            push(0, 0, m)
        lax.fori_loop(0, count, functools.partial(run, sides, middles), fields_of(0))
        for m in (0, 1):
            pltpu.matmul_acc_lhs(sides[m][0], rounded[CPB, 0:rows_of, :], 0)
        finish()
        for m in (0, 1):
            side_sum[0:rows_of, :] = pltpu.matmul_pop(sides[m][0])

    def finish():
        @pl.when(jnp.logical_not(jnp.logical_and(owner_shares, last_owner)))
        def _():
            put(CC, COARSEN - 1)

        def drain(copy, cond):
            @pl.when(cond)
            def _():
                copy.wait_send()

        relaxed = jnp.logical_or(
            jnp.logical_and(owner, lead_next), jnp.logical_and(phase == 1, group > 0)
        )
        drain(weight_to(back), jnp.logical_or(shares, owner_shares))
        drain(special(TO_LEFT, LEFT, back), has_next)
        drain(special(TO_RHS, RHS, back), shares)
        drain(special(TO_FIRST, FIRST, back), phase < 2)
        drain(special(TO_FINAL, FINAL, back), relaxed)
        drain(special(TO_SECOND, SECOND, back), relaxed)
        drain(special(TO_CHANGE, CHANGE, back), changes)
        drain(relay_of(FIRST), first_owner)
        drain(relay_of(FINAL), jnp.logical_and(lead, group > 0))
        drain(relay_of(SECOND), jnp.logical_and(phase == 1, group > 0))

    pl.run_scoped(
        loop, *[pltpu.ACC(m)((rows_of, chans), f32) for m in (0, 1) for _ in range(2 * BLOCKS)]
    )


def per_device(devices, inputs, guess, weights):
    chans, cells = inputs.shape
    return pl.pallas_call(
        functools.partial(kernel, devices),
        name="cycle",
        out_shape=pltpu.VMEM((COARSEN, chans, cells), jnp.float32),
        in_specs=[pl.BlockSpec(memory_space=pltpu.HBM)] * 3,
        out_specs=pl.BlockSpec(memory_space=pltpu.VMEM),
        scratch_shapes=[
            pltpu.VMEM((2, chans, cells), jnp.float32),
            pltpu.VMEM((COARSEN + 1,) + weights.shape[1:], jnp.bfloat16),
            pltpu.VMEM((STATES, cells, chans), jnp.float32),
            pltpu.VMEM((ROUNDED, cells + 2 * WIDTH, chans), jnp.bfloat16),
            pltpu.VMEM((2, 2, cells + 16, chans // 2), jnp.float32),
            pltpu.VMEM((cells, chans), jnp.float32),
            pltpu.VMEM((cells, chans), jnp.float32),
            pltpu.SemaphoreType.DMA((TO_RHS - TO_LEFT + 1,)),
            pltpu.SemaphoreType.DMA((FINAL - LEFT + 1,)),
            pltpu.SemaphoreType.DMA((1,)),
            pltpu.SemaphoreType.DMA((ROUNDED + 1,)),
            pltpu.SemaphoreType.DMA((2,)),
            pltpu.SemaphoreType.DMA((COARSEN, PIECES)),
        ],
        compiler_params=pltpu.CompilerParams(
            collective_id=0, has_side_effects=True, vmem_limit_bytes=56 * 2**20,
        ),
    )(*[pltpu.with_memory_space_constraint(a, pltpu.HBM) for a in (inputs, guess, weights)])


def solution(mesh):
    return jax.shard_map(
        functools.partial(per_device, mesh.shape["layer"]),
        mesh=mesh,
        in_specs=(P(None, "batch"), P("layer", None, "batch"), P("layer", None, None)),
        out_specs=P("layer", None, "batch"),
        check_vma=False,
    )
```

```python
import functools

import jax
import jax.numpy as jnp
from jax import lax
from jax.experimental import pallas as pl
from jax.experimental.pallas import tpu as pltpu
from jax.sharding import PartitionSpec as P

WIDTH = 16
COARSEN = 4
NONE = 15
PIECES = 2
BLOCKS = 8
ZERO, CP, LF, CC, RH, RHM, TT, PSI, QQ, XZ, OUT, TMP, DUMP = range(13)
STATES = 13
CPB, LFB, OUTB, CCB, TMPB, LEFT, FIRST, SECOND, FINAL, UNSENT = range(10)
TO_LEFT, TO_FIRST, TO_SECOND, TO_FINAL, TO_CHANGE, TO_RHS, CHANGE, RHS = range(10, 18)
ROUNDED = 18
WEIGHT = ROUNDED
NOTHING, PSI_OF_LEFT, FIRST_POINT, START, PUT_0, PUT_1, PUT_2, PUT_OUT, OWNER_0, OWNER, CHANGES, KEEP = range(12)
FIELDS = ("src", "dst", "w", "add", "factor", "rsrc", "rdst", "by", "recv", "relay", "need", "op")
BY_ONE, BY_TWO = 0, 1
QUARTER, WHOLE, FOUR = 0, 1, 2
ROUNDED_OF = {CP: CPB, LF: LFB, CC: CCB, OUT: OUTB, TMP: TMPB}


def step(src, dst, w, add=ZERO, factor=QUARTER, send=UNSENT, by=BY_ONE,
         recv=NONE, relay=0, need=0, op=NOTHING, rsrc=None):
    if rsrc is None:
        rsrc = ROUNDED_OF[src] if recv == NONE else recv
    rdst = ROUNDED_OF.get(dst, UNSENT) if send == UNSENT else send
    return dict(src=src, dst=dst, w=w, add=add, factor=factor, rsrc=rsrc, rdst=rdst,
                by=by, recv=recv, relay=relay, need=need, op=op)


def programs():
    def fine(send=UNSENT, first=NOTHING, op=NOTHING):
        return [step(CP, CP, 0, op=first), step(CP, CP, 1), step(CP, CP, 2),
                step(CP, CP, 3, send=send, op=op)]

    def again(send=UNSENT, op=NOTHING):
        return [step(LF, CC, 0, recv=LEFT, op=PSI_OF_LEFT), step(CC, CC, 1),
                step(CC, CC, 2), step(CC, RH, 3, add=QQ, send=send, op=op)]

    def whole(recv, dst, relay=0, need=0):
        return step(TMP, dst, COARSEN, add=RHM, factor=WHOLE, recv=recv, relay=relay, need=need)

    def own(src, dst, **kw):
        return step(src, dst, 0, add=RH, factor=WHOLE, **kw)

    last = [step(OUT, OUT, 1, op=PUT_1), step(OUT, OUT, 2, op=PUT_2)]
    body = fine(TO_LEFT) + again()
    mate = fine(TO_LEFT) + again(TO_RHS)
    final = [whole(FINAL, LF, relay=1)]
    owner_second = [whole(SECOND, TMP), step(TMP, PSI, 0, factor=WHOLE, op=OWNER)]
    relaxed = [whole(FIRST, TMP, need=1), own(TMP, CC)] + final + [
        step(LF, OUT, 0, op=PUT_OUT)]
    return {
        "start": fine(TO_LEFT, KEEP, START) + last,
        "lead_first": body + [own(LF, CC, recv=FIRST, send=TO_FIRST, by=BY_TWO, op=PUT_0)] + last,
        "mate_first": mate + [own(LF, CC, recv=FIRST, op=PUT_0)] + last,
        "owner_first": body + [
            step(TMP, XZ, 0, factor=FOUR), whole(FIRST, LF, relay=1, need=1),
            own(LF, CC, send=TO_SECOND, op=OWNER_0)] + last,
        "head": fine(TO_LEFT) + again(TO_RHS, FIRST_POINT) + [
            own(LF, CC, recv=FINAL),
            step(LF, XZ, COARSEN, factor=FOUR, need=2, rsrc=FINAL),
            step(TMP, TMP, COARSEN, factor=FOUR, recv=SECOND, op=CHANGES),
            step(LF, OUT, 0, rsrc=FINAL, op=PUT_OUT)] + last,
        "lead": body + [
            own(LF, TMP, recv=FIRST, send=TO_FIRST, by=BY_TWO),
            whole(FINAL, LF, relay=1, need=1),
            own(LF, CC, send=TO_FINAL, by=BY_TWO, op=PUT_0),
            whole(SECOND, TMP, relay=1),
            own(TMP, TMP, send=TO_SECOND, by=BY_TWO)] + last,
        "mate": mate + [own(LF, CC, recv=FINAL, op=PUT_0)] + last,
        "owner": body + relaxed + owner_second + last,
        "owner_last": body + relaxed + last + owner_second,
    }


def packed(values):
    words = []
    for start in (0, 8):
        word = sum(v << (4 * k) for k, v in enumerate(values[start:start + 8]))
        words.append(word - 2**32 if word >= 2**31 else word)
    return words


def kernel(
    devices, x_hbm, g_hbm, w_hbm, o_ref,
    xg, w, st, rounded, part, side_sum, base,
    send_sem, relay_sem, extra_sem, recv_sem, load_sem, weight_sem,
):
    f32, bf16 = jnp.float32, jnp.bfloat16
    p = lax.axis_index("layer")
    phase = lax.rem(p, COARSEN)
    owner = phase == COARSEN - 1
    group = lax.div(p, COARSEN)
    lead = lax.rem(p, 2) == 1
    mate = jnp.logical_not(lead)
    _, cells, chans = st.shape

    own_load = pltpu.make_async_copy(g_hbm.at[0], xg.at[0], load_sem.at[0])
    x_load = pltpu.make_async_copy(x_hbm, xg.at[0], load_sem.at[0])
    start_load = pltpu.make_async_copy(x_hbm, xg.at[1], load_sem.at[1])
    first_owner = jnp.logical_and(owner, group == 0)

    def weight_loads(j):
        rows = w.shape[1] // PIECES
        return [
            pltpu.make_async_copy(
                w_hbm.at[j, pl.ds(n * rows, rows)], w.at[j, pl.ds(n * rows, rows)],
                weight_sem.at[j, n],
            )
            for n in range(PIECES)
        ]

    @pl.when(p == 0)
    def _():
        x_load.start()

    @pl.when(p > 0)
    def _():
        own_load.start()

    for load in weight_loads(0) + weight_loads(1):
        load.start()

    @pl.when(first_owner)
    def _():
        start_load.start()

    barrier = pltpu.get_barrier_semaphore()

    def greet(by, cond):
        @pl.when(cond)
        def _():
            pl.semaphore_signal(
                barrier, inc=1, device_id={"layer": p + by},
                device_id_type=pl.DeviceIdType.MESH,
            )
        return cond.astype(jnp.int32)

    has_next = p < devices - 1
    lead_next = jnp.logical_and(lead, p + 2 < devices)
    last_owner = p + COARSEN >= devices
    greeted = (
        greet(1, has_next) + greet(-1, p > 0)
        + greet(COARSEN - 1, jnp.logical_and(phase == 0, group > 0))
        + greet(1 - COARSEN, jnp.logical_and(owner, group > 0))
        + greet(2, lead_next) + greet(-2, jnp.logical_and(lead, p >= 2))
    )
    shares = jnp.logical_and(mate, p > 0)
    owner_shares = jnp.logical_and(owner, group > 0)
    changes = jnp.logical_and(phase == 0, group > 0)

    roles = [
        ("start", p == 0),
        ("lead_first", jnp.logical_and(group == 0, phase == 1)),
        ("mate_first", jnp.logical_and(group == 0, phase == 2)),
        ("owner_first", first_owner),
        ("head", changes),
        ("lead", jnp.logical_and(group > 0, phase == 1)),
        ("mate", jnp.logical_and(group > 0, phase == 2)),
        ("owner_last", jnp.logical_and(owner, jnp.logical_and(group > 0, last_owner))),
    ]
    listed = programs()

    def chosen(value_of):
        value = jnp.int32(value_of(listed["owner"]))
        for name, cond in roles:
            value = jnp.where(cond, jnp.int32(value_of(listed[name])), value)
        return value

    count = chosen(len)
    words = {
        field: [
            chosen(lambda steps: packed([s[field] for s in steps])[half]) for half in (0, 1)
        ]
        for field in FIELDS
    }

    def entry(field, i):
        low, high = words[field]
        word = jnp.where(i < 8, low, high)
        return jnp.bitwise_and(
            lax.shift_right_logical(word, 4 * jnp.bitwise_and(i, 7)), 15
        )

    def remote(src, dst, ssem, rsem, by):
        return pltpu.make_async_remote_copy(
            src_ref=src, dst_ref=dst, send_sem=ssem, recv_sem=rsem,
            device_id={"layer": p + by}, device_id_type=pl.DeviceIdType.MESH,
        )

    def inner(slot):
        return rounded.at[slot, pl.ds(WIDTH, cells)]

    def landing(slot):
        return jnp.where(slot == TO_RHS, RHS, slot - (TO_LEFT - LEFT))

    def message(slot, by):
        to = landing(slot)
        return remote(inner(slot), inner(to), send_sem.at[slot - TO_LEFT], recv_sem.at[to], by)

    def relay_of(slot):
        return remote(inner(slot), inner(slot), relay_sem.at[slot - LEFT], recv_sem.at[slot], -1)

    back = jnp.where(p > 0, -1, 1)

    def arrived(slot):
        remote(inner(slot), inner(slot), extra_sem.at[0], recv_sem.at[slot], back).wait_recv()

    def weight_to(by):
        return remote(w_hbm.at[0], w.at[COARSEN], extra_sem.at[0], recv_sem.at[WEIGHT], by)

    def special(slot, to, by):
        return remote(inner(slot), inner(to), send_sem.at[slot - TO_LEFT], recv_sem.at[to], by)

    def rounded_store(slot, value):
        rounded[slot, WIDTH:WIDTH + cells, :] = value.astype(bf16)

    def distance(code):
        return jnp.where(code == BY_TWO, 2, 1)

    half = chans // 2
    rounded[:, 0:WIDTH, :] = jnp.zeros((ROUNDED, WIDTH, chans), bf16)
    rounded[:, WIDTH + cells:, :] = jnp.zeros((ROUNDED, WIDTH, chans), bf16)
    part[:, :, 0:8, :] = jnp.zeros((2, 2, 8, half), f32)
    part[:, :, 8 + cells:, :] = jnp.zeros((2, 2, 8, half), f32)
    st[ZERO] = jnp.zeros((cells, chans), f32)

    def put(slot, n):
        o_ref[n] = st[slot].T

    pl.semaphore_wait(barrier, greeted)

    @pl.when(owner_shares)
    def _():
        weight_to(1 - COARSEN).start()

    own_load.wait()
    for load in weight_loads(2):
        load.start()
    loaded = xg[0].T
    st[LF] = loaded
    st[CP] = loaded
    rounded_store(CPB, loaded)

    @pl.when(first_owner)
    def _():
        start_load.wait()
        start = xg[1].T
        st[TMP] = start
        rounded_store(TMPB, start)

    def send_solved():
        @pl.when(lead_next)
        def _():
            special(TO_FINAL, FINAL, 2).start()
            special(TO_SECOND, SECOND, 2).start()

    @pl.when(shares)
    def _():
        weight_to(1).start()

    rows_of = cells // BLOCKS
    col = lax.rem(lax.broadcasted_iota(jnp.int32, (rows_of, chans), 0), WIDTH)
    order = [
        [(1, 0), (0, 0), (2, 0), (0, 1), (1, 1)],
        [(1, 2), (0, 2), (2, 2), (2, 1), (1, 1)],
    ]

    def push(which, k, m):
        dy, dx = order[m][k]
        tap = 3 * dy + dx
        pltpu.matmul_push_rhs(
            w[which, :, tap * chans:(tap + 1) * chans], k % 2, m, transpose=True
        )

    def wait_weights(j):
        for load in weight_loads(j):
            load.wait()

    def fields_of(i):
        return tuple(entry(field, i) for field in FIELDS)

    def run(sides, middles, i, fields):
        f = dict(zip(FIELDS, fields))

        @pl.when(f["need"] == 1)
        def _():
            arrived(RHS)
            st[RHM] = rounded[RHS, WIDTH:WIDTH + cells, :].astype(f32)

        received = f["recv"] != NONE

        @pl.when(received)
        def _():
            arrived(f["recv"])

            @pl.when(f["relay"] == 1)
            def _():
                relay_of(f["recv"]).start()

        source = f["rsrc"]

        def lhs(dy, r):
            return rounded[source, WIDTH * dy + r * rows_of:WIDTH * dy + (r + 1) * rows_of, :]

        def stream(k):
            for m in (0, 1):
                dy = order[m][k][0]
                total = sides[m] if k < 3 else middles[m]
                taken = range(BLOCKS) if k < 4 else range(m, BLOCKS, 2)
                for n, r in enumerate(taken):
                    pltpu.matmul_acc_lhs(total[r], lhs(dy, r), k % 2 if n == 0 else None)

        for m in (0, 1):
            push(f["w"], 1, m)
        stream(0)
        later = fields_of(i + 1)
        following = dict(zip(FIELDS, later))
        next_weight = jnp.logical_and(i + 1 < count, following["need"] > 0)

        @pl.when(received)
        def _():
            st[f["src"]] = rounded[source, WIDTH:WIDTH + cells, :].astype(f32)

        @pl.when(jnp.logical_or(i < COARSEN - 1, next_weight))
        def _():
            @pl.when(i < COARSEN - 1)
            def _():
                wait_weights(i + 1)

            @pl.when(next_weight)
            def _():
                remote(w.at[0], w.at[COARSEN], extra_sem.at[0], recv_sem.at[WEIGHT], back).wait_recv()

        for k in range(1, 5):
            for m in (0, 1):
                if k < 4:
                    push(f["w"], k + 1, m)
            stream(k)
        for m in (0, 1):
            push(following["w"], 0, m)
        for r in range(BLOCKS):
            for m in (0, 1):
                t = pltpu.matmul_pop(sides[m][r])
                t = jnp.where(col == (0 if m else WIDTH - 1), 0.0, t)
                for h in (0, 1):
                    part[m, h, 8 + r * rows_of:8 + (r + 1) * rows_of, :] = t[:, h * half:(h + 1) * half]
        base[...] = st[f["src"]] + st[f["add"]]

        factor = jnp.where(f["factor"] == QUARTER, 0.25, jnp.where(f["factor"] == WHOLE, 1.0, 4.0))
        for r in range(BLOCKS):
            at = slice(r * rows_of, (r + 1) * rows_of)
            middle = pltpu.matmul_pop(middles[0][r]) + pltpu.matmul_pop(middles[1][r])
            side = jnp.concatenate([
                part[0, h, 7 + r * rows_of:7 + (r + 1) * rows_of, :]
                + part[1, h, 9 + r * rows_of:9 + (r + 1) * rows_of, :] for h in (0, 1)
            ], 1)
            new = base[at] + factor * jnp.tanh(middle + side)
            st[f["dst"], at] = new
            rounded[f["rdst"], WIDTH + r * rows_of:WIDTH + (r + 1) * rows_of, :] = new.astype(bf16)

        @pl.when(jnp.logical_and(
            jnp.logical_and(f["rdst"] > UNSENT, has_next), f["op"] != OWNER_0
        ))
        def _():
            message(f["rdst"], distance(f["by"])).start()

        op = f["op"]

        @pl.when(op != NOTHING)
        def _():
            @pl.when(op == PSI_OF_LEFT)
            def _():
                psi = st[LF] + 4.0 * (st[CC] - base[...])
                st[QQ] = (st[CP] - psi) - st[CP]

            @pl.when(op == KEEP)
            def _():
                st[TT] = 4.0 * (st[CP] - base[...])

            @pl.when(op == START)
            def _():
                psi = st[LF] + st[TT]
                rhs = st[CP] + ((st[CP] - psi) - st[CP])
                first = psi + rhs
                st[CC] = first
                rounded_store(TO_FIRST, first)
                special(TO_FIRST, FIRST, 1).start()

            @pl.when(op == FIRST_POINT)
            def _():
                rounded_store(TO_FIRST, (st[CP] - (st[QQ] + st[CP])) + st[RH])
                special(TO_FIRST, FIRST, 1).start()

            @pl.when(op == OWNER_0)
            def _():
                for r in range(4):
                    at = slice(r * cells // 4, (r + 1) * cells // 4)
                    cc, xi = st[CC, at], st[XZ, at]
                    psi = st[LF, at] + (cc - base[at])
                    solved = xi + ((cc - xi) + (st[RH, at] - (cc - psi)))
                    rounded[TO_FINAL, WIDTH + at.start:WIDTH + at.stop, :] = solved.astype(bf16)
                    st[PSI, at] = solved
                send_solved()
                for r in range(4):
                    at = slice(r * cells // 4, (r + 1) * cells // 4)
                    st[TT, at] = st[CC, at] - base[at]
                    st[CC, at] = st[PSI, at]

            @pl.when(jnp.logical_or(op == PUT_0, jnp.logical_or(op == START, op == OWNER_0)))
            def _():
                t = jnp.where(op == PUT_0, st[f["dst"]] - base[...], st[TT])
                out = st[LF] + 0.25 * t
                st[OUT] = out
                rounded_store(OUTB, out)

            @pl.when(op == OWNER)
            def _():
                arrived(CHANGE)
                for r in range(4):
                    at = slice(r * cells // 4, (r + 1) * cells // 4)
                    inner_at = slice(WIDTH + at.start, WIDTH + at.stop)
                    cc = st[CC, at]
                    change = rounded[CHANGE, inner_at, :].astype(f32)
                    second = st[RH, at] - (cc - st[PSI, at])
                    solved = change + ((cc - st[ZERO, at]) + second)
                    rounded[TO_SECOND, inner_at, :] = cc.astype(bf16)
                    rounded[TO_FINAL, inner_at, :] = solved.astype(bf16)
                    st[CC, at] = solved
                send_solved()

            put_at = jnp.where(
                op == OWNER, COARSEN - 1, jnp.where(op == PUT_1, 1, jnp.where(op == PUT_2, 2, 0))
            )

            @pl.when(jnp.logical_and(op >= START, op <= OWNER))
            def _():
                put(jnp.where(op == OWNER, CC, OUT), put_at)

            @pl.when(op == CHANGES)
            def _():
                rounded_store(TO_CHANGE, st[XZ] - st[TMP])
                special(TO_CHANGE, CHANGE, COARSEN - 1).start()

        return later

    def loop(*totals):
        sides = (totals[:BLOCKS], totals[2 * BLOCKS:3 * BLOCKS])
        middles = (totals[BLOCKS:2 * BLOCKS], totals[3 * BLOCKS:])
        wait_weights(0)
        for load in weight_loads(3):
            load.start()
        for m in (0, 1):
            push(0, 0, m)
        lax.fori_loop(0, count, functools.partial(run, sides, middles), fields_of(0))
        for m in (0, 1):
            pltpu.matmul_acc_lhs(sides[m][0], rounded[CPB, 0:rows_of, :], 0)
        finish()
        for m in (0, 1):
            side_sum[0:rows_of, :] = pltpu.matmul_pop(sides[m][0])

    def finish():
        @pl.when(jnp.logical_not(jnp.logical_and(owner_shares, last_owner)))
        def _():
            put(CC, COARSEN - 1)

        def drain(copy, cond):
            @pl.when(cond)
            def _():
                copy.wait_send()

        relaxed = jnp.logical_or(
            jnp.logical_and(owner, lead_next), jnp.logical_and(phase == 1, group > 0)
        )
        drain(weight_to(back), jnp.logical_or(shares, owner_shares))
        drain(special(TO_LEFT, LEFT, back), has_next)
        drain(special(TO_RHS, RHS, back), shares)
        drain(special(TO_FIRST, FIRST, back), phase < 2)
        drain(special(TO_FINAL, FINAL, back), relaxed)
        drain(special(TO_SECOND, SECOND, back), relaxed)
        drain(special(TO_CHANGE, CHANGE, back), changes)
        drain(relay_of(FIRST), first_owner)
        drain(relay_of(FINAL), jnp.logical_and(lead, group > 0))
        drain(relay_of(SECOND), jnp.logical_and(phase == 1, group > 0))

    pl.run_scoped(
        loop, *[pltpu.ACC(m)((rows_of, chans), f32) for m in (0, 1) for _ in range(2 * BLOCKS)]
    )


def per_device(devices, inputs, guess, weights):
    chans, cells = inputs.shape
    return pl.pallas_call(
        functools.partial(kernel, devices),
        name="cycle",
        out_shape=pltpu.VMEM((COARSEN, chans, cells), jnp.float32),
        in_specs=[pl.BlockSpec(memory_space=pltpu.HBM)] * 3,
        out_specs=pl.BlockSpec(memory_space=pltpu.VMEM),
        scratch_shapes=[
            pltpu.VMEM((2, chans, cells), jnp.float32),
            pltpu.VMEM((COARSEN + 1,) + weights.shape[1:], jnp.bfloat16),
            pltpu.VMEM((STATES, cells, chans), jnp.float32),
            pltpu.VMEM((ROUNDED, cells + 2 * WIDTH, chans), jnp.bfloat16),
            pltpu.VMEM((2, 2, cells + 16, chans // 2), jnp.float32),
            pltpu.VMEM((cells, chans), jnp.float32),
            pltpu.VMEM((cells, chans), jnp.float32),
            pltpu.SemaphoreType.DMA((TO_RHS - TO_LEFT + 1,)),
            pltpu.SemaphoreType.DMA((FINAL - LEFT + 1,)),
            pltpu.SemaphoreType.DMA((1,)),
            pltpu.SemaphoreType.DMA((ROUNDED + 1,)),
            pltpu.SemaphoreType.DMA((2,)),
            pltpu.SemaphoreType.DMA((COARSEN, PIECES)),
        ],
        compiler_params=pltpu.CompilerParams(
            collective_id=0, has_side_effects=True, vmem_limit_bytes=56 * 2**20,
        ),
    )(*[pltpu.with_memory_space_constraint(a, pltpu.HBM) for a in (inputs, guess, weights)])


def solution(mesh):
    return jax.shard_map(
        functools.partial(per_device, mesh.shape["layer"]),
        mesh=mesh,
        in_specs=(P(None, "batch"), P("layer", None, "batch"), P("layer", None, None)),
        out_specs=P("layer", None, "batch"),
        check_vma=False,
    )
```

```python
import functools

import jax
import jax.numpy as jnp
from jax import lax
from jax.experimental import pallas as pl
from jax.experimental.pallas import tpu as pltpu
from jax.sharding import PartitionSpec as P

WIDTH = 16
COARSEN = 4
NONE = 15
PIECES = 2
BLOCKS = 8
ZERO, CP, LF, CC, RH, RHM, TT, PSI, QQ, XZ, OUT, TMP, DUMP = range(13)
STATES = 13
CPB, LFB, OUTB, CCB, TMPB, LEFT, FIRST, SECOND, FINAL, UNSENT = range(10)
TO_LEFT, TO_FIRST, TO_SECOND, TO_FINAL, TO_CHANGE, TO_RHS, CHANGE, RHS = range(10, 18)
ROUNDED = 18
WEIGHT = ROUNDED
NOTHING, PSI_OF_LEFT, FIRST_POINT, START, PUT_0, PUT_1, PUT_2, PUT_OUT, OWNER_0, OWNER, CHANGES, KEEP = range(12)
FIELDS = ("src", "dst", "w", "add", "factor", "rsrc", "rdst", "by", "recv", "relay", "need", "op")
BY_ONE, BY_TWO = 0, 1
QUARTER, WHOLE, FOUR = 0, 1, 2
ROUNDED_OF = {CP: CPB, LF: LFB, CC: CCB, OUT: OUTB, TMP: TMPB}


def step(src, dst, w, add=ZERO, factor=QUARTER, send=UNSENT, by=BY_ONE,
         recv=NONE, relay=0, need=0, op=NOTHING, rsrc=None):
    if rsrc is None:
        rsrc = ROUNDED_OF[src] if recv == NONE else recv
    rdst = ROUNDED_OF.get(dst, UNSENT) if send == UNSENT else send
    return dict(src=src, dst=dst, w=w, add=add, factor=factor, rsrc=rsrc, rdst=rdst,
                by=by, recv=recv, relay=relay, need=need, op=op)


def programs():
    def fine(send=UNSENT, first=NOTHING, op=NOTHING):
        return [step(CP, CP, 0, op=first), step(CP, CP, 1), step(CP, CP, 2),
                step(CP, CP, 3, send=send, op=op)]

    def again(send=UNSENT, op=NOTHING):
        return [step(LF, CC, 0, recv=LEFT, op=PSI_OF_LEFT), step(CC, CC, 1),
                step(CC, CC, 2), step(CC, RH, 3, add=QQ, send=send, op=op)]

    def whole(recv, dst, relay=0, need=0):
        return step(TMP, dst, COARSEN, add=RHM, factor=WHOLE, recv=recv, relay=relay, need=need)

    def own(src, dst, **kw):
        return step(src, dst, 0, add=RH, factor=WHOLE, **kw)

    last = [step(OUT, OUT, 1, op=PUT_1), step(OUT, OUT, 2, op=PUT_2)]
    body = fine(TO_LEFT) + again()
    mate = fine(TO_LEFT) + again(TO_RHS)
    final = [whole(FINAL, LF, relay=1)]
    owner_second = [whole(SECOND, TMP), step(TMP, PSI, 0, factor=WHOLE, op=OWNER)]
    relaxed = [whole(FIRST, TMP, need=1), own(TMP, CC)] + final + [
        step(LF, OUT, 0, op=PUT_OUT)]
    return {
        "start": fine(TO_LEFT, KEEP, START) + last,
        "lead_first": body + [own(LF, CC, recv=FIRST, send=TO_FIRST, by=BY_TWO, op=PUT_0)] + last,
        "mate_first": mate + [own(LF, CC, recv=FIRST, op=PUT_0)] + last,
        "owner_first": body + [
            step(TMP, XZ, 0, factor=FOUR), whole(FIRST, LF, relay=1, need=1),
            own(LF, CC, send=TO_SECOND, op=OWNER_0)] + last,
        "head": fine(TO_LEFT) + again(TO_RHS, FIRST_POINT) + [
            own(LF, CC, recv=FINAL),
            step(LF, XZ, COARSEN, factor=FOUR, need=2, rsrc=FINAL),
            step(TMP, TMP, COARSEN, factor=FOUR, recv=SECOND, op=CHANGES),
            step(LF, OUT, 0, rsrc=FINAL, op=PUT_OUT)] + last,
        "lead": body + [
            own(LF, TMP, recv=FIRST, send=TO_FIRST, by=BY_TWO),
            whole(FINAL, LF, relay=1, need=1),
            own(LF, CC, send=TO_FINAL, by=BY_TWO, op=PUT_0),
            whole(SECOND, TMP, relay=1),
            own(TMP, TMP, send=TO_SECOND, by=BY_TWO)] + last,
        "mate": mate + [own(LF, CC, recv=FINAL, op=PUT_0)] + last,
        "owner": body + relaxed + owner_second + last,
        "owner_last": body + relaxed + last + owner_second,
    }


def packed(values):
    words = []
    for start in (0, 8):
        word = sum(v << (4 * k) for k, v in enumerate(values[start:start + 8]))
        words.append(word - 2**32 if word >= 2**31 else word)
    return words


def kernel(
    devices, x_hbm, g_hbm, w_hbm, o_ref,
    xg, w, st, rounded, part, side_sum, base,
    send_sem, relay_sem, extra_sem, recv_sem, load_sem, weight_sem,
):
    f32, bf16 = jnp.float32, jnp.bfloat16
    p = lax.axis_index("layer")
    phase = lax.rem(p, COARSEN)
    owner = phase == COARSEN - 1
    group = lax.div(p, COARSEN)
    lead = lax.rem(p, 2) == 1
    mate = jnp.logical_not(lead)
    _, cells, chans = st.shape

    own_load = pltpu.make_async_copy(g_hbm.at[0], xg.at[0], load_sem.at[0])
    x_load = pltpu.make_async_copy(x_hbm, xg.at[0], load_sem.at[0])
    start_load = pltpu.make_async_copy(x_hbm, xg.at[1], load_sem.at[1])
    first_owner = jnp.logical_and(owner, group == 0)

    def weight_loads(j):
        rows = w.shape[1] // PIECES
        return [
            pltpu.make_async_copy(
                w_hbm.at[j, pl.ds(n * rows, rows)], w.at[j, pl.ds(n * rows, rows)],
                weight_sem.at[j, n],
            )
            for n in range(PIECES)
        ]

    @pl.when(p == 0)
    def _():
        x_load.start()

    @pl.when(p > 0)
    def _():
        own_load.start()

    for load in weight_loads(0) + weight_loads(1):
        load.start()

    @pl.when(first_owner)
    def _():
        start_load.start()

    barrier = pltpu.get_barrier_semaphore()

    def greet(by, cond):
        @pl.when(cond)
        def _():
            pl.semaphore_signal(
                barrier, inc=1, device_id={"layer": p + by},
                device_id_type=pl.DeviceIdType.MESH,
            )
        return cond.astype(jnp.int32)

    has_next = p < devices - 1
    lead_next = jnp.logical_and(lead, p + 2 < devices)
    last_owner = p + COARSEN >= devices
    greeted = (
        greet(1, has_next) + greet(-1, p > 0)
        + greet(COARSEN - 1, jnp.logical_and(phase == 0, group > 0))
        + greet(1 - COARSEN, jnp.logical_and(owner, group > 0))
        + greet(2, lead_next) + greet(-2, jnp.logical_and(lead, p >= 2))
    )
    shares = jnp.logical_and(mate, p > 0)
    owner_shares = jnp.logical_and(owner, group > 0)
    changes = jnp.logical_and(phase == 0, group > 0)

    roles = [
        ("start", p == 0),
        ("lead_first", jnp.logical_and(group == 0, phase == 1)),
        ("mate_first", jnp.logical_and(group == 0, phase == 2)),
        ("owner_first", first_owner),
        ("head", changes),
        ("lead", jnp.logical_and(group > 0, phase == 1)),
        ("mate", jnp.logical_and(group > 0, phase == 2)),
        ("owner_last", jnp.logical_and(owner, jnp.logical_and(group > 0, last_owner))),
    ]
    listed = programs()

    def chosen(value_of):
        value = jnp.int32(value_of(listed["owner"]))
        for name, cond in roles:
            value = jnp.where(cond, jnp.int32(value_of(listed[name])), value)
        return value

    count = chosen(len)
    words = {
        field: [
            chosen(lambda steps: packed([s[field] for s in steps])[half]) for half in (0, 1)
        ]
        for field in FIELDS
    }

    def entry(field, i):
        low, high = words[field]
        word = jnp.where(i < 8, low, high)
        return jnp.bitwise_and(
            lax.shift_right_logical(word, 4 * jnp.bitwise_and(i, 7)), 15
        )

    def remote(src, dst, ssem, rsem, by):
        return pltpu.make_async_remote_copy(
            src_ref=src, dst_ref=dst, send_sem=ssem, recv_sem=rsem,
            device_id={"layer": p + by}, device_id_type=pl.DeviceIdType.MESH,
        )

    def inner(slot):
        return rounded.at[slot, pl.ds(WIDTH, cells)]

    def landing(slot):
        return jnp.where(slot == TO_RHS, RHS, slot - (TO_LEFT - LEFT))

    def message(slot, by):
        to = landing(slot)
        return remote(inner(slot), inner(to), send_sem.at[slot - TO_LEFT], recv_sem.at[to], by)

    def relay_of(slot):
        return remote(inner(slot), inner(slot), relay_sem.at[slot - LEFT], recv_sem.at[slot], -1)

    back = jnp.where(p > 0, -1, 1)

    def arrived(slot):
        remote(inner(slot), inner(slot), extra_sem.at[0], recv_sem.at[slot], back).wait_recv()

    def weight_to(by):
        return remote(w_hbm.at[0], w.at[COARSEN], extra_sem.at[0], recv_sem.at[WEIGHT], by)

    def special(slot, to, by):
        return remote(inner(slot), inner(to), send_sem.at[slot - TO_LEFT], recv_sem.at[to], by)

    def rounded_store(slot, value):
        rounded[slot, WIDTH:WIDTH + cells, :] = value.astype(bf16)

    def distance(code):
        return jnp.where(code == BY_TWO, 2, 1)

    half = chans // 2
    rounded[:, 0:WIDTH, :] = jnp.zeros((ROUNDED, WIDTH, chans), bf16)
    rounded[:, WIDTH + cells:, :] = jnp.zeros((ROUNDED, WIDTH, chans), bf16)
    part[:, :, 0:8, :] = jnp.zeros((2, 2, 8, half), f32)
    part[:, :, 8 + cells:, :] = jnp.zeros((2, 2, 8, half), f32)
    st[ZERO] = jnp.zeros((cells, chans), f32)

    def put(slot, n):
        o_ref[n] = st[slot].T

    pl.semaphore_wait(barrier, greeted)

    @pl.when(owner_shares)
    def _():
        weight_to(1 - COARSEN).start()

    own_load.wait()
    for load in weight_loads(2):
        load.start()
    loaded = xg[0].T
    st[LF] = loaded
    st[CP] = loaded
    rounded_store(CPB, loaded)

    @pl.when(first_owner)
    def _():
        start_load.wait()
        start = xg[1].T
        st[TMP] = start
        rounded_store(TMPB, start)

    def send_solved():
        @pl.when(lead_next)
        def _():
            special(TO_FINAL, FINAL, 2).start()
            special(TO_SECOND, SECOND, 2).start()

    rows_of = cells // BLOCKS
    col = lax.rem(lax.broadcasted_iota(jnp.int32, (rows_of, chans), 0), WIDTH)
    order = [
        [(1, 0), (0, 0), (2, 0), (0, 1), (1, 1)],
        [(1, 2), (0, 2), (2, 2), (2, 1), (1, 1)],
    ]

    def push(which, k, m):
        dy, dx = order[m][k]
        tap = 3 * dy + dx
        pltpu.matmul_push_rhs(
            w[which, :, tap * chans:(tap + 1) * chans], k % 2, m, transpose=True
        )

    def wait_weights(j):
        for load in weight_loads(j):
            load.wait()

    def fields_of(i):
        return tuple(entry(field, i) for field in FIELDS)

    def run(sides, middles, i, fields):
        f = dict(zip(FIELDS, fields))

        @pl.when(jnp.logical_and(shares, i == 1))
        def _():
            weight_to(1).start()

        @pl.when(f["need"] == 1)
        def _():
            arrived(RHS)
            st[RHM] = rounded[RHS, WIDTH:WIDTH + cells, :].astype(f32)

        received = f["recv"] != NONE

        @pl.when(received)
        def _():
            arrived(f["recv"])

            @pl.when(f["relay"] == 1)
            def _():
                relay_of(f["recv"]).start()

        source = f["rsrc"]

        def lhs(dy, r):
            return rounded[source, WIDTH * dy + r * rows_of:WIDTH * dy + (r + 1) * rows_of, :]

        def stream(k):
            for m in (0, 1):
                dy = order[m][k][0]
                total = sides[m] if k < 3 else middles[m]
                taken = range(BLOCKS) if k < 4 else range(m, BLOCKS, 2)
                for n, r in enumerate(taken):
                    pltpu.matmul_acc_lhs(total[r], lhs(dy, r), k % 2 if n == 0 else None)

        for m in (0, 1):
            push(f["w"], 1, m)
        stream(0)
        later = fields_of(i + 1)
        following = dict(zip(FIELDS, later))
        next_weight = jnp.logical_and(i + 1 < count, following["need"] > 0)

        @pl.when(received)
        def _():
            st[f["src"]] = rounded[source, WIDTH:WIDTH + cells, :].astype(f32)

        @pl.when(jnp.logical_or(i < COARSEN - 1, next_weight))
        def _():
            @pl.when(i < COARSEN - 1)
            def _():
                wait_weights(i + 1)

            @pl.when(next_weight)
            def _():
                remote(w.at[0], w.at[COARSEN], extra_sem.at[0], recv_sem.at[WEIGHT], back).wait_recv()

        for k in range(1, 5):
            for m in (0, 1):
                if k < 4:
                    push(f["w"], k + 1, m)
            stream(k)
        for m in (0, 1):
            push(following["w"], 0, m)
        for r in range(BLOCKS):
            for m in (0, 1):
                t = pltpu.matmul_pop(sides[m][r])
                t = jnp.where(col == (0 if m else WIDTH - 1), 0.0, t)
                for h in (0, 1):
                    part[m, h, 8 + r * rows_of:8 + (r + 1) * rows_of, :] = t[:, h * half:(h + 1) * half]
        base[...] = st[f["src"]] + st[f["add"]]

        factor = jnp.where(f["factor"] == QUARTER, 0.25, jnp.where(f["factor"] == WHOLE, 1.0, 4.0))
        for r in range(BLOCKS):
            at = slice(r * rows_of, (r + 1) * rows_of)
            middle = pltpu.matmul_pop(middles[0][r]) + pltpu.matmul_pop(middles[1][r])
            side = jnp.concatenate([
                part[0, h, 7 + r * rows_of:7 + (r + 1) * rows_of, :]
                + part[1, h, 9 + r * rows_of:9 + (r + 1) * rows_of, :] for h in (0, 1)
            ], 1)
            new = base[at] + factor * jnp.tanh(middle + side)
            st[f["dst"], at] = new
            rounded[f["rdst"], WIDTH + r * rows_of:WIDTH + (r + 1) * rows_of, :] = new.astype(bf16)

        @pl.when(jnp.logical_and(
            jnp.logical_and(f["rdst"] > UNSENT, has_next), f["op"] != OWNER_0
        ))
        def _():
            message(f["rdst"], distance(f["by"])).start()

        op = f["op"]

        @pl.when(op != NOTHING)
        def _():
            @pl.when(op == PSI_OF_LEFT)
            def _():
                psi = st[LF] + 4.0 * (st[CC] - base[...])
                st[QQ] = (st[CP] - psi) - st[CP]

            @pl.when(op == KEEP)
            def _():
                st[TT] = 4.0 * (st[CP] - base[...])

            @pl.when(op == START)
            def _():
                psi = st[LF] + st[TT]
                rhs = st[CP] + ((st[CP] - psi) - st[CP])
                first = psi + rhs
                st[CC] = first
                rounded_store(TO_FIRST, first)
                special(TO_FIRST, FIRST, 1).start()

            @pl.when(op == FIRST_POINT)
            def _():
                rounded_store(TO_FIRST, (st[CP] - (st[QQ] + st[CP])) + st[RH])
                special(TO_FIRST, FIRST, 1).start()

            @pl.when(op == OWNER_0)
            def _():
                for r in range(4):
                    at = slice(r * cells // 4, (r + 1) * cells // 4)
                    cc, xi = st[CC, at], st[XZ, at]
                    psi = st[LF, at] + (cc - base[at])
                    solved = xi + ((cc - xi) + (st[RH, at] - (cc - psi)))
                    rounded[TO_FINAL, WIDTH + at.start:WIDTH + at.stop, :] = solved.astype(bf16)
                    st[PSI, at] = solved
                send_solved()
                for r in range(4):
                    at = slice(r * cells // 4, (r + 1) * cells // 4)
                    st[TT, at] = st[CC, at] - base[at]
                    st[CC, at] = st[PSI, at]

            @pl.when(jnp.logical_or(op == PUT_0, jnp.logical_or(op == START, op == OWNER_0)))
            def _():
                t = jnp.where(op == PUT_0, st[f["dst"]] - base[...], st[TT])
                out = st[LF] + 0.25 * t
                st[OUT] = out
                rounded_store(OUTB, out)

            @pl.when(op == OWNER)
            def _():
                arrived(CHANGE)
                for r in range(4):
                    at = slice(r * cells // 4, (r + 1) * cells // 4)
                    inner_at = slice(WIDTH + at.start, WIDTH + at.stop)
                    cc = st[CC, at]
                    change = rounded[CHANGE, inner_at, :].astype(f32)
                    second = st[RH, at] - (cc - st[PSI, at])
                    solved = change + ((cc - st[ZERO, at]) + second)
                    rounded[TO_SECOND, inner_at, :] = cc.astype(bf16)
                    rounded[TO_FINAL, inner_at, :] = solved.astype(bf16)
                    st[CC, at] = solved
                send_solved()

            put_at = jnp.where(
                op == OWNER, COARSEN - 1, jnp.where(op == PUT_1, 1, jnp.where(op == PUT_2, 2, 0))
            )

            @pl.when(jnp.logical_and(op >= START, op <= OWNER))
            def _():
                put(jnp.where(op == OWNER, CC, OUT), put_at)

            @pl.when(op == CHANGES)
            def _():
                rounded_store(TO_CHANGE, st[XZ] - st[TMP])
                special(TO_CHANGE, CHANGE, COARSEN - 1).start()

        return later

    def loop(*totals):
        sides = (totals[:BLOCKS], totals[2 * BLOCKS:3 * BLOCKS])
        middles = (totals[BLOCKS:2 * BLOCKS], totals[3 * BLOCKS:])
        wait_weights(0)
        for load in weight_loads(3):
            load.start()
        for m in (0, 1):
            push(0, 0, m)
        lax.fori_loop(0, count, functools.partial(run, sides, middles), fields_of(0))
        for m in (0, 1):
            pltpu.matmul_acc_lhs(sides[m][0], rounded[CPB, 0:rows_of, :], 0)
        finish()
        for m in (0, 1):
            side_sum[0:rows_of, :] = pltpu.matmul_pop(sides[m][0])

    def finish():
        @pl.when(jnp.logical_not(jnp.logical_and(owner_shares, last_owner)))
        def _():
            put(CC, COARSEN - 1)

        def drain(copy, cond):
            @pl.when(cond)
            def _():
                copy.wait_send()

        relaxed = jnp.logical_or(
            jnp.logical_and(owner, lead_next), jnp.logical_and(phase == 1, group > 0)
        )
        drain(weight_to(back), jnp.logical_or(shares, owner_shares))
        drain(special(TO_LEFT, LEFT, back), has_next)
        drain(special(TO_RHS, RHS, back), shares)
        drain(special(TO_FIRST, FIRST, back), phase < 2)
        drain(special(TO_FINAL, FINAL, back), relaxed)
        drain(special(TO_SECOND, SECOND, back), relaxed)
        drain(special(TO_CHANGE, CHANGE, back), changes)
        drain(relay_of(FIRST), first_owner)
        drain(relay_of(FINAL), jnp.logical_and(lead, group > 0))
        drain(relay_of(SECOND), jnp.logical_and(phase == 1, group > 0))

    pl.run_scoped(
        loop, *[pltpu.ACC(m)((rows_of, chans), f32) for m in (0, 1) for _ in range(2 * BLOCKS)]
    )


def per_device(devices, inputs, guess, weights):
    chans, cells = inputs.shape
    return pl.pallas_call(
        functools.partial(kernel, devices),
        name="cycle",
        out_shape=pltpu.VMEM((COARSEN, chans, cells), jnp.float32),
        in_specs=[pl.BlockSpec(memory_space=pltpu.HBM)] * 3,
        out_specs=pl.BlockSpec(memory_space=pltpu.VMEM),
        scratch_shapes=[
            pltpu.VMEM((2, chans, cells), jnp.float32),
            pltpu.VMEM((COARSEN + 1,) + weights.shape[1:], jnp.bfloat16),
            pltpu.VMEM((STATES, cells, chans), jnp.float32),
            pltpu.VMEM((ROUNDED, cells + 2 * WIDTH, chans), jnp.bfloat16),
            pltpu.VMEM((2, 2, cells + 16, chans // 2), jnp.float32),
            pltpu.VMEM((cells, chans), jnp.float32),
            pltpu.VMEM((cells, chans), jnp.float32),
            pltpu.SemaphoreType.DMA((TO_RHS - TO_LEFT + 1,)),
            pltpu.SemaphoreType.DMA((FINAL - LEFT + 1,)),
            pltpu.SemaphoreType.DMA((1,)),
            pltpu.SemaphoreType.DMA((ROUNDED + 1,)),
            pltpu.SemaphoreType.DMA((2,)),
            pltpu.SemaphoreType.DMA((COARSEN, PIECES)),
        ],
        compiler_params=pltpu.CompilerParams(
            collective_id=0, has_side_effects=True, vmem_limit_bytes=56 * 2**20,
        ),
    )(*[pltpu.with_memory_space_constraint(a, pltpu.HBM) for a in (inputs, guess, weights)])


def solution(mesh):
    return jax.shard_map(
        functools.partial(per_device, mesh.shape["layer"]),
        mesh=mesh,
        in_specs=(P(None, "batch"), P("layer", None, "batch"), P("layer", None, None)),
        out_specs=P("layer", None, "batch"),
        check_vma=False,
    )
```

```python
import functools

import jax
import jax.numpy as jnp
from jax import lax
from jax.experimental import pallas as pl
from jax.experimental.pallas import tpu as pltpu
from jax.sharding import PartitionSpec as P

WIDTH = 16
COARSEN = 4
NONE = 15
PIECES = 2
BLOCKS = 8
ZERO, CP, LF, CC, RH, RHM, TT, PSI, QQ, XZ, OUT, TMP, DUMP = range(13)
STATES = 13
CPB, LFB, OUTB, CCB, TMPB, LEFT, FIRST, SECOND, FINAL, UNSENT = range(10)
TO_LEFT, TO_FIRST, TO_SECOND, TO_FINAL, TO_CHANGE, TO_RHS, CHANGE, RHS = range(10, 18)
ROUNDED = 18
WEIGHT = ROUNDED
NOTHING, PSI_OF_LEFT, FIRST_POINT, START, PUT_0, PUT_1, PUT_2, PUT_OUT, OWNER_0, OWNER, CHANGES, KEEP = range(12)
FIELDS = ("src", "dst", "w", "add", "factor", "rsrc", "rdst", "by", "recv", "relay", "need", "op")
BY_ONE, BY_TWO = 0, 1
QUARTER, WHOLE, FOUR = 0, 1, 2
ROUNDED_OF = {CP: CPB, LF: LFB, CC: CCB, OUT: OUTB, TMP: TMPB}


def step(src, dst, w, add=ZERO, factor=QUARTER, send=UNSENT, by=BY_ONE,
         recv=NONE, relay=0, need=0, op=NOTHING, rsrc=None):
    if rsrc is None:
        rsrc = ROUNDED_OF[src] if recv == NONE else recv
    rdst = ROUNDED_OF.get(dst, UNSENT) if send == UNSENT else send
    return dict(src=src, dst=dst, w=w, add=add, factor=factor, rsrc=rsrc, rdst=rdst,
                by=by, recv=recv, relay=relay, need=need, op=op)


def programs():
    def fine(send=UNSENT, first=NOTHING, op=NOTHING):
        return [step(CP, CP, 0, op=first), step(CP, CP, 1), step(CP, CP, 2),
                step(CP, CP, 3, send=send, op=op)]

    def again(send=UNSENT, op=NOTHING):
        return [step(LF, CC, 0, recv=LEFT, op=PSI_OF_LEFT), step(CC, CC, 1),
                step(CC, CC, 2), step(CC, RH, 3, add=QQ, send=send, op=op)]

    def whole(recv, dst, relay=0, need=0):
        return step(TMP, dst, COARSEN, add=RHM, factor=WHOLE, recv=recv, relay=relay, need=need)

    def own(src, dst, **kw):
        return step(src, dst, 0, add=RH, factor=WHOLE, **kw)

    last = [step(OUT, OUT, 1, op=PUT_1), step(OUT, OUT, 2, op=PUT_2)]
    body = fine(TO_LEFT) + again()
    mate = fine(TO_LEFT) + again(TO_RHS)
    final = [whole(FINAL, LF, relay=1)]
    owner_second = [whole(SECOND, TMP), step(TMP, PSI, 0, factor=WHOLE, op=OWNER)]
    relaxed = [whole(FIRST, TMP, need=1), own(TMP, CC)] + final + [
        step(LF, OUT, 0, op=PUT_OUT)]
    return {
        "start": fine(TO_LEFT, KEEP, START) + last,
        "lead_first": body + [own(LF, CC, recv=FIRST, send=TO_FIRST, by=BY_TWO, op=PUT_0)] + last,
        "mate_first": mate + [own(LF, CC, recv=FIRST, op=PUT_0)] + last,
        "owner_first": body + [
            step(TMP, XZ, 0, factor=FOUR), whole(FIRST, LF, relay=1, need=1),
            own(LF, CC, send=TO_SECOND, op=OWNER_0)] + last,
        "head": fine(TO_LEFT) + again(TO_RHS, FIRST_POINT) + [
            own(LF, CC, recv=FINAL),
            step(LF, XZ, COARSEN, factor=FOUR, need=2, rsrc=FINAL),
            step(TMP, TMP, COARSEN, factor=FOUR, recv=SECOND, op=CHANGES),
            step(LF, OUT, 0, rsrc=FINAL, op=PUT_OUT)] + last,
        "lead": body + [
            own(LF, TMP, recv=FIRST, send=TO_FIRST, by=BY_TWO),
            whole(FINAL, LF, relay=1, need=1),
            own(LF, CC, send=TO_FINAL, by=BY_TWO, op=PUT_0),
            whole(SECOND, TMP, relay=1),
            own(TMP, TMP, send=TO_SECOND, by=BY_TWO)] + last,
        "mate": mate + [own(LF, CC, recv=FINAL, op=PUT_0)] + last,
        "owner": body + relaxed + owner_second + last,
        "owner_last": body + relaxed + last + owner_second,
    }


def packed(values):
    words = []
    for start in (0, 8):
        word = sum(v << (4 * k) for k, v in enumerate(values[start:start + 8]))
        words.append(word - 2**32 if word >= 2**31 else word)
    return words


def kernel(
    devices, x_hbm, g_hbm, w_hbm, o_ref,
    xg, w, st, rounded, part, side_sum, base,
    send_sem, relay_sem, extra_sem, recv_sem, load_sem, weight_sem,
):
    f32, bf16 = jnp.float32, jnp.bfloat16
    p = lax.axis_index("layer")
    phase = lax.rem(p, COARSEN)
    owner = phase == COARSEN - 1
    group = lax.div(p, COARSEN)
    lead = lax.rem(p, 2) == 1
    mate = jnp.logical_not(lead)
    _, cells, chans = st.shape

    own_load = pltpu.make_async_copy(g_hbm.at[0], xg.at[0], load_sem.at[0])
    x_load = pltpu.make_async_copy(x_hbm, xg.at[0], load_sem.at[0])
    start_load = pltpu.make_async_copy(x_hbm, xg.at[1], load_sem.at[1])
    first_owner = jnp.logical_and(owner, group == 0)

    def weight_loads(j):
        rows = w.shape[1] // PIECES
        return [
            pltpu.make_async_copy(
                w_hbm.at[j, pl.ds(n * rows, rows)], w.at[j, pl.ds(n * rows, rows)],
                weight_sem.at[j, n],
            )
            for n in range(PIECES)
        ]

    @pl.when(p == 0)
    def _():
        x_load.start()

    @pl.when(p > 0)
    def _():
        own_load.start()

    for load in weight_loads(0) + weight_loads(1):
        load.start()

    @pl.when(first_owner)
    def _():
        start_load.start()

    barrier = pltpu.get_barrier_semaphore()

    def greet(by, cond):
        @pl.when(cond)
        def _():
            pl.semaphore_signal(
                barrier, inc=1, device_id={"layer": p + by},
                device_id_type=pl.DeviceIdType.MESH,
            )
        return cond.astype(jnp.int32)

    has_next = p < devices - 1
    lead_next = jnp.logical_and(lead, p + 2 < devices)
    last_owner = p + COARSEN >= devices
    greeted = (
        greet(1, has_next) + greet(-1, p > 0)
        + greet(COARSEN - 1, jnp.logical_and(phase == 0, group > 0))
        + greet(1 - COARSEN, jnp.logical_and(owner, group > 0))
        + greet(2, lead_next) + greet(-2, jnp.logical_and(lead, p >= 2))
    )
    shares = jnp.logical_and(mate, p > 0)
    owner_shares = jnp.logical_and(owner, group > 0)
    changes = jnp.logical_and(phase == 0, group > 0)

    roles = [
        ("start", p == 0),
        ("lead_first", jnp.logical_and(group == 0, phase == 1)),
        ("mate_first", jnp.logical_and(group == 0, phase == 2)),
        ("owner_first", first_owner),
        ("head", changes),
        ("lead", jnp.logical_and(group > 0, phase == 1)),
        ("mate", jnp.logical_and(group > 0, phase == 2)),
        ("owner_last", jnp.logical_and(owner, jnp.logical_and(group > 0, last_owner))),
    ]
    listed = programs()

    def chosen(value_of):
        value = jnp.int32(value_of(listed["owner"]))
        for name, cond in roles:
            value = jnp.where(cond, jnp.int32(value_of(listed[name])), value)
        return value

    count = chosen(len)
    words = {
        field: [
            chosen(lambda steps: packed([s[field] for s in steps])[half]) for half in (0, 1)
        ]
        for field in FIELDS
    }

    def entry(field, i):
        low, high = words[field]
        word = jnp.where(i < 8, low, high)
        return jnp.bitwise_and(
            lax.shift_right_logical(word, 4 * jnp.bitwise_and(i, 7)), 15
        )

    def remote(src, dst, ssem, rsem, by):
        return pltpu.make_async_remote_copy(
            src_ref=src, dst_ref=dst, send_sem=ssem, recv_sem=rsem,
            device_id={"layer": p + by}, device_id_type=pl.DeviceIdType.MESH,
        )

    def inner(slot):
        return rounded.at[slot, pl.ds(WIDTH, cells)]

    def landing(slot):
        return jnp.where(slot == TO_RHS, RHS, slot - (TO_LEFT - LEFT))

    def message(slot, by):
        to = landing(slot)
        return remote(inner(slot), inner(to), send_sem.at[slot - TO_LEFT], recv_sem.at[to], by)

    def relay_of(slot):
        return remote(inner(slot), inner(slot), relay_sem.at[slot - LEFT], recv_sem.at[slot], -1)

    back = jnp.where(p > 0, -1, 1)

    def arrived(slot):
        remote(inner(slot), inner(slot), extra_sem.at[0], recv_sem.at[slot], back).wait_recv()

    def weight_to(by):
        return remote(w_hbm.at[0], w.at[COARSEN], extra_sem.at[0], recv_sem.at[WEIGHT], by)

    def special(slot, to, by):
        return remote(inner(slot), inner(to), send_sem.at[slot - TO_LEFT], recv_sem.at[to], by)

    def rounded_store(slot, value):
        rounded[slot, WIDTH:WIDTH + cells, :] = value.astype(bf16)

    def distance(code):
        return jnp.where(code == BY_TWO, 2, 1)

    half = chans // 2
    rounded[:, 0:WIDTH, :] = jnp.zeros((ROUNDED, WIDTH, chans), bf16)
    rounded[:, WIDTH + cells:, :] = jnp.zeros((ROUNDED, WIDTH, chans), bf16)
    part[:, :, 0:8, :] = jnp.zeros((2, 2, 8, half), f32)
    part[:, :, 8 + cells:, :] = jnp.zeros((2, 2, 8, half), f32)
    st[ZERO] = jnp.zeros((cells, chans), f32)

    def put(slot, n):
        o_ref[n] = st[slot].T

    own_load.wait()
    for load in weight_loads(2):
        load.start()
    loaded = xg[0].T
    st[LF] = loaded
    st[CP] = loaded
    rounded_store(CPB, loaded)

    @pl.when(first_owner)
    def _():
        start_load.wait()
        start = xg[1].T
        st[TMP] = start
        rounded_store(TMPB, start)

    def send_solved():
        @pl.when(lead_next)
        def _():
            special(TO_FINAL, FINAL, 2).start()
            special(TO_SECOND, SECOND, 2).start()

    pl.semaphore_wait(barrier, greeted)

    @pl.when(owner_shares)
    def _():
        weight_to(1 - COARSEN).start()

    @pl.when(shares)
    def _():
        weight_to(1).start()

    rows_of = cells // BLOCKS
    col = lax.rem(lax.broadcasted_iota(jnp.int32, (rows_of, chans), 0), WIDTH)
    order = [
        [(1, 0), (0, 0), (2, 0), (0, 1), (1, 1)],
        [(1, 2), (0, 2), (2, 2), (2, 1), (1, 1)],
    ]

    def push(which, k, m):
        dy, dx = order[m][k]
        tap = 3 * dy + dx
        pltpu.matmul_push_rhs(
            w[which, :, tap * chans:(tap + 1) * chans], k % 2, m, transpose=True
        )

    def wait_weights(j):
        for load in weight_loads(j):
            load.wait()

    def fields_of(i):
        return tuple(entry(field, i) for field in FIELDS)

    def run(sides, middles, i, fields):
        f = dict(zip(FIELDS, fields))

        @pl.when(f["need"] == 1)
        def _():
            arrived(RHS)
            st[RHM] = rounded[RHS, WIDTH:WIDTH + cells, :].astype(f32)

        received = f["recv"] != NONE

        @pl.when(received)
        def _():
            arrived(f["recv"])

            @pl.when(f["relay"] == 1)
            def _():
                relay_of(f["recv"]).start()

        source = f["rsrc"]

        def lhs(dy, r):
            return rounded[source, WIDTH * dy + r * rows_of:WIDTH * dy + (r + 1) * rows_of, :]

        def stream(k):
            for m in (0, 1):
                dy = order[m][k][0]
                total = sides[m] if k < 3 else middles[m]
                taken = range(BLOCKS) if k < 4 else range(m, BLOCKS, 2)
                for n, r in enumerate(taken):
                    pltpu.matmul_acc_lhs(total[r], lhs(dy, r), k % 2 if n == 0 else None)

        for m in (0, 1):
            push(f["w"], 1, m)
        stream(0)
        later = fields_of(i + 1)
        following = dict(zip(FIELDS, later))
        next_weight = jnp.logical_and(i + 1 < count, following["need"] > 0)

        @pl.when(received)
        def _():
            st[f["src"]] = rounded[source, WIDTH:WIDTH + cells, :].astype(f32)

        @pl.when(jnp.logical_or(i < COARSEN - 1, next_weight))
        def _():
            @pl.when(i < COARSEN - 1)
            def _():
                wait_weights(i + 1)

            @pl.when(next_weight)
            def _():
                remote(w.at[0], w.at[COARSEN], extra_sem.at[0], recv_sem.at[WEIGHT], back).wait_recv()

        for k in range(1, 5):
            for m in (0, 1):
                if k < 4:
                    push(f["w"], k + 1, m)
            stream(k)
        for m in (0, 1):
            push(following["w"], 0, m)
        for r in range(BLOCKS):
            for m in (0, 1):
                t = pltpu.matmul_pop(sides[m][r])
                t = jnp.where(col == (0 if m else WIDTH - 1), 0.0, t)
                for h in (0, 1):
                    part[m, h, 8 + r * rows_of:8 + (r + 1) * rows_of, :] = t[:, h * half:(h + 1) * half]
        base[...] = st[f["src"]] + st[f["add"]]

        factor = jnp.where(f["factor"] == QUARTER, 0.25, jnp.where(f["factor"] == WHOLE, 1.0, 4.0))
        for r in range(BLOCKS):
            at = slice(r * rows_of, (r + 1) * rows_of)
            middle = pltpu.matmul_pop(middles[0][r]) + pltpu.matmul_pop(middles[1][r])
            side = jnp.concatenate([
                part[0, h, 7 + r * rows_of:7 + (r + 1) * rows_of, :]
                + part[1, h, 9 + r * rows_of:9 + (r + 1) * rows_of, :] for h in (0, 1)
            ], 1)
            new = base[at] + factor * jnp.tanh(middle + side)
            st[f["dst"], at] = new
            rounded[f["rdst"], WIDTH + r * rows_of:WIDTH + (r + 1) * rows_of, :] = new.astype(bf16)

        @pl.when(jnp.logical_and(
            jnp.logical_and(f["rdst"] > UNSENT, has_next), f["op"] != OWNER_0
        ))
        def _():
            message(f["rdst"], distance(f["by"])).start()

        op = f["op"]

        @pl.when(op != NOTHING)
        def _():
            @pl.when(op == PSI_OF_LEFT)
            def _():
                psi = st[LF] + 4.0 * (st[CC] - base[...])
                st[QQ] = (st[CP] - psi) - st[CP]

            @pl.when(op == KEEP)
            def _():
                st[TT] = 4.0 * (st[CP] - base[...])

            @pl.when(op == START)
            def _():
                psi = st[LF] + st[TT]
                rhs = st[CP] + ((st[CP] - psi) - st[CP])
                first = psi + rhs
                st[CC] = first
                rounded_store(TO_FIRST, first)
                special(TO_FIRST, FIRST, 1).start()

            @pl.when(op == FIRST_POINT)
            def _():
                rounded_store(TO_FIRST, (st[CP] - (st[QQ] + st[CP])) + st[RH])
                special(TO_FIRST, FIRST, 1).start()

            @pl.when(op == OWNER_0)
            def _():
                for r in range(4):
                    at = slice(r * cells // 4, (r + 1) * cells // 4)
                    cc, xi = st[CC, at], st[XZ, at]
                    psi = st[LF, at] + (cc - base[at])
                    solved = xi + ((cc - xi) + (st[RH, at] - (cc - psi)))
                    rounded[TO_FINAL, WIDTH + at.start:WIDTH + at.stop, :] = solved.astype(bf16)
                    st[PSI, at] = solved
                send_solved()
                for r in range(4):
                    at = slice(r * cells // 4, (r + 1) * cells // 4)
                    st[TT, at] = st[CC, at] - base[at]
                    st[CC, at] = st[PSI, at]

            @pl.when(jnp.logical_or(op == PUT_0, jnp.logical_or(op == START, op == OWNER_0)))
            def _():
                t = jnp.where(op == PUT_0, st[f["dst"]] - base[...], st[TT])
                out = st[LF] + 0.25 * t
                st[OUT] = out
                rounded_store(OUTB, out)

            @pl.when(op == OWNER)
            def _():
                arrived(CHANGE)
                for r in range(4):
                    at = slice(r * cells // 4, (r + 1) * cells // 4)
                    inner_at = slice(WIDTH + at.start, WIDTH + at.stop)
                    cc = st[CC, at]
                    change = rounded[CHANGE, inner_at, :].astype(f32)
                    second = st[RH, at] - (cc - st[PSI, at])
                    solved = change + ((cc - st[ZERO, at]) + second)
                    rounded[TO_SECOND, inner_at, :] = cc.astype(bf16)
                    rounded[TO_FINAL, inner_at, :] = solved.astype(bf16)
                    st[CC, at] = solved
                send_solved()

            put_at = jnp.where(
                op == OWNER, COARSEN - 1, jnp.where(op == PUT_1, 1, jnp.where(op == PUT_2, 2, 0))
            )

            @pl.when(jnp.logical_and(op >= START, op <= OWNER))
            def _():
                put(jnp.where(op == OWNER, CC, OUT), put_at)

            @pl.when(op == CHANGES)
            def _():
                rounded_store(TO_CHANGE, st[XZ] - st[TMP])
                special(TO_CHANGE, CHANGE, COARSEN - 1).start()

        return later

    def loop(*totals):
        sides = (totals[:BLOCKS], totals[2 * BLOCKS:3 * BLOCKS])
        middles = (totals[BLOCKS:2 * BLOCKS], totals[3 * BLOCKS:])
        wait_weights(0)
        for load in weight_loads(3):
            load.start()
        for m in (0, 1):
            push(0, 0, m)
        lax.fori_loop(0, count, functools.partial(run, sides, middles), fields_of(0))
        for m in (0, 1):
            pltpu.matmul_acc_lhs(sides[m][0], rounded[CPB, 0:rows_of, :], 0)
        finish()
        for m in (0, 1):
            side_sum[0:rows_of, :] = pltpu.matmul_pop(sides[m][0])

    def finish():
        @pl.when(jnp.logical_not(jnp.logical_and(owner_shares, last_owner)))
        def _():
            put(CC, COARSEN - 1)

        def drain(copy, cond):
            @pl.when(cond)
            def _():
                copy.wait_send()

        relaxed = jnp.logical_or(
            jnp.logical_and(owner, lead_next), jnp.logical_and(phase == 1, group > 0)
        )
        drain(weight_to(back), jnp.logical_or(shares, owner_shares))
        drain(special(TO_LEFT, LEFT, back), has_next)
        drain(special(TO_RHS, RHS, back), shares)
        drain(special(TO_FIRST, FIRST, back), phase < 2)
        drain(special(TO_FINAL, FINAL, back), relaxed)
        drain(special(TO_SECOND, SECOND, back), relaxed)
        drain(special(TO_CHANGE, CHANGE, back), changes)
        drain(relay_of(FIRST), first_owner)
        drain(relay_of(FINAL), jnp.logical_and(lead, group > 0))
        drain(relay_of(SECOND), jnp.logical_and(phase == 1, group > 0))

    pl.run_scoped(
        loop, *[pltpu.ACC(m)((rows_of, chans), f32) for m in (0, 1) for _ in range(2 * BLOCKS)]
    )


def per_device(devices, inputs, guess, weights):
    chans, cells = inputs.shape
    return pl.pallas_call(
        functools.partial(kernel, devices),
        name="cycle",
        out_shape=pltpu.VMEM((COARSEN, chans, cells), jnp.float32),
        in_specs=[pl.BlockSpec(memory_space=pltpu.HBM)] * 3,
        out_specs=pl.BlockSpec(memory_space=pltpu.VMEM),
        scratch_shapes=[
            pltpu.VMEM((2, chans, cells), jnp.float32),
            pltpu.VMEM((COARSEN + 1,) + weights.shape[1:], jnp.bfloat16),
            pltpu.VMEM((STATES, cells, chans), jnp.float32),
            pltpu.VMEM((ROUNDED, cells + 2 * WIDTH, chans), jnp.bfloat16),
            pltpu.VMEM((2, 2, cells + 16, chans // 2), jnp.float32),
            pltpu.VMEM((cells, chans), jnp.float32),
            pltpu.VMEM((cells, chans), jnp.float32),
            pltpu.SemaphoreType.DMA((TO_RHS - TO_LEFT + 1,)),
            pltpu.SemaphoreType.DMA((FINAL - LEFT + 1,)),
            pltpu.SemaphoreType.DMA((1,)),
            pltpu.SemaphoreType.DMA((ROUNDED + 1,)),
            pltpu.SemaphoreType.DMA((2,)),
            pltpu.SemaphoreType.DMA((COARSEN, PIECES)),
        ],
        compiler_params=pltpu.CompilerParams(
            collective_id=0, has_side_effects=True, vmem_limit_bytes=56 * 2**20,
        ),
    )(*[pltpu.with_memory_space_constraint(a, pltpu.HBM) for a in (inputs, guess, weights)])


def solution(mesh):
    return jax.shard_map(
        functools.partial(per_device, mesh.shape["layer"]),
        mesh=mesh,
        in_specs=(P(None, "batch"), P("layer", None, "batch"), P("layer", None, None)),
        out_specs=P("layer", None, "batch"),
        check_vma=False,
    )
```

```python
import functools

import jax
import jax.numpy as jnp
from jax import lax
from jax.experimental import pallas as pl
from jax.experimental.pallas import tpu as pltpu
from jax.sharding import PartitionSpec as P

WIDTH = 16
COARSEN = 4
NONE = 15
PIECES = 2
BLOCKS = 8
ZERO, CP, LF, CC, RH, RHM, TT, PSI, QQ, XZ, OUT, TMP, DUMP = range(13)
STATES = 13
CPB, LFB, OUTB, CCB, TMPB, LEFT, FIRST, SECOND, FINAL, UNSENT = range(10)
TO_LEFT, TO_FIRST, TO_SECOND, TO_FINAL, TO_CHANGE, TO_RHS, CHANGE, RHS = range(10, 18)
ROUNDED = 18
WEIGHT = ROUNDED
NOTHING, PSI_OF_LEFT, FIRST_POINT, START, PUT_0, PUT_1, PUT_2, PUT_OUT, OWNER_0, OWNER, CHANGES, KEEP = range(12)
FIELDS = ("src", "dst", "w", "add", "factor", "rsrc", "rdst", "by", "recv", "relay", "need", "op")
BY_ONE, BY_TWO = 0, 1
QUARTER, WHOLE, FOUR = 0, 1, 2
ROUNDED_OF = {CP: CPB, LF: LFB, CC: CCB, OUT: OUTB, TMP: TMPB}


def step(src, dst, w, add=ZERO, factor=QUARTER, send=UNSENT, by=BY_ONE,
         recv=NONE, relay=0, need=0, op=NOTHING, rsrc=None):
    if rsrc is None:
        rsrc = ROUNDED_OF[src] if recv == NONE else recv
    rdst = ROUNDED_OF.get(dst, UNSENT) if send == UNSENT else send
    return dict(src=src, dst=dst, w=w, add=add, factor=factor, rsrc=rsrc, rdst=rdst,
                by=by, recv=recv, relay=relay, need=need, op=op)


def programs():
    def fine(send=UNSENT, first=NOTHING, op=NOTHING):
        return [step(CP, CP, 0, op=first), step(CP, CP, 1), step(CP, CP, 2),
                step(CP, CP, 3, send=send, op=op)]

    def again(send=UNSENT, op=NOTHING):
        return [step(LF, CC, 0, recv=LEFT, op=PSI_OF_LEFT), step(CC, CC, 1),
                step(CC, CC, 2), step(CC, RH, 3, add=QQ, send=send, op=op)]

    def whole(recv, dst, relay=0, need=0):
        return step(TMP, dst, COARSEN, add=RHM, factor=WHOLE, recv=recv, relay=relay, need=need)

    def own(src, dst, **kw):
        return step(src, dst, 0, add=RH, factor=WHOLE, **kw)

    last = [step(OUT, OUT, 1, op=PUT_1), step(OUT, OUT, 2, op=PUT_2)]
    body = fine(TO_LEFT) + again()
    mate = fine(TO_LEFT) + again(TO_RHS)
    final = [whole(FINAL, LF, relay=1)]
    owner_second = [whole(SECOND, TMP), step(TMP, PSI, 0, factor=WHOLE, op=OWNER)]
    relaxed = [whole(FIRST, TMP, need=1), own(TMP, CC)] + final + [
        step(LF, OUT, 0, op=PUT_OUT)]
    return {
        "start": fine(TO_LEFT, KEEP, START) + last,
        "lead_first": body + [own(LF, CC, recv=FIRST, send=TO_FIRST, by=BY_TWO, op=PUT_0)] + last,
        "mate_first": mate + [own(LF, CC, recv=FIRST, op=PUT_0)] + last,
        "owner_first": body + [
            step(TMP, XZ, 0, factor=FOUR), whole(FIRST, LF, relay=1, need=1),
            own(LF, CC, send=TO_SECOND, op=OWNER_0)] + last,
        "head": fine(TO_LEFT) + again(TO_RHS, FIRST_POINT) + [
            own(LF, CC, recv=FINAL),
            step(LF, XZ, COARSEN, factor=FOUR, need=2, rsrc=FINAL),
            step(TMP, TMP, COARSEN, factor=FOUR, recv=SECOND, op=CHANGES),
            step(LF, OUT, 0, rsrc=FINAL, op=PUT_OUT)] + last,
        "lead": body + [
            own(LF, TMP, recv=FIRST, send=TO_FIRST, by=BY_TWO),
            whole(FINAL, LF, relay=1, need=1),
            own(LF, CC, send=TO_FINAL, by=BY_TWO, op=PUT_0),
            whole(SECOND, TMP, relay=1),
            own(TMP, TMP, send=TO_SECOND, by=BY_TWO)] + last,
        "mate": mate + [own(LF, CC, recv=FINAL, op=PUT_0)] + last,
        "owner": body + relaxed + owner_second + last,
        "owner_last": body + relaxed + last + owner_second,
    }


def packed(values):
    words = []
    for start in (0, 8):
        word = sum(v << (4 * k) for k, v in enumerate(values[start:start + 8]))
        words.append(word - 2**32 if word >= 2**31 else word)
    return words


def kernel(
    devices, x_hbm, g_hbm, w_hbm, o_ref,
    xg, w, st, rounded, part, side_sum, base,
    send_sem, relay_sem, extra_sem, recv_sem, load_sem, weight_sem,
):
    f32, bf16 = jnp.float32, jnp.bfloat16
    p = lax.axis_index("layer")
    phase = lax.rem(p, COARSEN)
    owner = phase == COARSEN - 1
    group = lax.div(p, COARSEN)
    lead = lax.rem(p, 2) == 1
    mate = jnp.logical_not(lead)
    _, cells, chans = st.shape

    own_load = pltpu.make_async_copy(g_hbm.at[0], xg.at[0], load_sem.at[0])
    x_load = pltpu.make_async_copy(x_hbm, xg.at[0], load_sem.at[0])
    start_load = pltpu.make_async_copy(x_hbm, xg.at[1], load_sem.at[1])
    first_owner = jnp.logical_and(owner, group == 0)

    def weight_loads(j):
        rows = w.shape[1] // PIECES
        return [
            pltpu.make_async_copy(
                w_hbm.at[j, pl.ds(n * rows, rows)], w.at[j, pl.ds(n * rows, rows)],
                weight_sem.at[j, n],
            )
            for n in range(PIECES)
        ]

    @pl.when(p == 0)
    def _():
        x_load.start()

    @pl.when(p > 0)
    def _():
        own_load.start()

    for load in weight_loads(0) + weight_loads(1):
        load.start()

    @pl.when(first_owner)
    def _():
        start_load.start()

    barrier = pltpu.get_barrier_semaphore()

    def greet(by, cond):
        @pl.when(cond)
        def _():
            pl.semaphore_signal(
                barrier, inc=1, device_id={"layer": p + by},
                device_id_type=pl.DeviceIdType.MESH,
            )
        return cond.astype(jnp.int32)

    has_next = p < devices - 1
    lead_next = jnp.logical_and(lead, p + 2 < devices)
    last_owner = p + COARSEN >= devices
    greeted = (
        greet(1, has_next) + greet(-1, p > 0)
        + greet(COARSEN - 1, jnp.logical_and(phase == 0, group > 0))
        + greet(1 - COARSEN, jnp.logical_and(owner, group > 0))
        + greet(2, lead_next) + greet(-2, jnp.logical_and(lead, p >= 2))
    )
    shares = jnp.logical_and(mate, p > 0)
    owner_shares = jnp.logical_and(owner, group > 0)
    changes = jnp.logical_and(phase == 0, group > 0)

    roles = [
        ("start", p == 0),
        ("lead_first", jnp.logical_and(group == 0, phase == 1)),
        ("mate_first", jnp.logical_and(group == 0, phase == 2)),
        ("owner_first", first_owner),
        ("head", changes),
        ("lead", jnp.logical_and(group > 0, phase == 1)),
        ("mate", jnp.logical_and(group > 0, phase == 2)),
        ("owner_last", jnp.logical_and(owner, jnp.logical_and(group > 0, last_owner))),
    ]
    listed = programs()

    def chosen(value_of):
        value = jnp.int32(value_of(listed["owner"]))
        for name, cond in roles:
            value = jnp.where(cond, jnp.int32(value_of(listed[name])), value)
        return value

    count = chosen(len)
    words = {
        field: [
            chosen(lambda steps: packed([s[field] for s in steps])[half]) for half in (0, 1)
        ]
        for field in FIELDS
    }

    def entry(field, i):
        low, high = words[field]
        word = jnp.where(i < 8, low, high)
        return jnp.bitwise_and(
            lax.shift_right_logical(word, 4 * jnp.bitwise_and(i, 7)), 15
        )

    def remote(src, dst, ssem, rsem, by):
        return pltpu.make_async_remote_copy(
            src_ref=src, dst_ref=dst, send_sem=ssem, recv_sem=rsem,
            device_id={"layer": p + by}, device_id_type=pl.DeviceIdType.MESH,
        )

    def inner(slot):
        return rounded.at[slot, pl.ds(WIDTH, cells)]

    def landing(slot):
        return jnp.where(slot == TO_RHS, RHS, slot - (TO_LEFT - LEFT))

    def message(slot, by):
        to = landing(slot)
        return remote(inner(slot), inner(to), send_sem.at[slot - TO_LEFT], recv_sem.at[to], by)

    def relay_of(slot):
        return remote(inner(slot), inner(slot), relay_sem.at[slot - LEFT], recv_sem.at[slot], -1)

    back = jnp.where(p > 0, -1, 1)

    def arrived(slot):
        remote(inner(slot), inner(slot), extra_sem.at[0], recv_sem.at[slot], back).wait_recv()

    def weight_to(by):
        return remote(w_hbm.at[0], w.at[COARSEN], extra_sem.at[0], recv_sem.at[WEIGHT], by)

    def special(slot, to, by):
        return remote(inner(slot), inner(to), send_sem.at[slot - TO_LEFT], recv_sem.at[to], by)

    def rounded_store(slot, value):
        rounded[slot, WIDTH:WIDTH + cells, :] = value.astype(bf16)

    def distance(code):
        return jnp.where(code == BY_TWO, 2, 1)

    half = chans // 2
    rounded[:, 0:WIDTH, :] = jnp.zeros((ROUNDED, WIDTH, chans), bf16)
    rounded[:, WIDTH + cells:, :] = jnp.zeros((ROUNDED, WIDTH, chans), bf16)
    part[:, :, 0:8, :] = jnp.zeros((2, 2, 8, half), f32)
    part[:, :, 8 + cells:, :] = jnp.zeros((2, 2, 8, half), f32)
    st[ZERO] = jnp.zeros((cells, chans), f32)

    def put(slot, n):
        o_ref[n] = st[slot].T

    pl.semaphore_wait(barrier, greeted)

    @pl.when(owner_shares)
    def _():
        weight_to(1 - COARSEN).start()

    own_load.wait()
    for load in weight_loads(2):
        load.start()
    loaded = xg[0].T
    st[LF] = loaded
    st[CP] = loaded
    rounded_store(CPB, loaded)

    @pl.when(first_owner)
    def _():
        start_load.wait()
        start = xg[1].T
        st[TMP] = start
        rounded_store(TMPB, start)

    def send_solved():
        @pl.when(lead_next)
        def _():
            special(TO_FINAL, FINAL, 2).start()
            special(TO_SECOND, SECOND, 2).start()

    @pl.when(shares)
    def _():
        weight_to(1).start()

    rows_of = cells // BLOCKS
    col = lax.rem(lax.broadcasted_iota(jnp.int32, (rows_of, chans), 0), WIDTH)
    order = [
        [(1, 0), (0, 0), (2, 0), (0, 1), (1, 1)],
        [(1, 2), (0, 2), (2, 2), (2, 1), (1, 1)],
    ]

    def push(which, k, m):
        dy, dx = order[m][k]
        tap = 3 * dy + dx
        pltpu.matmul_push_rhs(
            w[which, :, tap * chans:(tap + 1) * chans], k % 2, m, transpose=True
        )

    def wait_weights(j):
        for load in weight_loads(j):
            load.wait()

    def fields_of(i):
        return tuple(entry(field, i) for field in FIELDS)

    def run(sides, middles, i, fields):
        f = dict(zip(FIELDS, fields))

        @pl.when(f["need"] == 1)
        def _():
            arrived(RHS)
            st[RHM] = rounded[RHS, WIDTH:WIDTH + cells, :].astype(f32)

        received = f["recv"] != NONE

        @pl.when(received)
        def _():
            arrived(f["recv"])

            @pl.when(f["relay"] == 1)
            def _():
                relay_of(f["recv"]).start()

        source = f["rsrc"]

        def lhs(dy, r):
            return rounded[source, WIDTH * dy + r * rows_of:WIDTH * dy + (r + 1) * rows_of, :]

        def stream(k):
            for m in (0, 1):
                dy = order[m][k][0]
                total = sides[m] if k < 3 else middles[m]
                taken = range(BLOCKS) if k < 4 else range(m, BLOCKS, 2)
                for n, r in enumerate(taken):
                    pltpu.matmul_acc_lhs(total[r], lhs(dy, r), k % 2 if n == 0 else None)

        for m in (0, 1):
            push(f["w"], 1, m)
        stream(0)
        later = fields_of(i + 1)
        following = dict(zip(FIELDS, later))
        next_weight = jnp.logical_and(i + 1 < count, following["need"] > 0)

        @pl.when(received)
        def _():
            st[f["src"]] = rounded[source, WIDTH:WIDTH + cells, :].astype(f32)

        @pl.when(jnp.logical_or(i < COARSEN - 1, next_weight))
        def _():
            @pl.when(i < COARSEN - 1)
            def _():
                wait_weights(i + 1)

            @pl.when(next_weight)
            def _():
                remote(w.at[0], w.at[COARSEN], extra_sem.at[0], recv_sem.at[WEIGHT], back).wait_recv()

        for k in range(1, 5):
            for m in (0, 1):
                if k < 4:
                    push(f["w"], k + 1, m)
            stream(k)
        for m in (0, 1):
            push(following["w"], 0, m)
        for r in range(BLOCKS):
            for m in (0, 1):
                t = pltpu.matmul_pop(sides[m][r])
                t = jnp.where(col == (0 if m else WIDTH - 1), 0.0, t)
                for h in (0, 1):
                    part[m, h, 8 + r * rows_of:8 + (r + 1) * rows_of, :] = t[:, h * half:(h + 1) * half]
        base[...] = st[f["src"]] + st[f["add"]]

        factor = jnp.where(f["factor"] == QUARTER, 0.25, jnp.where(f["factor"] == WHOLE, 1.0, 4.0))
        for r in range(BLOCKS):
            at = slice(r * rows_of, (r + 1) * rows_of)
            middle = pltpu.matmul_pop(middles[0][r]) + pltpu.matmul_pop(middles[1][r])
            side = jnp.concatenate([
                part[0, h, 7 + r * rows_of:7 + (r + 1) * rows_of, :]
                + part[1, h, 9 + r * rows_of:9 + (r + 1) * rows_of, :] for h in (0, 1)
            ], 1)
            new = base[at] + factor * jnp.tanh(middle + side)
            st[f["dst"], at] = new
            rounded[f["rdst"], WIDTH + r * rows_of:WIDTH + (r + 1) * rows_of, :] = new.astype(bf16)

        @pl.when(jnp.logical_and(
            jnp.logical_and(f["rdst"] > UNSENT, has_next), f["op"] != OWNER_0
        ))
        def _():
            message(f["rdst"], distance(f["by"])).start()

        op = f["op"]

        @pl.when(op != NOTHING)
        def _():
            @pl.when(op == PSI_OF_LEFT)
            def _():
                psi = st[LF] + 4.0 * (st[CC] - base[...])
                st[QQ] = (st[CP] - psi) - st[CP]

            @pl.when(op == KEEP)
            def _():
                st[TT] = 4.0 * (st[CP] - base[...])

            @pl.when(op == START)
            def _():
                psi = st[LF] + st[TT]
                rhs = st[CP] + ((st[CP] - psi) - st[CP])
                first = psi + rhs
                st[CC] = first
                rounded_store(TO_FIRST, first)
                special(TO_FIRST, FIRST, 1).start()

            @pl.when(op == FIRST_POINT)
            def _():
                rounded_store(TO_FIRST, (st[CP] - (st[QQ] + st[CP])) + st[RH])
                special(TO_FIRST, FIRST, 1).start()

            @pl.when(op == OWNER_0)
            def _():
                for r in range(4):
                    at = slice(r * cells // 4, (r + 1) * cells // 4)
                    cc, xi = st[CC, at], st[XZ, at]
                    psi = st[LF, at] + (cc - base[at])
                    solved = xi + ((cc - xi) + (st[RH, at] - (cc - psi)))
                    rounded[TO_FINAL, WIDTH + at.start:WIDTH + at.stop, :] = solved.astype(bf16)
                    st[PSI, at] = solved
                send_solved()
                for r in range(4):
                    at = slice(r * cells // 4, (r + 1) * cells // 4)
                    st[TT, at] = st[CC, at] - base[at]
                    st[CC, at] = st[PSI, at]

            @pl.when(jnp.logical_or(op == PUT_0, jnp.logical_or(op == START, op == OWNER_0)))
            def _():
                t = jnp.where(op == PUT_0, st[f["dst"]] - base[...], st[TT])
                out = st[LF] + 0.25 * t
                st[OUT] = out
                rounded_store(OUTB, out)

            @pl.when(op == OWNER)
            def _():
                arrived(CHANGE)

                @pl.when(lead_next)
                def _():
                    rounded_store(TO_SECOND, st[CC])

                for r in range(4):
                    at = slice(r * cells // 4, (r + 1) * cells // 4)
                    inner_at = slice(WIDTH + at.start, WIDTH + at.stop)
                    cc = st[CC, at]
                    change = rounded[CHANGE, inner_at, :].astype(f32)
                    second = st[RH, at] - (cc - st[PSI, at])
                    solved = change + ((cc - st[ZERO, at]) + second)
                    st[CC, at] = solved

                @pl.when(lead_next)
                def _():
                    rounded_store(TO_FINAL, st[CC])

                send_solved()

            put_at = jnp.where(
                op == OWNER, COARSEN - 1, jnp.where(op == PUT_1, 1, jnp.where(op == PUT_2, 2, 0))
            )

            @pl.when(jnp.logical_and(op >= START, op <= OWNER))
            def _():
                put(jnp.where(op == OWNER, CC, OUT), put_at)

            @pl.when(op == CHANGES)
            def _():
                rounded_store(TO_CHANGE, st[XZ] - st[TMP])
                special(TO_CHANGE, CHANGE, COARSEN - 1).start()

        return later

    def loop(*totals):
        sides = (totals[:BLOCKS], totals[2 * BLOCKS:3 * BLOCKS])
        middles = (totals[BLOCKS:2 * BLOCKS], totals[3 * BLOCKS:])
        wait_weights(0)
        for load in weight_loads(3):
            load.start()
        for m in (0, 1):
            push(0, 0, m)
        lax.fori_loop(0, count, functools.partial(run, sides, middles), fields_of(0))
        for m in (0, 1):
            pltpu.matmul_acc_lhs(sides[m][0], rounded[CPB, 0:rows_of, :], 0)
        finish()
        for m in (0, 1):
            side_sum[0:rows_of, :] = pltpu.matmul_pop(sides[m][0])

    def finish():
        @pl.when(jnp.logical_not(jnp.logical_and(owner_shares, last_owner)))
        def _():
            put(CC, COARSEN - 1)

        def drain(copy, cond):
            @pl.when(cond)
            def _():
                copy.wait_send()

        relaxed = jnp.logical_or(
            jnp.logical_and(owner, lead_next), jnp.logical_and(phase == 1, group > 0)
        )
        drain(weight_to(back), jnp.logical_or(shares, owner_shares))
        drain(special(TO_LEFT, LEFT, back), has_next)
        drain(special(TO_RHS, RHS, back), shares)
        drain(special(TO_FIRST, FIRST, back), phase < 2)
        drain(special(TO_FINAL, FINAL, back), relaxed)
        drain(special(TO_SECOND, SECOND, back), relaxed)
        drain(special(TO_CHANGE, CHANGE, back), changes)
        drain(relay_of(FIRST), first_owner)
        drain(relay_of(FINAL), jnp.logical_and(lead, group > 0))
        drain(relay_of(SECOND), jnp.logical_and(phase == 1, group > 0))

    pl.run_scoped(
        loop, *[pltpu.ACC(m)((rows_of, chans), f32) for m in (0, 1) for _ in range(2 * BLOCKS)]
    )


def per_device(devices, inputs, guess, weights):
    chans, cells = inputs.shape
    return pl.pallas_call(
        functools.partial(kernel, devices),
        name="cycle",
        out_shape=pltpu.VMEM((COARSEN, chans, cells), jnp.float32),
        in_specs=[pl.BlockSpec(memory_space=pltpu.HBM)] * 3,
        out_specs=pl.BlockSpec(memory_space=pltpu.VMEM),
        scratch_shapes=[
            pltpu.VMEM((2, chans, cells), jnp.float32),
            pltpu.VMEM((COARSEN + 1,) + weights.shape[1:], jnp.bfloat16),
            pltpu.VMEM((STATES, cells, chans), jnp.float32),
            pltpu.VMEM((ROUNDED, cells + 2 * WIDTH, chans), jnp.bfloat16),
            pltpu.VMEM((2, 2, cells + 16, chans // 2), jnp.float32),
            pltpu.VMEM((cells, chans), jnp.float32),
            pltpu.VMEM((cells, chans), jnp.float32),
            pltpu.SemaphoreType.DMA((TO_RHS - TO_LEFT + 1,)),
            pltpu.SemaphoreType.DMA((FINAL - LEFT + 1,)),
            pltpu.SemaphoreType.DMA((1,)),
            pltpu.SemaphoreType.DMA((ROUNDED + 1,)),
            pltpu.SemaphoreType.DMA((2,)),
            pltpu.SemaphoreType.DMA((COARSEN, PIECES)),
        ],
        compiler_params=pltpu.CompilerParams(
            collective_id=0, has_side_effects=True, vmem_limit_bytes=56 * 2**20,
        ),
    )(*[pltpu.with_memory_space_constraint(a, pltpu.HBM) for a in (inputs, guess, weights)])


def solution(mesh):
    return jax.shard_map(
        functools.partial(per_device, mesh.shape["layer"]),
        mesh=mesh,
        in_specs=(P(None, "batch"), P("layer", None, "batch"), P("layer", None, None)),
        out_specs=P("layer", None, "batch"),
        check_vma=False,
    )
```
